128 devices in a mesh: wide: 16 (over z, y), narrow: 8 (over x, core).
Axes of the slice: x: 4, y: 4, z: 4, core: 2. Of those that a mesh axis runs over, the one named last changes fastest.
Arguments:
- velocity: float32 [3, 512, 16384], P(None, None, ('wide', 'narrow')), may hold values from -6 to 6
- element_slot: int32 [128, 128], P(('wide', 'narrow')), may hold values from 0 to 127, as said below
- corner_vertex: int32 [8, 16384], P(None, ('wide', 'narrow')), may hold values from 0 to 17407, as said below
- axial_size: float32 [16], P('wide'), may hold values from 0.5 to 2
- arc_size: float32 [16], replicated, may hold values from 0.5 to 2
- radial_size: float32 [16], replicated, may hold values from 0.3 to 1.5
- fdm_vectors: float32 [10, 10], replicated, may hold values from -2 to 2
- fdm_values: float32 [10], replicated, may hold values from 0.5 to 60
Outputs:
- velocity_out: float32 [3, 512, 16384], P(None, None, ('wide', 'narrow'))
- coarse_residual: float32 [3, 17408], P(None, ('wide', 'narrow'))
The draws below stay inside these ranges and needn't reach their ends.
Inputs may be any that keep to these rules, and one draw needn't show every extreme that they name: `element_slot`: each device's row is a permutation of the block positions of its 128 elements. `corner_vertex`: the ids of a permutation of the 17408 vertices of the coarse grid (vertex at axial index, around index and radial offset 0 to 16, periodic along and around the pipe); corner a * 4 + b * 2 + c lies at axial offset a, around offset b, radial offset c of its element; elements that share a corner share its id.
All inputs are finite; a program needn't handle non-finite values.
Results may differ from the reference program's by a relative error of at most 0.0001.
Values sent between devices are 32-bit elements; how exact they have to be, the bound alone decides.
No kernel may reach another device: no remote copies, remote signals or barrier semaphores. Data moves between devices by JAX's collectives and lax.ppermute only.
A program may use at most 128 MiB of HBM per device.

```python
import math
from functools import partial
import jax
import jax.numpy as jnp
import numpy as np
from jax import lax

POINTS = 8
SPAN = 10
AXIAL_DEV = 1
AROUND_DEV = 8
RADIAL = 16
STEPS = 2
ELEMS_DEV = 128
AXIAL = 16
AROUND = 64
ELEMS = 16384
VERTICES = 17408
N_WIDE = 16
N_NARROW = 8


def layout_tables(key):
    wide_count = AXIAL // AXIAL_DEV
    narrow_count = AROUND // AROUND_DEV
    slot_keys = jax.random.split(jax.random.fold_in(key, 11), wide_count * narrow_count)
    slot_rows = jax.vmap(lambda sub_key: jax.random.permutation(sub_key, ELEMS_DEV))(slot_keys).astype(jnp.int32)
    relabel = jax.random.permutation(jax.random.fold_in(key, 12), VERTICES).astype(jnp.int32)
    return (slot_rows, relabel)


def draw_element_slot(key, part):
    return layout_tables(key)[0]


def draw_corner_vertex(key, part):
    slot_rows, relabel = layout_tables(key)
    narrow_count = AROUND // AROUND_DEV
    stored = jnp.arange(ELEMS, dtype=jnp.int32)
    device = stored // ELEMS_DEV
    position = slot_rows[device, stored % ELEMS_DEV]
    axial_index = device // narrow_count * AXIAL_DEV + position // (AROUND_DEV * RADIAL)
    around_index = device % narrow_count * AROUND_DEV + position // RADIAL % AROUND_DEV
    radial_index = position % RADIAL
    corners = []
    for corner in range(8):
        axial_spacing = corner // 4
        step_t = corner // 2 % 2
        step_r = corner % 2
        structured = ((axial_index + axial_spacing) % AXIAL * AROUND + (around_index + step_t) % AROUND) * (RADIAL + 1) + radial_index + step_r
        corners.append(relabel[structured])
    return jnp.stack(corners)


def block_scale(rng, dims, cuts, least, top_value):
    factor_of, own = 1.0, jax.random.fold_in(rng, 6)
    for dim, parts in cuts:
        steps = jnp.exp(jax.random.uniform(jax.random.fold_in(own, dim), (parts,), jnp.float32, least / len(cuts), top_value / len(cuts)))
        factor_of = factor_of * jnp.repeat(steps, dims[dim] // parts).reshape([-1 if axis == dim else 1 for axis in range(len(dims))])
    return factor_of


def noise(stream_key, shape, scale, reach, cuts=(), held_as=jnp.bfloat16):
    gain = block_scale(stream_key, shape, cuts, -0.22, 0.18) if cuts else 1.0
    values = jax.random.normal(stream_key, shape, jnp.float32) * scale * gain
    return jnp.minimum(jnp.maximum(values, -reach), reach).astype(held_as)


def setup_inputs(seed: int = 0) -> dict:
    seeds = jax.random.split(jax.random.key(seed), 9)
    return {
        "velocity": noise(seeds[0], (3, POINTS * POINTS * POINTS, ELEMS), 1.0, 6.0, ((2, 128),), jnp.float32),
        "element_slot": draw_element_slot(jax.random.fold_in(seeds[8], 71), 0),
        "corner_vertex": draw_corner_vertex(jax.random.fold_in(seeds[8], 71), 0),
        "axial_size": jnp.clip(jnp.exp(math.log(2.0) - 1.3862944 * jax.random.uniform(seeds[3], (AXIAL,), jnp.float32) ** block_scale(seeds[3], (AXIAL,), ((0, 16),), -0.2, 0.2)), 0.5, 2.0),
        "arc_size": jnp.clip(jnp.exp(jax.random.uniform(seeds[4], (RADIAL,), jnp.float32, math.log(0.5), math.log(2.0))), 0.5, 2.0),
        "radial_size": jnp.clip(jnp.exp(jax.random.uniform(seeds[5], (RADIAL,), jnp.float32, math.log(0.3), math.log(1.5))), 0.3, 1.5),
        "fdm_vectors": noise(seeds[6], (SPAN, SPAN), SPAN ** -0.5, 2.0, (), jnp.float32),
        "fdm_values": jnp.clip(jnp.exp(jax.random.uniform(seeds[7], (SPAN,), jnp.float32, math.log(0.5), math.log(60.0))), 0.5, 60.0),
    }


SIGMA = 4.0
VISCOSITY = 0.05
HIGH_ACCURACY = lax.Precision.HIGHEST


def node_tables():
    gll_nodes = np.array([-1.0, -0.8717401485096066, -0.5917001814331423, -0.2092992179024789, 0.2092992179024789, 0.5917001814331423, 0.8717401485096066, 1.0])
    gll_weights = np.array([1.0 / 28.0, 0.2107042271435061, 0.3411226924835044, 0.4124587946587038, 0.4124587946587038, 0.3411226924835044, 0.2107042271435061, 1.0 / 28.0])
    bary_scale = np.array([np.prod([gll_nodes[target] - gll_nodes[partner] for partner in range(8) if partner != target]) for target in range(8)])
    derivative = np.zeros((8, 8))
    for target in range(8):
        for source in range(8):
            if target != source:
                derivative[target, source] = bary_scale[target] / (bary_scale[source] * (gll_nodes[target] - gll_nodes[source]))
        derivative[target, target] = -np.sum(derivative[target])
    fine_nodes = np.array([-0.9815606342467192, -0.9041172563704749, -0.7699026741943047, -0.5873179542866175, -0.3678314989981802, -0.1252334085114689, 0.1252334085114689, 0.3678314989981802, 0.5873179542866175, 0.7699026741943047, 0.9041172563704749, 0.9815606342467192])
    fine_weights = np.array([0.0471753363865118, 0.1069393259953184, 0.1600783285433462, 0.2031674267230659, 0.2334925365383548, 0.2491470458134028, 0.2491470458134028, 0.2334925365383548, 0.2031674267230659, 0.1600783285433462, 0.1069393259953184, 0.0471753363865118])
    interp = np.ones((12, 8))
    for source in range(8):
        for partner in range(8):
            if partner != source:
                interp[:, source] = interp[:, source] * (fine_nodes - gll_nodes[partner]) / (gll_nodes[source] - gll_nodes[partner])
    linear = np.stack([(1.0 - gll_nodes) / 2.0, (1.0 + gll_nodes) / 2.0])
    corner_map = (linear[:, None, None, :, None, None] * linear[None, :, None, None, :, None] * linear[None, None, :, None, None, :]).reshape(8, 512)
    mass_gll = gll_weights[:, None, None] * gll_weights[None, :, None] * gll_weights[None, None, :]
    mass_fine = fine_weights[:, None, None] * fine_weights[None, :, None] * fine_weights[None, None, :]
    return tuple(jnp.asarray(matrix, jnp.float32) for matrix in (derivative, interp, corner_map, mass_gll, mass_fine))


def apply_first(matrix, tensor):
    return jnp.einsum('ai,cijkb->cajkb', matrix, tensor, precision=HIGH_ACCURACY)


def apply_second(matrix, tensor):
    return jnp.einsum('aj,cijkb->ciakb', matrix, tensor, precision=HIGH_ACCURACY)


def apply_third(matrix, tensor):
    return jnp.einsum('ak,cijkb->cijab', matrix, tensor, precision=HIGH_ACCURACY)


def to_fine(tensor, interp):
    return apply_third(interp, apply_second(interp, apply_first(interp, tensor)))


def to_gll(tensor, interp):
    return apply_third(interp.T, apply_second(interp.T, apply_first(interp.T, tensor)))


def element_residual(velocity, lengths, tables):
    derivative, interp, corner_map, mass_gll, mass_fine = tables
    block_width = velocity.shape[-1]
    tensor = velocity.reshape(3, 8, 8, 8, block_width)
    inverse = 2.0 / lengths
    volume = lengths[0] * lengths[1] * lengths[2] / 8.0
    grad_z = apply_first(derivative, tensor) * inverse[0]
    grad_t = apply_second(derivative, tensor) * inverse[1]
    grad_r = apply_third(derivative, tensor) * inverse[2]
    fine_vel = to_fine(tensor, interp)
    convective_term = fine_vel[0:1] * to_fine(grad_z, interp) + fine_vel[1:2] * to_fine(grad_t, interp) + fine_vel[2:3] * to_fine(grad_r, interp)
    convective_term = convective_term * (mass_fine[:, :, :, None] * volume)
    advect_velocity = to_gll(convective_term, interp)
    weight = mass_gll[:, :, :, None] * volume
    stiff = apply_first(derivative.T, grad_z * weight) * inverse[0]
    stiff = stiff + apply_second(derivative.T, grad_t * weight) * inverse[1]
    stiff = stiff + apply_third(derivative.T, grad_r * weight) * inverse[2]
    return -(advect_velocity + VISCOSITY * stiff).reshape(3, 512, block_width)


def quadratic_form(direction, lengths, tables):
    derivative = tables[0]
    mass_gll = tables[3]
    block_width = direction.shape[-1]
    tensor = direction.reshape(3, 8, 8, 8, block_width)
    inverse = 2.0 / lengths
    volume = lengths[0] * lengths[1] * lengths[2] / 8.0
    weight = mass_gll[:, :, :, None] * volume
    grad_z = apply_first(derivative, tensor) * inverse[0]
    grad_t = apply_second(derivative, tensor) * inverse[1]
    grad_r = apply_third(derivative, tensor) * inverse[2]
    return jnp.sum(weight * (SIGMA * tensor * tensor + VISCOSITY * (grad_z * grad_z + grad_t * grad_t + grad_r * grad_r)))


def fdm_solve(extended, lengths, vectors, values):
    block_width = extended.shape[-1]
    tensor = extended.reshape(3, 10, 10, 10, block_width)
    spectral = apply_third(vectors.T, apply_second(vectors.T, apply_first(vectors.T, tensor)))
    squared = (2.0 / lengths) ** 2
    volume = lengths[0] * lengths[1] * lengths[2] / 8.0
    scaling = volume * (SIGMA + VISCOSITY * (values[:, None, None, None] * squared[0] + values[None, :, None, None] * squared[1] + values[None, None, :, None] * squared[2]))
    spectral = spectral / scaling
    restored = apply_third(vectors, apply_second(vectors, apply_first(vectors, spectral)))
    return restored[:, 1:9, 1:9, 1:9].reshape(3, 512, block_width)


def blockwise(function, arrays, block_width):
    blocks_total = arrays[0].shape[-1] // block_width

    def single(block_index):
        pieces = [lax.dynamic_slice_in_dim(member, block_index * block_width, block_width, member.ndim - 1) for member in arrays]
        return function(*pieces)

    stacked = lax.map(single, jnp.arange(blocks_total, dtype=jnp.int32))
    if stacked.ndim == 1:
        return jnp.sum(stacked)
    reordered = jnp.moveaxis(stacked, 0, -2)
    return reordered.reshape(reordered.shape[:-2] + (blocks_total * block_width,))


def node_masks(elem_count):
    node_index = jnp.arange(512)
    node_i = node_index // 64
    node_j = (node_index // 8) % 8
    node_k = node_index % 8
    radial_pos = jnp.arange(elem_count) % RADIAL
    on_wall = ((node_k == 0)[:, None] & (radial_pos == 0)[None]) | ((node_k == 7)[:, None] & (radial_pos == RADIAL - 1)[None])
    wall_keep = jnp.where(on_wall, 0.0, 1.0).astype(jnp.float32)
    face_z = jnp.where((node_i == 0) | (node_i == 7), 2.0, 1.0)[:, None]
    face_t = jnp.where((node_j == 0) | (node_j == 7), 2.0, 1.0)[:, None]
    inner_r = ((node_k == 0)[:, None] & (radial_pos > 0)[None]) | ((node_k == 7)[:, None] & (radial_pos < RADIAL - 1)[None])
    sharing = (face_z * face_t * jnp.where(inner_r, 2.0, 1.0)).astype(jnp.float32)
    return wall_keep, sharing


def take_part(tensor, axis_pos, start, stop):
    return lax.slice_in_dim(tensor, start, stop, axis=axis_pos)


def shifted(tensor, elem_axis, offset, periodic):
    if periodic:
        return jnp.roll(tensor, offset, axis=elem_axis)
    elem_count = tensor.shape[elem_axis]
    zero_part = jnp.zeros_like(take_part(tensor, elem_axis, 0, 1))
    if offset > 0:
        return jnp.concatenate([zero_part, take_part(tensor, elem_axis, 0, elem_count - 1)], axis=elem_axis)
    return jnp.concatenate([take_part(tensor, elem_axis, 1, elem_count), zero_part], axis=elem_axis)


def shared_sum(tensor, node_axis, elem_axis, periodic):
    low_plane = take_part(tensor, node_axis, 0, 1)
    high_plane = take_part(tensor, node_axis, 7, 8)
    next_low = shifted(low_plane, elem_axis, -1, periodic)
    previous_upper_plane = shifted(high_plane, elem_axis, 1, periodic)
    middle = take_part(tensor, node_axis, 1, 7)
    return jnp.concatenate([low_plane + previous_upper_plane, middle, high_plane + next_low], axis=node_axis)


def widened(tensor, node_axis, elem_axis, periodic):
    lower = shifted(take_part(tensor, node_axis, 6, 7), elem_axis, 1, periodic)
    upper = shifted(take_part(tensor, node_axis, 1, 2), elem_axis, -1, periodic)
    return jnp.concatenate([lower, tensor, upper], axis=node_axis)


def reference(velocity, element_slot, corner_vertex, axial_size, arc_size, radial_size, fdm_vectors, fdm_values):
    tables = node_tables()
    devices = N_WIDE * N_NARROW
    block_width = min(128, ELEMS_DEV)
    inverse_slot = jnp.zeros((devices, ELEMS_DEV), jnp.int32).at[jnp.arange(devices)[:, None], element_slot].set(
        jnp.broadcast_to(jnp.arange(ELEMS_DEV, dtype=jnp.int32)[None], (devices, ELEMS_DEV)))

    def to_struct(tensor):
        channels = tensor.shape[0]
        grouped = tensor.reshape(channels, -1, devices, ELEMS_DEV)
        placed = jnp.take_along_axis(grouped, inverse_slot[None, None], axis=3)
        placed = placed.reshape(channels, -1, N_WIDE, N_NARROW, AXIAL_DEV, AROUND_DEV, RADIAL)
        placed = placed.transpose(0, 1, 2, 4, 3, 5, 6)
        return placed.reshape(channels, -1, ELEMS)

    def from_struct(tensor):
        channels = tensor.shape[0]
        placed = tensor.reshape(channels, -1, N_WIDE, AXIAL_DEV, N_NARROW, AROUND_DEV, RADIAL)
        placed = placed.transpose(0, 1, 2, 4, 3, 5, 6).reshape(channels, -1, devices, ELEMS_DEV)
        stored = jnp.take_along_axis(placed, element_slot[None, None], axis=3)
        return stored.reshape(channels, -1, ELEMS)

    def assemble(tensor):
        channels = tensor.shape[0]
        grid_view = tensor.reshape(channels, 8, 8, 8, AXIAL, AROUND, RADIAL)
        grid_view = shared_sum(grid_view, 1, 4, True)
        grid_view = shared_sum(grid_view, 2, 5, True)
        grid_view = shared_sum(grid_view, 3, 6, False)
        return grid_view.reshape(tensor.shape)

    def widen(tensor):
        grid_view = tensor.reshape(3, 8, 8, 8, AXIAL, AROUND, RADIAL)
        grid_view = widened(grid_view, 1, 4, True)
        grid_view = widened(grid_view, 2, 5, True)
        grid_view = widened(grid_view, 3, 6, False)
        return grid_view.reshape(3, 1000, ELEMS)

    shape_grid = (AXIAL, AROUND, RADIAL)
    axial_len = jnp.broadcast_to(axial_size[:, None, None], shape_grid)
    around_len = jnp.broadcast_to(arc_size[None, None, :], shape_grid)
    radial_len = jnp.broadcast_to(radial_size[None, None, :], shape_grid)
    lengths = jnp.stack([axial_len, around_len, radial_len]).reshape(3, ELEMS)
    volume = lengths[0] * lengths[1] * lengths[2] / 8.0
    node_mass = tables[3].reshape(512)[:, None] * volume[None]
    wall_keep, sharing = node_masks(ELEMS)

    stored_first = to_struct(velocity)
    summed = assemble(jnp.concatenate([stored_first * node_mass[None], node_mass[None]], 0))
    velocity_now = summed[:3] / summed[3:4] * wall_keep
    residual_fn = partial(element_residual, tables=tables)
    solve_fn = partial(fdm_solve, vectors=fdm_vectors, values=fdm_values)
    quad_fn = partial(quadratic_form, tables=tables)
    for step_index in range(STEPS):
        local_res = blockwise(residual_fn, (velocity_now, lengths), block_width) * wall_keep
        assembled = assemble(local_res)
        extended = widen(assembled)
        correction = blockwise(solve_fn, (extended, lengths), block_width)
        direction = assemble(correction / sharing) * wall_keep
        numerator = jnp.sum(assembled * direction / sharing)
        denominator = blockwise(quad_fn, (direction, lengths), block_width)
        velocity_now = velocity_now + (numerator / denominator) * direction
    final_res = blockwise(residual_fn, (velocity_now, lengths), block_width) * wall_keep
    corner_sums = jnp.einsum('qp,cpe->cqe', tables[2], final_res, precision=HIGH_ACCURACY)
    vertex_ids = to_struct(corner_vertex[None]).reshape(-1)
    coarse = jax.ops.segment_sum(corner_sums.reshape(3, -1).T, vertex_ids, num_segments=VERTICES).T
    return from_struct(velocity_now), coarse
```

```python
from functools import partial

import jax
import jax.numpy as jnp
import ml_dtypes
import numpy as np
from jax import lax
from jax.experimental import pallas as pl
from jax.experimental.pallas import tpu as pltpu
from jax.sharding import PartitionSpec as P

RADIAL = 16
SIGMA = 4.0
VISCOSITY = 0.05
F32 = jnp.float32
BF16 = jnp.bfloat16
EXACT = lax.Precision.HIGHEST
BOTH = ("wide", "narrow")


def node_tables():
    x = np.array(
        [-1.0, -0.8717401485096066, -0.5917001814331423, -0.2092992179024789]
    )
    x = np.concatenate([x, -x[::-1]])
    w = np.array([1.0 / 28.0, 0.2107042271435061, 0.3411226924835044, 0.4124587946587038])
    w = np.concatenate([w, w[::-1]])
    scale = np.array([np.prod([x[t] - x[p] for p in range(8) if p != t]) for t in range(8)])
    deriv = np.zeros((8, 8))
    for t in range(8):
        for s in range(8):
            if t != s:
                deriv[t, s] = scale[t] / (scale[s] * (x[t] - x[s]))
        deriv[t, t] = -np.sum(deriv[t])
    y = np.array(
        [
            -0.9815606342467192,
            -0.9041172563704749,
            -0.7699026741943047,
            -0.5873179542866175,
            -0.3678314989981802,
            -0.1252334085114689,
        ]
    )
    y = np.concatenate([y, -y[::-1]])
    v = np.array(
        [
            0.0471753363865118,
            0.1069393259953184,
            0.1600783285433462,
            0.2031674267230659,
            0.2334925365383548,
            0.2491470458134028,
        ]
    )
    v = np.concatenate([v, v[::-1]])
    interp = np.ones((12, 8))
    for s in range(8):
        for p in range(8):
            if p != s:
                interp[:, s] = interp[:, s] * (y - x[p]) / (x[s] - x[p])
    linear = np.stack([(1.0 - x) / 2.0, (1.0 + x) / 2.0])
    return w, deriv, v, interp, linear


W, D, VF, J, LIN = node_tables()
B = J @ D
JV = J.T * VF[None, :]
STIFF = D.T @ (W[:, None] * D)
WJK = np.kron(W, W)


def two_parts(matrix):
    hi = matrix.astype(np.float32).astype(ml_dtypes.bfloat16)
    lo = (matrix - hi.astype(np.float64)).astype(ml_dtypes.bfloat16)
    return hi, lo


def four_terms(matrix):
    hi, lo = two_parts(matrix)
    return np.concatenate([hi, lo, hi, lo], axis=1)


def three_terms(matrix):
    hi, lo = two_parts(matrix)
    return np.concatenate([hi, lo, hi], axis=1)


FINE = four_terms(np.concatenate([np.kron(J, J), np.kron(B, J), np.kron(J, B)]))
BACK = three_terms(np.kron(JV, JV))
STIFF_JK = four_terms(
    np.concatenate([np.kron(STIFF, np.diag(W)), np.kron(np.diag(W), STIFF)])
)
GRAD_JK = four_terms(np.concatenate([np.kron(D, np.eye(8)), np.kron(np.eye(8), D)]))


def call(kernel, outs, args, scratch=(), spaces=None):
    spaces = spaces or {}
    return pl.pallas_call(
        kernel,
        out_shape=[jax.ShapeDtypeStruct(s, d) for s, d in outs],
        in_specs=[
            pl.BlockSpec(memory_space=spaces.get(i, pltpu.VMEM)) for i in range(len(args))
        ],
        out_specs=[pl.BlockSpec(memory_space=pltpu.VMEM) for _ in outs],
        scratch_shapes=list(scratch),
        compiler_params=pltpu.CompilerParams(vmem_limit_bytes=56 << 20),
        name=kernel.func.__name__ if isinstance(kernel, partial) else kernel.__name__,
    )(*args)


def iota(shape, dim):
    return lax.broadcasted_iota(jnp.int32, shape, dim)


def lanes_by(x, shift):
    return pltpu.roll(x, shift % x.shape[-1], x.ndim - 1)


def rows_by(x, shift):
    return pltpu.roll(x, shift % 8, x.ndim - 2)


def split(x):
    hi = x.astype(BF16)
    return hi, (x - hi.astype(F32)).astype(BF16)


def dot(a, b):
    return jnp.dot(a, b, preferred_element_type=F32)


def even_odd(matrix, xs, sign):
    n_out, n_in = matrix.shape
    half = n_in // 2
    even = [xs[i] + xs[n_in - 1 - i] for i in range(half)]
    odd = [xs[i] - xs[n_in - 1 - i] for i in range(half)]
    outs = [None] * n_out
    for a in range(n_out // 2):
        e = sum(
            float((matrix[a, i] + matrix[a, n_in - 1 - i]) / 2) * even[i] for i in range(half)
        )
        o = sum(
            float((matrix[a, i] - matrix[a, n_in - 1 - i]) / 2) * odd[i] for i in range(half)
        )
        outs[a] = e + o
        outs[n_out - 1 - a] = e - o if sign > 0 else o - e
    return outs


def keep_rows(rows):
    k = iota((rows, 128), 0) & 7
    r = iota((rows, 128), 1) & (RADIAL - 1)
    wall = ((k == 0) & (r == 0)) | ((k == 7) & (r == RADIAL - 1))
    return jnp.where(wall, 0.0, 1.0).astype(F32)


def radial_parts(x):
    r = iota((8, 128), 1) & (RADIAL - 1)
    below = jnp.where(r > 0, lanes_by(x, 1), 0.0)
    above = jnp.where(r < RADIAL - 1, lanes_by(x, -1), 0.0)
    return below, above


def radial_sum(x, below, above):
    k = iota((8, 128), 0)
    return x + jnp.where(k == 0, rows_by(below, 1), jnp.where(k == 7, rows_by(above, -1), 0.0))


def pack_low(plane_of):
    et = iota((8, 128), 1) >> 4
    out = jnp.zeros((8, 128), F32)
    for i in range(8):
        out = jnp.where(et == i, lanes_by(plane_of(i), 16 * i), out)
    return out


def pack_high(plane_of):
    et = iota((8, 128), 1) >> 4
    out = jnp.zeros((8, 128), F32)
    for i in range(8):
        out = jnp.where(et == i, lanes_by(plane_of(i), 16 * i + 16), out)
    return out


def from_low(plane, packed, i):
    lane = iota((8, 128), 1)
    return jnp.where(lane < 16, lanes_by(packed, -16 * i), lanes_by(plane, 16))


def from_high(plane, packed, i):
    lane = iota((8, 128), 1)
    return jnp.where(lane >= 112, lanes_by(packed, 112 - 16 * i), lanes_by(plane, -16))


def start_kernel(vel, slot, corner, arc, rad, axial, mv, low, high, lanes, place):
    ht = jnp.broadcast_to(arc[...], (8, 16))
    hr = jnp.broadcast_to(rad[...], (8, 16))
    spread = ((iota((16, 256), 1) & 15) == iota((16, 256), 0)).astype(F32)
    ht = jnp.dot(ht, spread, precision=EXACT, preferred_element_type=F32)[0:1]
    hr = jnp.dot(hr, spread, precision=EXACT, preferred_element_type=F32)[0:1]
    hz = jnp.zeros((1, 256), F32) + axial[0]
    g = ht * hr / 8.0
    vol = hz * g
    r = iota((1, 256), 1) & (RADIAL - 1)
    g_low = g + jnp.where(r > 0, lanes_by(g, 1), 0.0)
    g_high = g + jnp.where(r < RADIAL - 1, lanes_by(g, -1), 0.0)
    rows = [
        vol,
        vol * (2.0 / hz),
        vol * (2.0 / ht),
        vol * (2.0 / hr),
        VISCOSITY * vol * (2.0 / hz) * (2.0 / hz),
        VISCOSITY * vol * (2.0 / ht) * (2.0 / ht),
        VISCOSITY * vol * (2.0 / hr) * (2.0 / hr),
        hz,
        1.0 / g,
        1.0 / g_low,
        1.0 / g_high,
    ]
    for n, row in enumerate(rows):
        lanes[n : n + 1] = row
    for n in range(len(rows), 16):
        lanes[n : n + 1] = jnp.zeros((1, 256), F32)
    hot = (slot[...] == iota((128, 128), 0)).astype(F32)
    nt = (((1,), (1,)), ((), ()))

    def body(c, carry):
        x = vel[c].reshape(512, 128)
        y = lax.dot_general(x, hot, nt, precision=EXACT, preferred_element_type=F32)
        mv[c] = (y * vol[:, :128]).reshape(8, 64, 128)
        low[c] = pack_low(lambda i: mv[c, i, 0:8])
        high[c] = pack_high(lambda i: mv[c, i, 56:64])
        return carry

    lax.fori_loop(0, 3, body, 0)
    ids = lax.dot_general(
        corner[...].astype(F32), hot, nt, precision=EXACT, preferred_element_type=F32
    )
    place[...] = (ids + 0.5).astype(jnp.int32)


def solve_tables_kernel(vectors, values, lanes, forward, inverse, scale):
    s = vectors[...]
    ident = (iota((10, 10), 0) == iota((10, 10), 1)).astype(F32)
    st = lax.dot_general(
        ident, s, (((1,), (1,)), ((), ())), precision=EXACT, preferred_element_type=F32
    )

    def mul(a, b):
        return jnp.dot(a, b, precision=EXACT, preferred_element_type=F32)

    row, col = iota((112, 10), 0), iota((112, 10), 1)
    live = row < 100
    by_b = ((row // 10 == col) & live).astype(F32)
    by_c = ((row % 10 == col) & live).astype(F32)
    node, pos = iota((10, 160), 0), iota((10, 160), 1)
    slot = pos & 15
    k_of = jnp.where(slot < 8, slot + 1, jnp.where(slot == 8, 0, jnp.where(slot == 9, 9, -1)))
    by_j = (node == (pos >> 4)).astype(F32)
    by_k = (node == k_of).astype(F32)
    full = mul(mul(by_b, st), by_j) * mul(mul(by_c, st), by_k)
    hi, lo = split(full)
    forward[:, 0:160] = hi
    forward[:, 160:320] = lo
    forward[:, 320:480] = hi

    row8, col8 = iota((64, 10), 0), iota((64, 10), 1)
    by_j8 = ((row8 >> 3) + 1 == col8).astype(F32)
    by_k8 = ((row8 & 7) + 1 == col8).astype(F32)
    node2, pos2 = iota((10, 112), 0), iota((10, 112), 1)
    b_of = jnp.where(pos2 < 100, pos2 // 10, -1)
    c_of = jnp.where(pos2 < 100, pos2 % 10, -1)
    to_b = (node2 == b_of).astype(F32)
    to_c = (node2 == c_of).astype(F32)
    full = mul(mul(by_j8, s), to_b) * mul(mul(by_k8, s), to_c)
    hi, lo = split(full)
    inverse[:, 0:112] = hi
    inverse[:, 112:224] = lo
    inverse[:, 224:336] = hi

    lam = jnp.broadcast_to(values[...], (8, 10))
    nt = (((1,), (1,)), ((), ()))
    lam_b = lax.dot_general(by_b, lam, nt, precision=EXACT, preferred_element_type=F32)[:, 0:1]
    lam_c = lax.dot_general(by_c, lam, nt, precision=EXACT, preferred_element_type=F32)[:, 0:1]
    vol = lanes[0:1, :128]
    flat = (
        SIGMA * vol
        + lam_b * jnp.broadcast_to(lanes[5:6, :128], (112, 128))
        + lam_c * jnp.broadcast_to(lanes[6:7, :128], (112, 128))
    )
    for a in range(10):
        scale[a] = 1.0 / (flat + values[0:1, a : a + 1] * lanes[4:5, :128])


def around_sum_kernel(field, tlo, thi, lanes, out, down, up):
    def body(c, carry):
        lo, hi = tlo[c], thi[c]
        for i in range(8):
            x = field[c, i]
            first, last = x[0:8], x[56:64]
            head = first + from_low(last, lo, i)
            tail = last + from_high(first, hi, i)
            out[c, i] = x
            out[c, i, 0:8] = head
            out[c, i, 56:64] = tail
        base = pl.multiple_of(c * 64, 64)
        down[pl.ds(base, 64)] = out[c, 0]
        up[pl.ds(base, 64)] = out[c, 7]
        return carry

    lax.fori_loop(0, 3, body, 0)
    hz = jnp.broadcast_to(lanes[7:8, :128], (8, 128))
    down[192:200] = hz
    up[192:200] = hz


def finish_sum(field, zlo, zhi, out, factor):
    def body(c, carry):
        base = pl.multiple_of(c * 64, 64)
        for i in range(8):
            x = field[c, i]
            if i == 0:
                x = x + zlo[pl.ds(base, 64)]
            if i == 7:
                x = x + zhi[pl.ds(base, 64)]
            for j in range(8):
                v = x[8 * j : 8 * j + 8]
                below, above = radial_parts(v)
                out[c, i, 8 * j : 8 * j + 8] = radial_sum(v, below, above) * factor(i, j)
        return carry

    lax.fori_loop(0, 3, body, 0)


def residual(u, lanes, fine, back, stiff, wjk, res, xu, xw, xs, pf, qf, xc, yf, sz, ks):
    def put(ref, at, rb, half, x):
        hi, lo = split(x)
        for term, part in enumerate((hi, hi, lo, lo)):
            ref[at, pl.ds(pl.multiple_of(term * 64 + rb * 16, 16), 16),
                half * 128 : half * 128 + 128] = part

    def first(t, carry):
        c, rb = t // 4, t % 4
        rows = pl.ds(pl.multiple_of(rb * 16, 16), 16)
        x = [u[c, i, rows] for i in range(8)]
        for a, val in enumerate(even_odd(J, x, 1)):
            put(xu, c * 6 + a // 2, rb, a % 2, val)
        for a, val in enumerate(even_odd(B, x, -1)):
            put(xw, c * 6 + a // 2, rb, a % 2, val)
        for i in range(8):
            put(xs, c * 4 + i // 2, rb, i % 2, x[i])
        for i, val in enumerate(even_odd(STIFF, x, 1)):
            sz[c, i, rows] = val
        return carry

    lax.fori_loop(0, 12, first, 0)

    def second(p, carry):
        for c in range(3):
            pf[c] = dot(fine[...], xu[c * 6 + p])
            qf[c] = dot(fine[0:144], xw[c * 6 + p])
        lz, lt, lr = lanes[1:2], lanes[2:3], lanes[3:4]
        for r in range(9):
            rows = slice(16 * r, 16 * r + 16)
            vz = pf[0, rows] * lz
            vt = pf[1, rows] * lt
            vr = pf[2, rows] * lr
            for c in range(3):
                conv = (
                    vz * qf[c, rows]
                    + vt * pf[c, 144 + 16 * r : 160 + 16 * r]
                    + vr * pf[c, 288 + 16 * r : 304 + 16 * r]
                )
                hi, lo = split(conv)
                xc[c, rows] = hi
                xc[c, 144 + 16 * r : 160 + 16 * r] = hi
                xc[c, 288 + 16 * r : 304 + 16 * r] = lo
        for c in range(3):
            y = dot(back[...], xc[c])
            yf[c, 2 * p] = y[:, :128]
            yf[c, 2 * p + 1] = y[:, 128:]
        return carry

    lax.fori_loop(0, 6, second, 0)

    def third(t, carry):
        y = dot(stiff[...], xs[t])
        c, p = t // 4, t % 4
        ks[c, 2 * p] = y[:, :128]
        ks[c, 2 * p + 1] = y[:, 128:]
        return carry

    lax.fori_loop(0, 12, third, 0)
    kz, kt, kr = lanes[4:5, :128], lanes[5:6, :128], lanes[6:7, :128]
    keep = keep_rows(16)

    def fourth(t, carry):
        c, rb = t // 4, t % 4
        rows = pl.ds(pl.multiple_of(rb * 16, 16), 16)
        more = pl.ds(pl.multiple_of(64 + rb * 16, 16), 16)
        adv = even_odd(JV, [yf[c, a, rows] for a in range(12)], 1)
        wz = wjk[rows] * kz
        for i in range(8):
            plane = float(W[i]) * (kt * ks[c, i, rows] + kr * ks[c, i, more])
            res[c, i, rows] = -(adv[i] + wz * sz[c, i, rows] + plane) * keep
        return carry

    lax.fori_loop(0, 12, fourth, 0)


def pack_two(res, low, high):
    def body(c, carry):
        for n in range(2):
            low[c, 8 * n : 8 * n + 8] = pack_low(lambda i: res[c, i, 8 * n : 8 * n + 8])
            high[c, 8 * n : 8 * n + 8] = pack_high(
                lambda i: res[c, i, 48 + 8 * n : 56 + 8 * n]
            )
        return carry

    lax.fori_loop(0, 3, body, 0)


def project_kernel(
    field, zlo, zhi, lanes, fine, back, stiff, wjk, u, res, low, high, *scratch
):
    hz = lanes[7:8, :128]
    inner = 1.0 / hz
    first = 1.0 / (hz + zlo[192:193])
    last = 1.0 / (hz + zhi[192:193])
    k = iota((8, 128), 0)
    rk = jnp.where(
        k == 0, lanes[9:10, :128], jnp.where(k == 7, lanes[10:11, :128], lanes[8:9, :128])
    )
    rk = rk * keep_rows(8)
    by_plane = {0: rk * first, 7: rk * last}
    middle = rk * inner

    def factor(i, j):
        f = by_plane.get(i, middle)
        return 0.5 * f if j in (0, 7) else f

    finish_sum(field, zlo, zhi, u, factor)
    residual(u, lanes, fine, back, stiff, wjk, res, *scratch)
    pack_two(res, low, high)


def step_length(sums):
    total = jnp.sum(sums[...], axis=0, keepdims=True)
    return total[:, 0:1] / total[:, 1:2]


def advance(u_old, d, sums, u):
    alpha = step_length(sums)

    def body(t, carry):
        c, i = t // 8, t % 8
        u[c, i] = u_old[c, i] + alpha * d[c, i]
        return carry

    lax.fori_loop(0, 24, body, 0)


def advance_kernel(
    u_old, d, sums, lanes, fine, back, stiff, wjk, u, res, low, high, *scratch
):
    advance(u_old, d, sums, u)
    residual(u, lanes, fine, back, stiff, wjk, res, *scratch)
    pack_two(res, low, high)


def around_widen_kernel(res, tlo, thi, out, down, up):
    lane = iota((8, 128), 1)

    def body(c, carry):
        lo6, lo7, hi0, hi1 = tlo[c, 0:8], tlo[c, 8:16], thi[c, 0:8], thi[c, 8:16]
        for i in range(8):
            x = res[c, i]
            first, last = x[0:8], x[56:64]
            out[c, i, 0:64] = x
            out[c, i, 0:8] = first + from_low(last, lo7, i)
            out[c, i, 56:64] = last + from_high(first, hi0, i)
            out[c, i, 64:72] = jnp.where(
                lane < 64, lanes_by(lo6, -16 * i), lanes_by(hi1, 112 - 16 * i)
            )
        for n in range(2):
            down[c, n] = out[c, n]
            up[c, n] = out[c, 6 + n]
        return carry

    lax.fori_loop(0, 3, body, 0)


def solve_kernel(
    field, zlo, zhi, vectors, forward, inverse, scale, corr, low, high, xf, yf, xb
):
    lane = iota((8, 128), 1)
    k = iota((8, 128), 0)
    r = lane & (RADIAL - 1)

    def widen(c, p):
        for half in range(2):
            n = 2 * p + half
            if n == 0:
                e = zlo[c, 0]
            elif n == 1:
                e = field[c, 0] + zlo[c, 1]
            elif n == 8:
                e = field[c, 7] + zhi[c, 0]
            elif n == 9:
                e = zhi[c, 1]
            else:
                e = field[c, n - 1]
            extra = e[64:72]
            planes = [e[8 * j : 8 * j + 8] for j in range(8)]
            under = jnp.where(lane < 16, extra, lanes_by(planes[6], 16))
            over = jnp.where(lane >= 112, extra, lanes_by(planes[1], -16))
            for j, v in enumerate([under] + planes + [over]):
                below, above = radial_parts(v)
                own = radial_sum(v, below, above)
                side = jnp.where(k == 0, rows_by(below, 2), jnp.where(k == 1, above, 0.0))
                hi, lo = split(jnp.concatenate([own, side], axis=0))
                cols = slice(half * 128, half * 128 + 128)
                xf[16 * j : 16 * j + 16, cols] = hi
                xf[160 + 16 * j : 176 + 16 * j, cols] = hi
                xf[320 + 16 * j : 336 + 16 * j, cols] = lo

    def body(c, carry):
        for p in range(5):
            widen(c, p)
            y = dot(forward[...], xf[...])
            yf[c, 2 * p] = y[:, :128]
            yf[c, 2 * p + 1] = y[:, 128:]
        return carry

    lax.fori_loop(0, 3, body, 0)

    def mid(t, carry):
        c, rb = t // 7, t % 7
        rows = pl.ds(pl.multiple_of(rb * 16, 16), 16)
        y = [yf[c, i, rows] for i in range(10)]
        spec = []
        for a in range(10):
            acc = vectors[0, a] * y[0]
            for i in range(1, 10):
                acc = acc + vectors[i, a] * y[i]
            spec.append(acc * scale[a, rows])
        for i in range(8):
            acc = vectors[i + 1, 0] * spec[0]
            for a in range(1, 10):
                acc = acc + vectors[i + 1, a] * spec[a]
            hi, lo = split(acc)
            cols = slice((i % 2) * 128, (i % 2) * 128 + 128)
            for term, part in enumerate((hi, hi, lo)):
                xb[c * 4 + i // 2, pl.ds(pl.multiple_of(term * 112 + rb * 16, 16), 16),
                   cols] = part
        return carry

    lax.fori_loop(0, 21, mid, 0)

    inner = ((k == 0) & (r > 0)) | ((k == 7) & (r < RADIAL - 1))
    share = jnp.where(inner, 0.5, 1.0).astype(F32)

    def last(c, carry):
        for p in range(4):
            y = dot(inverse[...], xb[c * 4 + p])
            for half in range(2):
                i = 2 * p + half
                for j in range(8):
                    f = (0.5 if i in (0, 7) else 1.0) * (0.5 if j in (0, 7) else 1.0)
                    corr[c, i, 8 * j : 8 * j + 8] = (
                        y[8 * j : 8 * j + 8, half * 128 : half * 128 + 128] * (share * f)
                    )
        low[c] = pack_low(lambda i: corr[c, i, 0:8])
        high[c] = pack_high(lambda i: corr[c, i, 56:64])
        return carry

    lax.fori_loop(0, 3, last, 0)


def direction_kernel(field, zlo, zhi, res, lanes, grad, wjk, d, sums, xs, acc):
    keep = keep_rows(8)
    finish_sum(field, zlo, zhi, d, lambda i, j: keep)
    acc[...] = jnp.zeros_like(acc)
    vol = lanes[0:1, :128]
    kz, kt, kr = lanes[4:5, :128], lanes[5:6, :128], lanes[6:7, :128]

    def first(t, carry):
        c, rb = t // 4, t % 4
        rows = pl.ds(pl.multiple_of(rb * 16, 16), 16)
        x = [d[c, i, rows] for i in range(8)]
        num = sum(x[i] * res[c, i, rows] for i in range(8))
        sq = sum(float(W[i]) * (x[i] * x[i]) for i in range(8))
        gz = sum(float(W[i]) * (g * g) for i, g in enumerate(even_odd(D, x, -1)))
        acc[0] += num
        acc[1] += wjk[rows] * (SIGMA * vol * sq + kz * gz)
        for i in range(8):
            hi, lo = split(x[i])
            for term, part in enumerate((hi, hi, lo, lo)):
                xs[c * 4 + i // 2, pl.ds(pl.multiple_of(term * 64 + rb * 16, 16), 16),
                   (i % 2) * 128 : (i % 2) * 128 + 128] = part
        return carry

    lax.fori_loop(0, 12, first, 0)

    def second(c, carry):
        total = jnp.zeros((16, 128), F32)
        for p in range(4):
            y = dot(grad[...], xs[c * 4 + p])
            for half in range(2):
                v = y[:, half * 128 : half * 128 + 128]
                v = v * v
                plane = jnp.zeros((16, 128), F32)
                for q in range(4):
                    rows = slice(16 * q, 16 * q + 16)
                    plane = plane + wjk[rows] * (
                        kt * v[rows] + kr * v[64 + 16 * q : 80 + 16 * q]
                    )
                total = total + float(W[2 * p + half]) * plane
        acc[1] += total
        return carry

    lax.fori_loop(0, 3, second, 0)
    num = jnp.sum(jnp.sum(acc[0], axis=0, keepdims=True), axis=1, keepdims=True)
    den = jnp.sum(jnp.sum(acc[1], axis=0, keepdims=True), axis=1, keepdims=True)
    at = iota((128, 128), 1)
    sums[...] = jnp.where(at == 0, num, jnp.where(at == 1, den, 0.0))


def last_kernel(
    u_old, d, sums, lanes, fine, back, stiff, wjk, slot, place, vel, dense, u, res, *scratch
):
    advance(u_old, d, sums, u)
    residual(u, lanes, fine, back, stiff, wjk, res, *scratch)
    hot = (slot[...] == iota((128, 128), 0)).astype(F32)
    nt = (((1,), (1,)), ((), ()))
    row, col = iota((8, 64), 0), iota((8, 64), 1)

    def weight(node, upper):
        out = jnp.zeros((8, 64), F32)
        for n in range(8):
            out = jnp.where(
                node == n, jnp.where(upper, float(LIN[1, n]), float(LIN[0, n])), out
            )
        return out

    corner_jk = weight(col >> 3, (row & 2) != 0) * weight(col & 7, (row & 1) != 0)
    owner = place[...] // 136
    place_in = place[...] - owner * 136
    dev = iota((128, 128), 0)
    dense[...] = jnp.zeros_like(dense)

    def body(c, carry):
        flat = u[c].reshape(512, 128)
        vel[c] = jnp.dot(flat, hot, precision=EXACT, preferred_element_type=F32).reshape(
            8, 64, 128
        )
        planes = [res[c, i] for i in range(8)]
        z1 = sum(float(LIN[1, i]) * planes[i] for i in range(1, 8))
        z0 = sum(float(LIN[0, i]) * planes[i] for i in range(7))
        s0 = jnp.dot(corner_jk, z0, precision=EXACT, preferred_element_type=F32)
        s1 = jnp.dot(corner_jk, z1, precision=EXACT, preferred_element_type=F32)
        left, right = [], []
        pos = iota((408, 128), 0)
        for q in range(8):
            val = (s1 if q >= 4 else s0)[q % 4 : q % 4 + 1]
            left.append(jnp.where(owner[q : q + 1] == dev, val, 0.0))
            right.append((place_in[q : q + 1] + c * 136 == pos).astype(F32))
        dense[...] += lax.dot_general(
            jnp.concatenate(left, axis=1),
            jnp.concatenate(right, axis=1),
            nt,
            precision=EXACT,
            preferred_element_type=F32,
        )
        return carry

    lax.fori_loop(0, 3, body, 0)


FIELD = (3, 8, 64, 128)


def both_ways(axis, to_next, to_prev):
    n = lax.axis_size(axis)
    up = [(i, (i + 1) % n) for i in range(n)]
    down = [((i + 1) % n, i) for i in range(n)]
    return lax.ppermute(to_next, axis, up), lax.ppermute(to_prev, axis, down)


def residual_scratch():
    return [
        pltpu.VMEM((18, 256, 256), BF16),
        pltpu.VMEM((18, 256, 256), BF16),
        pltpu.VMEM((12, 256, 256), BF16),
        pltpu.VMEM((3, 432, 256), F32),
        pltpu.VMEM((3, 144, 256), F32),
        pltpu.VMEM((3, 432, 256), BF16),
        pltpu.VMEM((3, 12, 64, 128), F32),
        pltpu.VMEM(FIELD, F32),
        pltpu.VMEM((3, 8, 128, 128), F32),
    ]


def shards(vel, slot, corner, axial, arc, rad, vectors, values):
    fine, back, stiff, grad = (jnp.asarray(m) for m in (FINE, BACK, STIFF_JK, GRAD_JK))
    wjk = jnp.asarray(np.broadcast_to(WJK[:, None], (64, 128)).astype(np.float32))
    smem = pltpu.SMEM
    mv, low, high, lanes, place = call(
        start_kernel,
        [(FIELD, F32), ((3, 8, 128), F32), ((3, 8, 128), F32), ((16, 256), F32),
         ((8, 128), jnp.int32)],
        (vel.reshape(FIELD), slot, corner, arc[None], rad[None], axial),
        spaces={5: smem},
    )
    forward, inverse, scale = call(
        solve_tables_kernel,
        [((112, 480), BF16), ((64, 336), BF16), ((10, 112, 128), F32)],
        (vectors, values[None], lanes),
    )

    def sum_rounds(field, low, high):
        tlo, thi = both_ways("narrow", high, low)
        out, down, up = call(
            around_sum_kernel,
            [(FIELD, F32), ((200, 128), F32), ((200, 128), F32)],
            (field, tlo, thi, lanes),
        )
        zlo, zhi = both_ways("wide", up, down)
        return out, zlo, zhi

    local = (lanes, fine, back, stiff, wjk)
    packs = [(FIELD, F32), (FIELD, F32), ((3, 16, 128), F32), ((3, 16, 128), F32)]
    u, res, low, high = call(
        project_kernel, packs, (*sum_rounds(mv, low, high), *local), residual_scratch()
    )
    sums = None
    for step in range(2):
        if step > 0:
            u, res, low, high = call(
                advance_kernel, packs, (u, d, sums, *local), residual_scratch()
            )
        tlo, thi = both_ways("narrow", high, low)
        wide_field, down, up = call(
            around_widen_kernel,
            [((3, 8, 72, 128), F32), ((3, 2, 72, 128), F32), ((3, 2, 72, 128), F32)],
            (res, tlo, thi),
        )
        zlo, zhi = both_ways("wide", up, down)
        corr, low, high = call(
            solve_kernel,
            [(FIELD, F32), ((3, 8, 128), F32), ((3, 8, 128), F32)],
            (wide_field, zlo, zhi, vectors, forward, inverse, scale),
            [
                pltpu.VMEM((480, 256), BF16),
                pltpu.VMEM((3, 10, 112, 128), F32),
                pltpu.VMEM((12, 336, 256), BF16),
            ],
            spaces={3: smem},
        )
        d, part = call(
            direction_kernel,
            [(FIELD, F32), ((128, 128), F32)],
            (*sum_rounds(corr, low, high), res, lanes, grad, wjk),
            [pltpu.VMEM((12, 256, 256), BF16), pltpu.VMEM((2, 16, 128), F32)],
        )
        sums = lax.all_to_all(part, BOTH, 0, 0, tiled=True)
    out, dense = call(
        last_kernel,
        [(FIELD, F32), ((128, 408), F32)],
        (u, d, sums, *local, slot, place),
        [pltpu.VMEM(FIELD, F32), pltpu.VMEM(FIELD, F32)] + residual_scratch(),
    )
    coarse = jnp.sum(lax.all_to_all(dense, BOTH, 0, 0, tiled=True), axis=0)
    return out.reshape(3, 512, 128), coarse.reshape(3, 136)


def solution(mesh):
    return jax.shard_map(
        shards,
        mesh=mesh,
        in_specs=(P(None, None, BOTH), P(BOTH, None), P(None, BOTH), P("wide"), P(), P(), P(), P()),
        out_specs=(P(None, None, BOTH), P(None, BOTH)),
        check_vma=False,
    )
```

```python
from functools import partial

import jax
import jax.numpy as jnp
import ml_dtypes
import numpy as np
from jax import lax
from jax.experimental import pallas as pl
from jax.experimental.pallas import tpu as pltpu
from jax.sharding import PartitionSpec as P

RADIAL = 16
SIGMA = 4.0
VISCOSITY = 0.05
F32 = jnp.float32
BF16 = jnp.bfloat16
EXACT = lax.Precision.HIGHEST
BOTH = ("wide", "narrow")


def node_tables():
    x = np.array(
        [-1.0, -0.8717401485096066, -0.5917001814331423, -0.2092992179024789]
    )
    x = np.concatenate([x, -x[::-1]])
    w = np.array([1.0 / 28.0, 0.2107042271435061, 0.3411226924835044, 0.4124587946587038])
    w = np.concatenate([w, w[::-1]])
    scale = np.array([np.prod([x[t] - x[p] for p in range(8) if p != t]) for t in range(8)])
    deriv = np.zeros((8, 8))
    for t in range(8):
        for s in range(8):
            if t != s:
                deriv[t, s] = scale[t] / (scale[s] * (x[t] - x[s]))
        deriv[t, t] = -np.sum(deriv[t])
    y = np.array(
        [
            -0.9815606342467192,
            -0.9041172563704749,
            -0.7699026741943047,
            -0.5873179542866175,
            -0.3678314989981802,
            -0.1252334085114689,
        ]
    )
    y = np.concatenate([y, -y[::-1]])
    v = np.array(
        [
            0.0471753363865118,
            0.1069393259953184,
            0.1600783285433462,
            0.2031674267230659,
            0.2334925365383548,
            0.2491470458134028,
        ]
    )
    v = np.concatenate([v, v[::-1]])
    interp = np.ones((12, 8))
    for s in range(8):
        for p in range(8):
            if p != s:
                interp[:, s] = interp[:, s] * (y - x[p]) / (x[s] - x[p])
    linear = np.stack([(1.0 - x) / 2.0, (1.0 + x) / 2.0])
    return w, deriv, v, interp, linear


W, D, VF, J, LIN = node_tables()
B = J @ D
JV = J.T * VF[None, :]
STIFF = D.T @ (W[:, None] * D)
WJK = np.kron(W, W)


def two_parts(matrix):
    hi = matrix.astype(np.float32).astype(ml_dtypes.bfloat16)
    lo = (matrix - hi.astype(np.float64)).astype(ml_dtypes.bfloat16)
    return hi, lo


def four_terms(matrix):
    hi, lo = two_parts(matrix)
    return np.concatenate([hi, lo, hi, lo], axis=1)


def three_terms(matrix):
    hi, lo = two_parts(matrix)
    return np.concatenate([hi, lo, hi], axis=1)


FINE = four_terms(np.concatenate([np.kron(J, J), np.kron(B, J), np.kron(J, B)]))
BACK = three_terms(np.kron(JV, JV))
STIFF_JK = four_terms(
    np.concatenate([np.kron(STIFF, np.diag(W)), np.kron(np.diag(W), STIFF)])
)
GRAD_JK = four_terms(np.concatenate([np.kron(D, np.eye(8)), np.kron(np.eye(8), D)]))


def call(kernel, outs, args, scratch=(), spaces=None, hbm_out=()):
    spaces = spaces or {}
    args = [
        pltpu.with_memory_space_constraint(a, spaces.get(i, pltpu.VMEM))
        for i, a in enumerate(args)
    ]
    return pl.pallas_call(
        kernel,
        out_shape=[
            jax.ShapeDtypeStruct(s, d) if i in hbm_out else pltpu.VMEM(s, d)
            for i, (s, d) in enumerate(outs)
        ],
        in_specs=[
            pl.BlockSpec(memory_space=spaces.get(i, pltpu.VMEM)) for i in range(len(args))
        ],
        out_specs=[pl.BlockSpec(memory_space=pltpu.VMEM) for _ in outs],
        scratch_shapes=list(scratch),
        compiler_params=pltpu.CompilerParams(vmem_limit_bytes=32 << 20),
        name=kernel.func.__name__ if isinstance(kernel, partial) else kernel.__name__,
    )(*args)


def iota(shape, dim):
    return lax.broadcasted_iota(jnp.int32, shape, dim)


def lanes_by(x, shift):
    return pltpu.roll(x, shift % x.shape[-1], x.ndim - 1)


def rows_by(x, shift):
    return pltpu.roll(x, shift % 8, x.ndim - 2)


def split(x):
    hi = x.astype(BF16)
    return hi, (x - hi.astype(F32)).astype(BF16)


def dot(a, b):
    return jnp.dot(a, b, preferred_element_type=F32)


def even_odd(matrix, xs, sign):
    n_out, n_in = matrix.shape
    half = n_in // 2
    even = [xs[i] + xs[n_in - 1 - i] for i in range(half)]
    odd = [xs[i] - xs[n_in - 1 - i] for i in range(half)]
    outs = [None] * n_out
    for a in range(n_out // 2):
        e = sum(
            float((matrix[a, i] + matrix[a, n_in - 1 - i]) / 2) * even[i] for i in range(half)
        )
        o = sum(
            float((matrix[a, i] - matrix[a, n_in - 1 - i]) / 2) * odd[i] for i in range(half)
        )
        outs[a] = e + o
        outs[n_out - 1 - a] = e - o if sign > 0 else o - e
    return outs


def keep_rows(rows):
    k = iota((rows, 128), 0) & 7
    r = iota((rows, 128), 1) & (RADIAL - 1)
    wall = ((k == 0) & (r == 0)) | ((k == 7) & (r == RADIAL - 1))
    return jnp.where(wall, 0.0, 1.0).astype(F32)


def radial_parts(x):
    r = iota((8, 128), 1) & (RADIAL - 1)
    below = jnp.where(r > 0, lanes_by(x, 1), 0.0)
    above = jnp.where(r < RADIAL - 1, lanes_by(x, -1), 0.0)
    return below, above


def radial_sum(x, below, above):
    k = iota((8, 128), 0)
    return x + jnp.where(k == 0, rows_by(below, 1), jnp.where(k == 7, rows_by(above, -1), 0.0))


def pack_low(plane_of):
    et = iota((8, 128), 1) >> 4
    out = jnp.zeros((8, 128), F32)
    for i in range(8):
        out = jnp.where(et == i, lanes_by(plane_of(i), 16 * i), out)
    return out


def pack_high(plane_of):
    et = iota((8, 128), 1) >> 4
    out = jnp.zeros((8, 128), F32)
    for i in range(8):
        out = jnp.where(et == i, lanes_by(plane_of(i), 16 * i + 16), out)
    return out


def from_low(plane, packed, i):
    lane = iota((8, 128), 1)
    return jnp.where(lane < 16, lanes_by(packed, -16 * i), lanes_by(plane, 16))


def from_high(plane, packed, i):
    lane = iota((8, 128), 1)
    return jnp.where(lane >= 112, lanes_by(packed, 112 - 16 * i), lanes_by(plane, -16))


def start_kernel(vel, slot, arc, rad, axial, mv, low, high, lanes):
    ht = jnp.broadcast_to(arc[...], (8, 16))
    hr = jnp.broadcast_to(rad[...], (8, 16))
    spread = ((iota((16, 256), 1) & 15) == iota((16, 256), 0)).astype(F32)
    ht = jnp.dot(ht, spread, precision=EXACT, preferred_element_type=F32)[0:1]
    hr = jnp.dot(hr, spread, precision=EXACT, preferred_element_type=F32)[0:1]
    hz = jnp.zeros((1, 256), F32) + axial[0]
    g = ht * hr / 8.0
    vol = hz * g
    r = iota((1, 256), 1) & (RADIAL - 1)
    g_low = g + jnp.where(r > 0, lanes_by(g, 1), 0.0)
    g_high = g + jnp.where(r < RADIAL - 1, lanes_by(g, -1), 0.0)
    rows = [
        vol,
        vol * (2.0 / hz),
        vol * (2.0 / ht),
        vol * (2.0 / hr),
        VISCOSITY * vol * (2.0 / hz) * (2.0 / hz),
        VISCOSITY * vol * (2.0 / ht) * (2.0 / ht),
        VISCOSITY * vol * (2.0 / hr) * (2.0 / hr),
        hz,
        1.0 / g,
        1.0 / g_low,
        1.0 / g_high,
    ]
    for n, row in enumerate(rows):
        lanes[n : n + 1] = row
    for n in range(len(rows), 16):
        lanes[n : n + 1] = jnp.zeros((1, 256), F32)
    hot = (slot[...] == iota((128, 128), 0)).astype(F32)
    nt = (((1,), (1,)), ((), ()))

    def body(c, carry):
        x = vel[c].reshape(512, 128)
        y = lax.dot_general(x, hot, nt, precision=EXACT, preferred_element_type=F32)
        mv[c] = (y * vol[:, :128]).reshape(8, 64, 128)
        low[c] = pack_low(lambda i: mv[c, i, 0:8])
        high[c] = pack_high(lambda i: mv[c, i, 56:64])
        return carry

    lax.fori_loop(0, 3, body, 0)


def solve_tables_kernel(vectors, values, lanes, forward, inverse, scale):
    s = vectors[...]
    ident = (iota((10, 10), 0) == iota((10, 10), 1)).astype(F32)
    st = lax.dot_general(
        ident, s, (((1,), (1,)), ((), ())), precision=EXACT, preferred_element_type=F32
    )

    def mul(a, b):
        return jnp.dot(a, b, precision=EXACT, preferred_element_type=F32)

    row, col = iota((112, 10), 0), iota((112, 10), 1)
    live = row < 100
    by_b = ((row // 10 == col) & live).astype(F32)
    by_c = ((row % 10 == col) & live).astype(F32)
    node, pos = iota((10, 160), 0), iota((10, 160), 1)
    slot = pos & 15
    k_of = jnp.where(slot < 8, slot + 1, jnp.where(slot == 8, 0, jnp.where(slot == 9, 9, -1)))
    by_j = (node == (pos >> 4)).astype(F32)
    by_k = (node == k_of).astype(F32)
    full = mul(mul(by_b, st), by_j) * mul(mul(by_c, st), by_k)
    hi, lo = split(full)
    forward[:, 0:160] = hi
    forward[:, 160:320] = lo
    forward[:, 320:480] = hi

    row8, col8 = iota((64, 10), 0), iota((64, 10), 1)
    by_j8 = ((row8 >> 3) + 1 == col8).astype(F32)
    by_k8 = ((row8 & 7) + 1 == col8).astype(F32)
    node2, pos2 = iota((10, 112), 0), iota((10, 112), 1)
    b_of = jnp.where(pos2 < 100, pos2 // 10, -1)
    c_of = jnp.where(pos2 < 100, pos2 % 10, -1)
    to_b = (node2 == b_of).astype(F32)
    to_c = (node2 == c_of).astype(F32)
    full = mul(mul(by_j8, s), to_b) * mul(mul(by_k8, s), to_c)
    hi, lo = split(full)
    inverse[:, 0:112] = hi
    inverse[:, 112:224] = lo
    inverse[:, 224:336] = hi

    lam = jnp.broadcast_to(values[...], (8, 10))
    nt = (((1,), (1,)), ((), ()))
    lam_b = lax.dot_general(by_b, lam, nt, precision=EXACT, preferred_element_type=F32)[:, 0:1]
    lam_c = lax.dot_general(by_c, lam, nt, precision=EXACT, preferred_element_type=F32)[:, 0:1]
    vol = lanes[0:1, :128]
    flat = (
        SIGMA * vol
        + lam_b * jnp.broadcast_to(lanes[5:6, :128], (112, 128))
        + lam_c * jnp.broadcast_to(lanes[6:7, :128], (112, 128))
    )
    for a in range(10):
        scale[a] = 1.0 / (flat + values[0:1, a : a + 1] * lanes[4:5, :128])


def around_sum_kernel(field, tlo, thi, lanes, out, down, up):
    def body(c, carry):
        lo, hi = tlo[c], thi[c]
        for i in range(8):
            x = field[c, i]
            first, last = x[0:8], x[56:64]
            head = first + from_low(last, lo, i)
            tail = last + from_high(first, hi, i)
            out[c, i] = x
            out[c, i, 0:8] = head
            out[c, i, 56:64] = tail
        base = pl.multiple_of(c * 64, 64)
        down[pl.ds(base, 64)] = out[c, 0]
        up[pl.ds(base, 64)] = out[c, 7]
        return carry

    lax.fori_loop(0, 3, body, 0)
    hz = jnp.broadcast_to(lanes[7:8, :128], (8, 128))
    down[192:200] = hz
    up[192:200] = hz


def finish_sum(field, zlo, zhi, out, factor):
    def body(c, carry):
        base = pl.multiple_of(c * 64, 64)
        for i in range(8):
            x = field[c, i]
            if i == 0:
                x = x + zlo[pl.ds(base, 64)]
            if i == 7:
                x = x + zhi[pl.ds(base, 64)]
            for j in range(8):
                v = x[8 * j : 8 * j + 8]
                below, above = radial_parts(v)
                out[c, i, 8 * j : 8 * j + 8] = radial_sum(v, below, above) * factor(i, j)
        return carry

    lax.fori_loop(0, 3, body, 0)


def put(ref, at, rb, half, x):
    hi, lo = split(x)
    for term, part in enumerate((hi, hi, lo, lo)):
        rows = pl.ds(pl.multiple_of(term * 64 + rb * 16, 16), 16)
        ref[at, rows, half * 128 : half * 128 + 128] = part


def along_pipe(u, xu, xw, xs=None, sz=None):
    def body(t, carry):
        c, rb = t // 4, t % 4
        rows = pl.ds(pl.multiple_of(rb * 16, 16), 16)
        x = [u[c, i, rows] for i in range(8)]
        for a, val in enumerate(even_odd(J, x, 1)):
            put(xu, c * 6 + a // 2, rb, a % 2, val)
        for a, val in enumerate(even_odd(B, x, -1)):
            put(xw, c * 6 + a // 2, rb, a % 2, val)
        if xs is None:
            return carry
        for i in range(8):
            put(xs, c * 4 + i // 2, rb, i % 2, x[i])
        for i, val in enumerate(even_odd(STIFF, x, 1)):
            sz[c, i, rows] = val
        return carry

    lax.fori_loop(0, 12, body, 0)


def fine_dots(p, at, fine, xu, xw, pf, qf):
    for c in range(3):
        pf[at, c] = dot(fine[...], xu[c * 6 + p])
        qf[at, c] = dot(fine[0:144], xw[c * 6 + p])


def stiff_dots(p, stiff, xs, ks):
    for t in (2 * p, 2 * p + 1):
        y = dot(stiff[...], xs[t])
        c, q = t // 4, t % 4
        ks[c, 2 * q] = y[:, :128]
        ks[c, 2 * q + 1] = y[:, 128:]


def put_conv(xc, c, r, conv):
    hi, lo = split(conv)
    xc[c, 16 * r : 16 * r + 16] = hi
    xc[c, 144 + 16 * r : 160 + 16 * r] = hi
    xc[c, 288 + 16 * r : 304 + 16 * r] = lo


def back_dots(p, back, xc, yf, count):
    for c in range(count):
        y = dot(back[...], xc[c])
        yf[c, 2 * p] = y[:, :128]
        yf[c, 2 * p + 1] = y[:, 128:]


def fine_rows(pf, qf, p, c, r):
    rows = slice(16 * r, 16 * r + 16)
    return (
        qf[p, c, rows],
        pf[p, c, 144 + 16 * r : 160 + 16 * r],
        pf[p, c, 288 + 16 * r : 304 + 16 * r],
    )


def velocity_rows(pf, lanes, p, r):
    rows = slice(16 * r, 16 * r + 16)
    return [pf[p, n, rows] * lanes[n + 1 : n + 2] for n in range(3)]


def stiff_plane(lanes, wjk, sz, ks, c, i, rb):
    rows = pl.ds(pl.multiple_of(rb * 16, 16), 16)
    more = pl.ds(pl.multiple_of(64 + rb * 16, 16), 16)
    kz, kt, kr = lanes[4:5, :128], lanes[5:6, :128], lanes[6:7, :128]
    plane = kt * ks[c, i, rows] + kr * ks[c, i, more]
    return wjk[rows] * kz * sz[c, i, rows] + float(W[i]) * plane


def residual(u, lanes, fine, back, stiff, wjk, res, pf, qf, xu, xw, xs, xc0, xc1, yf, sz, ks):
    along_pipe(u, xu, xw, xs, sz)
    fine_dots(0, 0, fine, xu, xw, pf, qf)
    for p in range(6):
        if p < 5:
            fine_dots(p + 1, (p + 1) % 2, fine, xu, xw, pf, qf)
        stiff_dots(p, stiff, xs, ks)
        xc = (xc0, xc1)[p % 2]
        for r in range(9):
            v = velocity_rows(pf, lanes, p % 2, r)
            for c in range(3):
                g = fine_rows(pf, qf, p % 2, c, r)
                put_conv(xc, c, r, v[0] * g[0] + v[1] * g[1] + v[2] * g[2])
        back_dots(p, back, xc, yf, 3)
    keep = keep_rows(16)

    def body(t, carry):
        c, rb = t // 4, t % 4
        rows = pl.ds(pl.multiple_of(rb * 16, 16), 16)
        adv = even_odd(JV, [yf[c, a, rows] for a in range(12)], 1)
        for i in range(8):
            res[c, i, rows] = -(adv[i] + stiff_plane(lanes, wjk, sz, ks, c, i, rb)) * keep
        return carry

    lax.fori_loop(0, 12, body, 0)


def change_kernel(
    u, d, lanes, fine, back, stiff, wjk, lin, quad, pf, qf, xu, xw, pd, qd, xd, xe, xs,
    xc0, xc1, yf, sz, ks
):
    along_pipe(u, xu, xw)
    along_pipe(d, xd, xe, xs, sz)
    fine_dots(0, 0, fine, xu, xw, pf, qf)
    fine_dots(0, 0, fine, xd, xe, pd, qd)
    for p in range(6):
        if p < 5:
            fine_dots(p + 1, (p + 1) % 2, fine, xu, xw, pf, qf)
            fine_dots(p + 1, (p + 1) % 2, fine, xd, xe, pd, qd)
        stiff_dots(p, stiff, xs, ks)
        xc = (xc0, xc1)[p % 2]
        for r in range(9):
            v = velocity_rows(pf, lanes, p % 2, r)
            w = velocity_rows(pd, lanes, p % 2, r)
            for c in range(3):
                g = fine_rows(pf, qf, p % 2, c, r)
                h = fine_rows(pd, qd, p % 2, c, r)
                put_conv(
                    xc,
                    c,
                    r,
                    (v[0] * h[0] + v[1] * h[1] + v[2] * h[2])
                    + (w[0] * g[0] + w[1] * g[1] + w[2] * g[2]),
                )
                put_conv(xc, 3 + c, r, w[0] * h[0] + w[1] * h[1] + w[2] * h[2])
        back_dots(p, back, xc, yf, 6)
    keep = keep_rows(16)

    def body(t, carry):
        c, rb = t // 4, t % 4
        rows = pl.ds(pl.multiple_of(rb * 16, 16), 16)
        one = even_odd(JV, [yf[c, a, rows] for a in range(12)], 1)
        two = even_odd(JV, [yf[3 + c, a, rows] for a in range(12)], 1)
        for i in range(8):
            lin[c, i, rows] = -(one[i] + stiff_plane(lanes, wjk, sz, ks, c, i, rb)) * keep
            quad[c, i, rows] = -two[i] * keep
        return carry

    lax.fori_loop(0, 12, body, 0)


def pack_two(res, low, high):
    def body(c, carry):
        for n in range(2):
            low[c, 8 * n : 8 * n + 8] = pack_low(lambda i: res[c, i, 8 * n : 8 * n + 8])
            high[c, 8 * n : 8 * n + 8] = pack_high(
                lambda i: res[c, i, 48 + 8 * n : 56 + 8 * n]
            )
        return carry

    lax.fori_loop(0, 3, body, 0)


def project_kernel(
    field, zlo, zhi, lanes, fine, back, stiff, wjk, u, res, low, high, *scratch
):
    hz = lanes[7:8, :128]
    inner = 1.0 / hz
    first = 1.0 / (hz + zlo[192:193])
    last = 1.0 / (hz + zhi[192:193])
    k = iota((8, 128), 0)
    rk = jnp.where(
        k == 0, lanes[9:10, :128], jnp.where(k == 7, lanes[10:11, :128], lanes[8:9, :128])
    )
    rk = rk * keep_rows(8)
    by_plane = {0: rk * first, 7: rk * last}
    middle = rk * inner

    def factor(i, j):
        f = by_plane.get(i, middle)
        return 0.5 * f if j in (0, 7) else f

    finish_sum(field, zlo, zhi, u, factor)
    residual(u, lanes, fine, back, stiff, wjk, res, *scratch)
    pack_two(res, low, high)


def step_length(sums):
    total = jnp.sum(sums[...], axis=0, keepdims=True)
    return total[:, 0:1] / total[:, 1:2]


def advance_kernel(u_old, d, sums, lanes, fine, back, stiff, wjk, u, res, low, high, *scratch):
    alpha = step_length(sums)

    def body(t, carry):
        c, i = t // 8, t % 8
        u[c, i] = u_old[c, i] + alpha * d[c, i]
        return carry

    lax.fori_loop(0, 24, body, 0)
    residual(u, lanes, fine, back, stiff, wjk, res, *scratch)
    pack_two(res, low, high)


def around_widen_kernel(res, tlo, thi, out, down, up):
    lane = iota((8, 128), 1)

    def body(c, carry):
        lo6, lo7, hi0, hi1 = tlo[c, 0:8], tlo[c, 8:16], thi[c, 0:8], thi[c, 8:16]
        for i in range(8):
            x = res[c, i]
            first, last = x[0:8], x[56:64]
            out[c, i, 0:64] = x
            out[c, i, 0:8] = first + from_low(last, lo7, i)
            out[c, i, 56:64] = last + from_high(first, hi0, i)
            out[c, i, 64:72] = jnp.where(
                lane < 64, lanes_by(lo6, -16 * i), lanes_by(hi1, 112 - 16 * i)
            )
        for n in range(2):
            down[c, n] = out[c, n]
            up[c, n] = out[c, 6 + n]
        return carry

    lax.fori_loop(0, 3, body, 0)


def widen_planes(e, xf, half):
    lane, k = iota((8, 128), 1), iota((8, 128), 0)
    extra = e[64:72]
    planes = [e[8 * j : 8 * j + 8] for j in range(8)]
    under = jnp.where(lane < 16, extra, lanes_by(planes[6], 16))
    over = jnp.where(lane >= 112, extra, lanes_by(planes[1], -16))
    cols = slice(half * 128, half * 128 + 128)
    for j, v in enumerate([under] + planes + [over]):
        below, above = radial_parts(v)
        own = radial_sum(v, below, above)
        side = jnp.where(k == 0, rows_by(below, 2), jnp.where(k == 1, above, 0.0))
        hi, lo = split(jnp.concatenate([own, side], axis=0))
        xf[16 * j : 16 * j + 16, cols] = hi
        xf[160 + 16 * j : 176 + 16 * j, cols] = hi
        xf[320 + 16 * j : 336 + 16 * j, cols] = lo


def transform_kernel(field, forward, out, *xf):
    def body(c, carry):
        for p in range(4):
            buf = xf[p % 2]
            for half in range(2):
                widen_planes(field[c, 2 * p + half], buf, half)
            y = dot(forward[...], buf[...])
            out[c, 2 * p] = y[:, :128]
            out[c, 2 * p + 1] = y[:, 128:]
        return carry

    lax.fori_loop(0, 3, body, 0)


def solve_kernel(
    own, zlo, zhi, vectors, forward, inverse, scale, corr, low, high, xf0, xf1, yf, xb
):
    def body(c, carry):
        for buf, halo, at in ((xf0, zlo, 0), (xf1, zhi, 8)):
            widen_planes(halo[c, 0], buf, 0)
            widen_planes(halo[c, 1], buf, 1)
        y0, y1 = dot(forward[...], xf0[...]), dot(forward[...], xf1[...])
        yf[c, 0] = y0[:, :128]
        yf[c, 1] = y0[:, 128:] + own[c, 0]
        yf[c, 2] = y1[:, :128] + own[c, 7]
        yf[c, 3] = y1[:, 128:]
        return carry

    lax.fori_loop(0, 3, body, 0)

    def mid(t, carry):
        c, rb = t // 7, t % 7
        rows = pl.ds(pl.multiple_of(rb * 16, 16), 16)
        y = (
            [yf[c, 0, rows], yf[c, 1, rows]]
            + [own[c, i, rows] for i in range(1, 7)]
            + [yf[c, 2, rows], yf[c, 3, rows]]
        )
        spec = []
        for a in range(10):
            acc = vectors[0, a] * y[0]
            for i in range(1, 10):
                acc = acc + vectors[i, a] * y[i]
            spec.append(acc * scale[a, rows])
        for i in range(8):
            acc = vectors[i + 1, 0] * spec[0]
            for a in range(1, 10):
                acc = acc + vectors[i + 1, a] * spec[a]
            hi, lo = split(acc)
            cols = slice((i % 2) * 128, (i % 2) * 128 + 128)
            for term, part in enumerate((hi, hi, lo)):
                xb[c * 4 + i // 2, pl.ds(pl.multiple_of(term * 112 + rb * 16, 16), 16),
                   cols] = part
        return carry

    lax.fori_loop(0, 21, mid, 0)

    k = iota((8, 128), 0)
    r = iota((8, 128), 1) & (RADIAL - 1)
    inner = ((k == 0) & (r > 0)) | ((k == 7) & (r < RADIAL - 1))
    share = jnp.where(inner, 0.5, 1.0).astype(F32)
    for t in range(12):
        c, p = t // 4, t % 4
        y = dot(inverse[...], xb[t])
        for half in range(2):
            i = 2 * p + half
            for j in range(8):
                f = (0.5 if i in (0, 7) else 1.0) * (0.5 if j in (0, 7) else 1.0)
                corr[c, i, 8 * j : 8 * j + 8] = (
                    y[8 * j : 8 * j + 8, half * 128 : half * 128 + 128] * (share * f)
                )

    def last(c, carry):
        low[c] = pack_low(lambda i: corr[c, i, 0:8])
        high[c] = pack_high(lambda i: corr[c, i, 56:64])
        return carry

    lax.fori_loop(0, 3, last, 0)


def direction_kernel(field, zlo, zhi, res, lanes, grad, wjk, d, sums, xs, acc):
    keep = keep_rows(8)
    finish_sum(field, zlo, zhi, d, lambda i, j: keep)
    acc[...] = jnp.zeros_like(acc)
    vol = lanes[0:1, :128]
    kz, kt, kr = lanes[4:5, :128], lanes[5:6, :128], lanes[6:7, :128]

    def first(t, carry):
        c, rb = t // 4, t % 4
        rows = pl.ds(pl.multiple_of(rb * 16, 16), 16)
        x = [d[c, i, rows] for i in range(8)]
        num = sum(x[i] * res[c, i, rows] for i in range(8))
        sq = sum(float(W[i]) * (x[i] * x[i]) for i in range(8))
        gz = sum(float(W[i]) * (g * g) for i, g in enumerate(even_odd(D, x, -1)))
        acc[0] += num
        acc[1] += wjk[rows] * (SIGMA * vol * sq + kz * gz)
        for i in range(8):
            hi, lo = split(x[i])
            for term, part in enumerate((hi, hi, lo, lo)):
                xs[c * 4 + i // 2, pl.ds(pl.multiple_of(term * 64 + rb * 16, 16), 16),
                   (i % 2) * 128 : (i % 2) * 128 + 128] = part
        return carry

    lax.fori_loop(0, 12, first, 0)

    def second(c, carry):
        total = jnp.zeros((16, 128), F32)
        for p in range(4):
            y = dot(grad[...], xs[c * 4 + p])
            for half in range(2):
                v = y[:, half * 128 : half * 128 + 128]
                v = v * v
                plane = jnp.zeros((16, 128), F32)
                for q in range(4):
                    rows = slice(16 * q, 16 * q + 16)
                    plane = plane + wjk[rows] * (
                        kt * v[rows] + kr * v[64 + 16 * q : 80 + 16 * q]
                    )
                total = total + float(W[2 * p + half]) * plane
        acc[1] += total
        return carry

    lax.fori_loop(0, 3, second, 0)
    num = jnp.sum(jnp.sum(acc[0], axis=0, keepdims=True), axis=1, keepdims=True)
    den = jnp.sum(jnp.sum(acc[1], axis=0, keepdims=True), axis=1, keepdims=True)
    at = iota((128, 128), 1)
    sums[...] = jnp.where(at == 0, num, jnp.where(at == 1, den, 0.0))


def route_kernel(slot, corner, inside, owner):
    hot = (slot[...] == iota((128, 128), 0)).astype(F32)
    nt = (((1,), (1,)), ((), ()))
    ids = corner[...].astype(F32)
    by_elem = lax.dot_general(hot, ids, nt, precision=EXACT, preferred_element_type=F32)
    by_corner = lax.dot_general(ids, hot, nt, precision=EXACT, preferred_element_type=F32)
    owner[...] = (by_corner + 0.5).astype(jnp.int32) // 136
    ids = (by_elem + 0.5).astype(jnp.int32)
    inside[...] = ids - ids // 136 * 136


def route_corners_kernel(res, lin, quad, inside, owner, part, dense, left, right):
    row, col = iota((8, 64), 0), iota((8, 64), 1)

    def weight(node, upper):
        acc = jnp.zeros((8, 64), F32)
        for n in range(8):
            acc = jnp.where(
                node == n, jnp.where(upper, float(LIN[1, n]), float(LIN[0, n])), acc
            )
        return acc

    corner_jk = weight(col >> 3, (row & 2) != 0) * weight(col & 7, (row & 1) != 0)
    pos, dev = iota((128, 256), 1), iota((128, 128), 0)
    for q in range(8):
        right[128 * q : 128 * q + 128] = (inside[:, q : q + 1] == pos).astype(F32).astype(BF16)
    for n, ref in enumerate((res, lin, quad)):
        for c in range(3):
            planes = [ref[c, i] for i in range(8)]
            z1 = sum(float(LIN[1, i]) * planes[i] for i in range(1, 8))
            z0 = sum(float(LIN[0, i]) * planes[i] for i in range(7))
            both = jnp.dot(
                corner_jk,
                jnp.concatenate([z0, z1], axis=1),
                precision=EXACT,
                preferred_element_type=F32,
            )
            hi = both.astype(BF16).astype(F32)
            mid = (both - hi).astype(BF16).astype(F32)
            for q in range(8):
                mine = owner[q : q + 1] == dev
                cols = slice((q // 4) * 128, (q // 4) * 128 + 128)
                for m, piece in enumerate((hi, mid, both - hi - mid)):
                    at = (3 * c + m) * 128
                    left[at : at + 128, 128 * q : 128 * q + 128] = jnp.where(
                        mine, piece[q % 4 : q % 4 + 1, cols], 0.0
                    ).astype(BF16)
        y = dot(left[...], right[...])
        for c in range(3):
            block = 3 * n + c
            total = (
                y[384 * c : 384 * c + 128]
                + y[384 * c + 128 : 384 * c + 256]
                + y[384 * c + 256 : 384 * c + 384]
            )
            total = lanes_by(total, 8 * block)
            first = slice(128 * block, 128 * block + 128)
            dense[:, first] = total[:, :128] if block == 0 else dense[:, first] + total[:, :128]
            dense[:, 128 * block + 128 : 128 * block + 256] = total[:, 128:]
    dense[:, 1152:1280] += lanes_by(part[...], 72)


def store_kernel(u, d, slot, u_out, d_out):
    hot = (slot[...] == iota((128, 128), 0)).astype(F32)

    def body(c, carry):
        for x, y in ((u, u_out), (d, d_out)):
            flat = x[c].reshape(512, 128)
            y[c] = jnp.dot(flat, hot, precision=EXACT, preferred_element_type=F32).reshape(
                8, 64, 128
            )
        return carry

    lax.fori_loop(0, 3, body, 0)


def end_kernel(u, d, total, vel, coarse):
    alpha = total[0:1, 1224:1225] / total[0:1, 1225:1226]
    one, two = lanes_by(total[...], -408), lanes_by(total[...], -816)
    coarse[...] = (total[...] + alpha * (one + alpha * two))[0:1, 0:512]

    def body(t, carry):
        c, i = t // 8, t % 8
        vel[c, i] = u[c, i] + alpha * d[c, i]
        return carry

    lax.fori_loop(0, 24, body, 0)


FIELD = (3, 8, 64, 128)


def both_ways(axis, to_next, to_prev):
    n = lax.axis_size(axis)
    up = [(i, (i + 1) % n) for i in range(n)]
    down = [((i + 1) % n, i) for i in range(n)]
    return lax.ppermute(to_next, axis, up), lax.ppermute(to_prev, axis, down)


def fine_scratch():
    return [
        pltpu.VMEM((2, 3, 432, 256), F32),
        pltpu.VMEM((2, 3, 144, 256), F32),
        pltpu.VMEM((18, 256, 256), BF16),
        pltpu.VMEM((18, 256, 256), BF16),
    ]


def local_scratch(count):
    return [
        pltpu.VMEM((12, 256, 256), BF16),
        pltpu.VMEM((count, 432, 256), BF16),
        pltpu.VMEM((count, 432, 256), BF16),
        pltpu.VMEM((count, 12, 64, 128), F32),
        pltpu.VMEM(FIELD, F32),
        pltpu.VMEM((3, 8, 128, 128), F32),
    ]


def shards(vel, slot, corner, axial, arc, rad, vectors, values):
    fine, back, stiff, grad = (jnp.asarray(m) for m in (FINE, BACK, STIFF_JK, GRAD_JK))
    wjk = jnp.asarray(np.broadcast_to(WJK[:, None], (64, 128)).astype(np.float32))
    smem = pltpu.SMEM
    small = ((3, 8, 128), F32)
    mv, low, high, lanes = call(
        start_kernel,
        [(FIELD, F32), small, small, ((16, 256), F32)],
        (vel.reshape(FIELD), slot, arc[None], rad[None], axial),
        spaces={4: smem},
    )
    inside, owner = call(
        route_kernel,
        [((128, 8), jnp.int32), ((8, 128), jnp.int32)],
        (slot, corner),
    )
    forward, inverse, scale = call(
        solve_tables_kernel,
        [((112, 480), BF16), ((64, 336), BF16), ((10, 112, 128), F32)],
        (vectors, values[None], lanes),
    )

    def sum_rounds(field, low, high):
        tlo, thi = both_ways("narrow", high, low)
        out, down, up = call(
            around_sum_kernel,
            [(FIELD, F32), ((200, 128), F32), ((200, 128), F32)],
            (field, tlo, thi, lanes),
        )
        zlo, zhi = both_ways("wide", up, down)
        return out, zlo, zhi

    fine, back, stiff, wjk, grad, mv = lax.optimization_barrier((fine, back, stiff, wjk, grad, mv))
    local = (lanes, fine, back, stiff, wjk)
    packs = [(FIELD, F32), (FIELD, F32), ((3, 16, 128), F32), ((3, 16, 128), F32)]
    u, res, low, high = call(
        project_kernel,
        packs,
        (*sum_rounds(mv, low, high), *local),
        fine_scratch() + local_scratch(3),
    )
    for step in range(2):
        if step > 0:
            sums = lax.all_to_all(part, BOTH, 0, 0, tiled=True)
            u, res, low, high = call(
                advance_kernel, packs, (u, d, sums, *local), fine_scratch() + local_scratch(3)
            )
        tlo, thi = both_ways("narrow", high, low)
        wide_field, down, up = call(
            around_widen_kernel,
            [((3, 8, 72, 128), F32), ((3, 2, 72, 128), F32), ((3, 2, 72, 128), F32)],
            (res, tlo, thi),
        )
        zlo, zhi = both_ways("wide", up, down)
        (own,) = call(
            transform_kernel,
            [((3, 8, 112, 128), F32)],
            (wide_field, forward),
            [pltpu.VMEM((480, 256), BF16), pltpu.VMEM((480, 256), BF16)],
        )
        zlo, zhi, own = lax.optimization_barrier((zlo, zhi, own))
        corr, low, high = call(
            solve_kernel,
            [(FIELD, F32), small, small],
            (own, zlo, zhi, vectors, forward, inverse, scale),
            [
                pltpu.VMEM((480, 256), BF16),
                pltpu.VMEM((480, 256), BF16),
                pltpu.VMEM((3, 4, 112, 128), F32),
                pltpu.VMEM((12, 336, 256), BF16),
            ],
            spaces={3: smem},
        )
        d, part = call(
            direction_kernel,
            [(FIELD, F32), ((128, 128), F32)],
            (*sum_rounds(corr, low, high), res, lanes, grad, wjk),
            [pltpu.VMEM((12, 256, 256), BF16), pltpu.VMEM((2, 16, 128), F32)],
        )
    lin, quad = call(
        change_kernel,
        [(FIELD, F32), (FIELD, F32)],
        (u, d, *local),
        fine_scratch() + fine_scratch() + local_scratch(6),
    )
    (dense,) = call(
        route_corners_kernel,
        [((128, 1280), F32)],
        (res, lin, quad, inside, owner, part),
        [pltpu.VMEM((1152, 1024), BF16), pltpu.VMEM((1024, 256), BF16)],
    )
    parts = lax.all_to_all(dense, BOTH, 0, 0, tiled=True)
    u, d = call(store_kernel, [(FIELD, F32), (FIELD, F32)], (u, d, slot))
    total = jnp.sum(parts, axis=0, keepdims=True)
    out, coarse = call(
        end_kernel, [(FIELD, F32), ((1, 512), F32)], (u, d, total), hbm_out={0}
    )
    return out.reshape(3, 512, 128), coarse[0, :408].reshape(3, 136)


def solution(mesh):
    return jax.shard_map(
        shards,
        mesh=mesh,
        in_specs=(P(None, None, BOTH), P(BOTH, None), P(None, BOTH), P("wide"), P(), P(), P(), P()),
        out_specs=(P(None, None, BOTH), P(None, BOTH)),
        check_vma=False,
    )
```

```python
from functools import partial

import jax
import jax.numpy as jnp
import ml_dtypes
import numpy as np
from jax import lax
from jax.experimental import pallas as pl
from jax.experimental.pallas import tpu as pltpu
from jax.sharding import PartitionSpec as P

RADIAL = 16
SIGMA = 4.0
VISCOSITY = 0.05
F32 = jnp.float32
BF16 = jnp.bfloat16
EXACT = lax.Precision.HIGHEST
BOTH = ("wide", "narrow")


def node_tables():
    x = np.array(
        [-1.0, -0.8717401485096066, -0.5917001814331423, -0.2092992179024789]
    )
    x = np.concatenate([x, -x[::-1]])
    w = np.array([1.0 / 28.0, 0.2107042271435061, 0.3411226924835044, 0.4124587946587038])
    w = np.concatenate([w, w[::-1]])
    scale = np.array([np.prod([x[t] - x[p] for p in range(8) if p != t]) for t in range(8)])
    deriv = np.zeros((8, 8))
    for t in range(8):
        for s in range(8):
            if t != s:
                deriv[t, s] = scale[t] / (scale[s] * (x[t] - x[s]))
        deriv[t, t] = -np.sum(deriv[t])
    y = np.array(
        [
            -0.9815606342467192,
            -0.9041172563704749,
            -0.7699026741943047,
            -0.5873179542866175,
            -0.3678314989981802,
            -0.1252334085114689,
        ]
    )
    y = np.concatenate([y, -y[::-1]])
    v = np.array(
        [
            0.0471753363865118,
            0.1069393259953184,
            0.1600783285433462,
            0.2031674267230659,
            0.2334925365383548,
            0.2491470458134028,
        ]
    )
    v = np.concatenate([v, v[::-1]])
    interp = np.ones((12, 8))
    for s in range(8):
        for p in range(8):
            if p != s:
                interp[:, s] = interp[:, s] * (y - x[p]) / (x[s] - x[p])
    linear = np.stack([(1.0 - x) / 2.0, (1.0 + x) / 2.0])
    return w, deriv, v, interp, linear


W, D, VF, J, LIN = node_tables()
B = J @ D
JV = J.T * VF[None, :]
STIFF = D.T @ (W[:, None] * D)
WJK = np.kron(W, W)


WJK_ROWS = np.broadcast_to(WJK[:, None], (64, 128)).astype(np.float32)


def two_parts(matrix):
    hi = matrix.astype(np.float32).astype(ml_dtypes.bfloat16)
    lo = (matrix - hi.astype(np.float64)).astype(ml_dtypes.bfloat16)
    return hi, lo


def four_terms(matrix):
    hi, lo = two_parts(matrix)
    return np.concatenate([hi, lo, hi, lo], axis=1)


def three_terms(matrix):
    hi, lo = two_parts(matrix)
    return np.concatenate([hi, lo, hi], axis=1)


FINE = four_terms(np.concatenate([np.kron(J, J), np.kron(B, J), np.kron(J, B)]))
BACK = three_terms(np.kron(JV, JV))
STIFF_JK = four_terms(
    np.concatenate([np.kron(STIFF, np.diag(W)), np.kron(np.diag(W), STIFF)])
)
COARSE_Z = LIN @ JV
COARSE_JK = three_terms(
    np.concatenate(
        [
            np.kron(COARSE_Z, COARSE_Z),
            np.kron(COARSE_Z, np.stack([JV[0], JV[7]])),
            np.zeros((8, 144)),
        ]
    )
)
GRAD_JK = four_terms(np.concatenate([np.kron(D, np.eye(8)), np.kron(np.eye(8), D)]))


def call(kernel, outs, args, scratch=(), spaces=None, hbm_out=(), free=False):
    spaces = spaces or {}
    args = [
        a if free and i not in spaces
        else pltpu.with_memory_space_constraint(a, spaces.get(i, pltpu.VMEM))
        for i, a in enumerate(args)
    ]
    return pl.pallas_call(
        kernel,
        out_shape=[
            (pltpu.HBM if i in hbm_out else pltpu.VMEM)(s, d)
            for i, (s, d) in enumerate(outs)
        ],
        in_specs=[
            pl.BlockSpec(memory_space=spaces.get(i, pltpu.VMEM)) for i in range(len(args))
        ],
        out_specs=[
            pl.BlockSpec(memory_space=pltpu.HBM if i in hbm_out else pltpu.VMEM)
            for i in range(len(outs))
        ],
        scratch_shapes=list(scratch),
        compiler_params=pltpu.CompilerParams(vmem_limit_bytes=32 << 20),
        name=kernel.func.__name__ if isinstance(kernel, partial) else kernel.__name__,
    )(*args)


def iota(shape, dim):
    return lax.broadcasted_iota(jnp.int32, shape, dim)


def lanes_by(x, shift):
    return pltpu.roll(x, shift % x.shape[-1], x.ndim - 1)


def rows_by(x, shift):
    return pltpu.roll(x, shift % 8, x.ndim - 2)


def split(x):
    hi = x.astype(BF16)
    return hi, (x - hi.astype(F32)).astype(BF16)


def dot(a, b):
    return jnp.dot(a, b, preferred_element_type=F32)


def even_odd(matrix, xs, sign):
    n_out, n_in = matrix.shape
    half = n_in // 2
    even = [xs[i] + xs[n_in - 1 - i] for i in range(half)]
    odd = [xs[i] - xs[n_in - 1 - i] for i in range(half)]
    outs = [None] * n_out
    for a in range(n_out // 2):
        e = sum(
            float((matrix[a, i] + matrix[a, n_in - 1 - i]) / 2) * even[i] for i in range(half)
        )
        o = sum(
            float((matrix[a, i] - matrix[a, n_in - 1 - i]) / 2) * odd[i] for i in range(half)
        )
        outs[a] = e + o
        outs[n_out - 1 - a] = e - o if sign > 0 else o - e
    return outs


def keep_rows(rows):
    k = iota((rows, 128), 0) & 7
    r = iota((rows, 128), 1) & (RADIAL - 1)
    wall = ((k == 0) & (r == 0)) | ((k == 7) & (r == RADIAL - 1))
    return jnp.where(wall, 0.0, 1.0).astype(F32)


def radial_parts(x):
    r = iota((8, 128), 1) & (RADIAL - 1)
    below = jnp.where(r > 0, lanes_by(x, 1), 0.0)
    above = jnp.where(r < RADIAL - 1, lanes_by(x, -1), 0.0)
    return below, above


def radial_sum(x, below, above):
    k = iota((8, 128), 0)
    return x + jnp.where(k == 0, rows_by(below, 1), jnp.where(k == 7, rows_by(above, -1), 0.0))


def pack_low(plane_of):
    et = iota((8, 128), 1) >> 4
    out = jnp.zeros((8, 128), F32)
    for i in range(8):
        out = jnp.where(et == i, lanes_by(plane_of(i), 16 * i), out)
    return out


def pack_high(plane_of):
    et = iota((8, 128), 1) >> 4
    out = jnp.zeros((8, 128), F32)
    for i in range(8):
        out = jnp.where(et == i, lanes_by(plane_of(i), 16 * i + 16), out)
    return out


def from_low(plane, packed, i):
    lane = iota((8, 128), 1)
    return jnp.where(lane < 16, lanes_by(packed, -16 * i), lanes_by(plane, 16))


def from_high(plane, packed, i):
    lane = iota((8, 128), 1)
    return jnp.where(lane >= 112, lanes_by(packed, 112 - 16 * i), lanes_by(plane, -16))


CONSTANTS = (FINE, BACK, STIFF_JK, GRAD_JK, COARSE_JK, WJK_ROWS)


def start_kernel(vel_hbm, slot_hbm, arc, rad, axial, *refs):
    n = len(CONSTANTS)
    hbm, mv, low, high, lanes = refs[:n], *refs[n : n + 4]
    held, (vel, slot, sems) = refs[n + 4 : 2 * n + 4], refs[2 * n + 4 :]
    pairs = [(slot_hbm, slot)] + [(vel_hbm.at[c], vel.at[c]) for c in range(3)]
    pairs += list(zip(hbm, held))
    copies = [pltpu.make_async_copy(a, b, sems.at[i]) for i, (a, b) in enumerate(pairs)]
    for copy in copies:
        copy.start()
    r = iota((1, 256), 1) & (RADIAL - 1)
    ht, hr = jnp.zeros((1, 256), F32), jnp.zeros((1, 256), F32)
    for i in range(RADIAL):
        ht = jnp.where(r == i, arc[i], ht)
        hr = jnp.where(r == i, rad[i], hr)
    hz = jnp.zeros((1, 256), F32) + axial[0]
    g = ht * hr / 8.0
    vol = hz * g
    g_low = g + jnp.where(r > 0, lanes_by(g, 1), 0.0)
    g_high = g + jnp.where(r < RADIAL - 1, lanes_by(g, -1), 0.0)
    rows = [
        vol,
        vol * (2.0 / hz),
        vol * (2.0 / ht),
        vol * (2.0 / hr),
        VISCOSITY * vol * (2.0 / hz) * (2.0 / hz),
        VISCOSITY * vol * (2.0 / ht) * (2.0 / ht),
        VISCOSITY * vol * (2.0 / hr) * (2.0 / hr),
        hz,
        1.0 / g,
        1.0 / g_low,
        1.0 / g_high,
    ]
    for n, row in enumerate(rows):
        lanes[n : n + 1] = row
    for n in range(len(rows), 16):
        lanes[n : n + 1] = jnp.zeros((1, 256), F32)
    copies[0].wait()
    hot = (slot[...] == iota((128, 128), 0)).astype(F32)
    nt = (((1,), (1,)), ((), ()))
    for c in range(3):
        copies[1 + c].wait()
        x = vel[c].reshape(512, 128)
        y = lax.dot_general(x, hot, nt, precision=EXACT, preferred_element_type=F32)
        mv[c] = (y * vol[:, :128]).reshape(8, 64, 128)
        low[c] = pack_low(lambda i: mv[c, i, 0:8])
        high[c] = pack_high(lambda i: mv[c, i, 56:64])
    for copy in copies[4:]:
        copy.wait()


def solve_tables_kernel(vectors, values, lanes, forward, inverse, scale):
    s = vectors[...]
    ident = (iota((10, 10), 0) == iota((10, 10), 1)).astype(F32)
    st = lax.dot_general(
        ident, s, (((1,), (1,)), ((), ())), precision=EXACT, preferred_element_type=F32
    )

    def mul(a, b):
        return jnp.dot(a, b, precision=EXACT, preferred_element_type=F32)

    row, col = iota((112, 10), 0), iota((112, 10), 1)
    live = row < 100
    by_b = ((row // 10 == col) & live).astype(F32)
    by_c = ((row % 10 == col) & live).astype(F32)
    node, pos = iota((10, 160), 0), iota((10, 160), 1)
    slot = pos & 15
    k_of = jnp.where(slot < 8, slot + 1, jnp.where(slot == 8, 0, jnp.where(slot == 9, 9, -1)))
    by_j = (node == (pos >> 4)).astype(F32)
    by_k = (node == k_of).astype(F32)
    full = mul(mul(by_b, st), by_j) * mul(mul(by_c, st), by_k)
    hi, lo = split(full)
    forward[:, 0:160] = hi
    forward[:, 160:320] = lo
    forward[:, 320:480] = hi

    row8, col8 = iota((64, 10), 0), iota((64, 10), 1)
    by_j8 = ((row8 >> 3) + 1 == col8).astype(F32)
    by_k8 = ((row8 & 7) + 1 == col8).astype(F32)
    node2, pos2 = iota((10, 112), 0), iota((10, 112), 1)
    b_of = jnp.where(pos2 < 100, pos2 // 10, -1)
    c_of = jnp.where(pos2 < 100, pos2 % 10, -1)
    to_b = (node2 == b_of).astype(F32)
    to_c = (node2 == c_of).astype(F32)
    full = mul(mul(by_j8, s), to_b) * mul(mul(by_k8, s), to_c)
    hi, lo = split(full)
    inverse[:, 0:112] = hi
    inverse[:, 112:224] = lo
    inverse[:, 224:336] = hi

    lam = jnp.broadcast_to(values[...], (8, 10))
    nt = (((1,), (1,)), ((), ()))
    lam_b = lax.dot_general(by_b, lam, nt, precision=EXACT, preferred_element_type=F32)[:, 0:1]
    lam_c = lax.dot_general(by_c, lam, nt, precision=EXACT, preferred_element_type=F32)[:, 0:1]
    vol = lanes[0:1, :128]
    flat = (
        SIGMA * vol
        + lam_b * jnp.broadcast_to(lanes[5:6, :128], (112, 128))
        + lam_c * jnp.broadcast_to(lanes[6:7, :128], (112, 128))
    )
    for a in range(10):
        scale[a] = 1.0 / (flat + values[0:1, a : a + 1] * lanes[4:5, :128])


def around_sum_kernel(field, tlo, thi, lanes, out, down, up):
    def body(c, carry):
        lo, hi = tlo[c], thi[c]
        for i in range(8):
            x = field[c, i]
            first, last = x[0:8], x[56:64]
            head = first + from_low(last, lo, i)
            tail = last + from_high(first, hi, i)
            out[c, i] = x
            out[c, i, 0:8] = head
            out[c, i, 56:64] = tail
        base = pl.multiple_of(c * 64, 64)
        down[pl.ds(base, 64)] = out[c, 0]
        up[pl.ds(base, 64)] = out[c, 7]
        return carry

    lax.fori_loop(0, 3, body, 0)
    hz = jnp.broadcast_to(lanes[7:8, :128], (8, 128))
    down[192:200] = hz
    up[192:200] = hz


def finish_sum(field, zlo, zhi, out, factor):
    def body(c, carry):
        base = pl.multiple_of(c * 64, 64)
        for i in range(8):
            x = field[c, i]
            if i == 0:
                x = x + zlo[pl.ds(base, 64)]
            if i == 7:
                x = x + zhi[pl.ds(base, 64)]
            for j in range(8):
                v = x[8 * j : 8 * j + 8]
                below, above = radial_parts(v)
                out[c, i, 8 * j : 8 * j + 8] = radial_sum(v, below, above) * factor(i, j)
        return carry

    lax.fori_loop(0, 3, body, 0)


def put(ref, at, rb, half, x):
    hi, lo = split(x)
    for term, part in enumerate((hi, hi, lo, lo)):
        rows = pl.ds(pl.multiple_of(term * 64 + rb * 16, 16), 16)
        ref[at, rows, half * 128 : half * 128 + 128] = part


def along_pipe(u, xu, xw, xs=None, sz=None):
    def body(t, carry):
        c, rb = t // 4, t % 4
        rows = pl.ds(pl.multiple_of(rb * 16, 16), 16)
        x = [u[c, i, rows] for i in range(8)]
        for a, val in enumerate(even_odd(J, x, 1)):
            put(xu, c * 6 + a // 2, rb, a % 2, val)
        for a, val in enumerate(even_odd(B, x, -1)):
            put(xw, c * 6 + a // 2, rb, a % 2, val)
        if xs is None:
            return carry
        for i in range(8):
            put(xs, c * 4 + i // 2, rb, i % 2, x[i])
        for i, val in enumerate(even_odd(STIFF, x, 1)):
            sz[c, i, rows] = val
        return carry

    lax.fori_loop(0, 12, body, 0)


def fine_dots(p, at, fine, xu, xw, pf, qf):
    for c in range(3):
        pf[at, c] = dot(fine[...], xu[c * 6 + p])
        qf[at, c] = dot(fine[0:144], xw[c * 6 + p])


def stiff_dots(p, stiff, xs, ks):
    for t in (2 * p, 2 * p + 1):
        y = dot(stiff[...], xs[t])
        c, q = t // 4, t % 4
        ks[c, 2 * q] = y[:, :128]
        ks[c, 2 * q + 1] = y[:, 128:]


def put_conv(xc, c, r, conv):
    hi, lo = split(conv)
    xc[c, 16 * r : 16 * r + 16] = hi
    xc[c, 144 + 16 * r : 160 + 16 * r] = hi
    xc[c, 288 + 16 * r : 304 + 16 * r] = lo


def back_dots(p, back, xc, yf, count):
    for c in range(count):
        y = dot(back[...], xc[c])
        yf[c, 2 * p] = y[:, :128]
        yf[c, 2 * p + 1] = y[:, 128:]


def fine_rows(pf, qf, p, c, r):
    rows = slice(16 * r, 16 * r + 16)
    return (
        qf[p, c, rows],
        pf[p, c, 144 + 16 * r : 160 + 16 * r],
        pf[p, c, 288 + 16 * r : 304 + 16 * r],
    )


def velocity_rows(pf, lanes, p, r):
    rows = slice(16 * r, 16 * r + 16)
    return [pf[p, n, rows] * lanes[n + 1 : n + 2] for n in range(3)]


def stiff_plane(lanes, wjk, sz, ks, c, i, rb):
    rows = pl.ds(pl.multiple_of(rb * 16, 16), 16)
    more = pl.ds(pl.multiple_of(64 + rb * 16, 16), 16)
    kz, kt, kr = lanes[4:5, :128], lanes[5:6, :128], lanes[6:7, :128]
    plane = kt * ks[c, i, rows] + kr * ks[c, i, more]
    return wjk[rows] * kz * sz[c, i, rows] + float(W[i]) * plane


def residual(u, lanes, fine, back, stiff, wjk, res, pf, qf, xu, xw, xs, xc0, xc1, yf, sz, ks):
    along_pipe(u, xu, xw, xs, sz)
    fine_dots(0, 0, fine, xu, xw, pf, qf)
    for p in range(6):
        if p < 5:
            fine_dots(p + 1, (p + 1) % 2, fine, xu, xw, pf, qf)
        stiff_dots(p, stiff, xs, ks)
        xc = (xc0, xc1)[p % 2]
        for r in range(9):
            v = velocity_rows(pf, lanes, p % 2, r)
            for c in range(3):
                g = fine_rows(pf, qf, p % 2, c, r)
                put_conv(xc, c, r, v[0] * g[0] + v[1] * g[1] + v[2] * g[2])
        back_dots(p, back, xc, yf, 3)
    keep = keep_rows(16)

    def body(t, carry):
        c, rb = t // 4, t % 4
        rows = pl.ds(pl.multiple_of(rb * 16, 16), 16)
        adv = even_odd(JV, [yf[c, a, rows] for a in range(12)], 1)
        for i in range(8):
            res[c, i, rows] = -(adv[i] + stiff_plane(lanes, wjk, sz, ks, c, i, rb)) * keep
        return carry

    lax.fori_loop(0, 12, body, 0)


def fields_kernel(u, fine, pf, qf, xu, xw):
    along_pipe(u, xu, xw)
    for p in range(6):
        fine_dots(p, p, fine, xu, xw, pf, qf)


def corner_weights():
    row, col = iota((8, 64), 0), iota((8, 64), 1)

    def weight(node, upper):
        acc = jnp.zeros((8, 64), F32)
        for n in range(8):
            acc = jnp.where(
                node == n, jnp.where(upper, float(LIN[1, n]), float(LIN[0, n])), acc
            )
        return acc

    return weight(col >> 3, (row & 2) != 0) * weight(col & 7, (row & 1) != 0)


def corners_kernel(res, out):
    weights = corner_weights()
    for c in range(3):
        planes = [res[c, i] for i in range(8)]
        z1 = sum(float(LIN[1, i]) * planes[i] for i in range(1, 8))
        z0 = sum(float(LIN[0, i]) * planes[i] for i in range(7))
        both = jnp.concatenate([z0, z1], axis=1)
        out[c] = jnp.dot(weights, both, precision=EXACT, preferred_element_type=F32)


def change_kernel(
    d, pf, qf, lanes, fine, stiff, wjk, coarse, out, pd, qd, xd, xe, xs, acc, xc, sz
):
    mean_w = LIN * W[None, :]
    mean_s = LIN @ STIFF

    def body(t, carry):
        c, rb = t // 4, t % 4
        rows = pl.ds(pl.multiple_of(rb * 16, 16), 16)
        x = [d[c, i, rows] for i in range(8)]
        for a, val in enumerate(even_odd(J, x, 1)):
            put(xd, c * 6 + a // 2, rb, a % 2, val)
        for a, val in enumerate(even_odd(B, x, -1)):
            put(xe, c * 6 + a // 2, rb, a % 2, val)
        for a in range(2):
            put(xs, c, rb, a, sum(float(mean_w[a, i]) * x[i] for i in range(8)))
            sz[c, a, rows] = sum(float(mean_s[a, i]) * x[i] for i in range(8))
        return carry

    lax.fori_loop(0, 12, body, 0)
    acc[...] = jnp.zeros_like(acc)

    def add_conv(n, p, r, conv):
        rows = slice(16 * r, 16 * r + 16)
        left, right = conv[:, :128], conv[:, 128:]
        for a in range(2):
            acc[n, rows, 128 * a : 128 * a + 128] += (
                float(COARSE_Z[a, 2 * p]) * left + float(COARSE_Z[a, 2 * p + 1]) * right
            )

    fine_dots(0, 0, fine, xd, xe, pd, qd)
    for p in range(6):
        if p < 5:
            fine_dots(p + 1, (p + 1) % 2, fine, xd, xe, pd, qd)
        for r in range(9):
            v = velocity_rows(pf, lanes, p, r)
            w = velocity_rows(pd, lanes, p % 2, r)
            for c in range(3):
                g = fine_rows(pf, qf, p, c, r)
                h = fine_rows(pd, qd, p % 2, c, r)
                one = (v[0] * h[0] + v[1] * h[1] + v[2] * h[2]) + (
                    w[0] * g[0] + w[1] * g[1] + w[2] * g[2]
                )
                add_conv(c, p, r, one)
                add_conv(3 + c, p, r, w[0] * h[0] + w[1] * h[1] + w[2] * h[2])
    r = iota((4, 256), 1) & (RADIAL - 1)
    upper = iota((4, 256), 0) & 1
    wall = ((upper == 0) & (r == 0)) | ((upper == 1) & (r == RADIAL - 1))
    wall = jnp.where(wall, 1.0, 0.0).astype(F32)
    keep = jnp.concatenate([keep_rows(64)] * 2, axis=1)
    wide = jnp.concatenate([wjk[...]] * 2, axis=1)
    kz, kt, kr = lanes[4:5], lanes[5:6], lanes[6:7]
    weights = corner_weights()
    for n in range(6):
        for q in range(9):
            put_conv(xc, n, q, acc[n, 16 * q : 16 * q + 16])
        y = dot(coarse[...], xc[n])
        total = y[0:4] - wall * y[4:8]
        if n < 3:
            ks = dot(stiff[...], xs[n])
            plane = jnp.concatenate([sz[n, 0], sz[n, 1]], axis=1) * wide * kz
            plane = (plane + kt * ks[0:64] + kr * ks[64:128]) * keep
            total = (
                total
                + jnp.dot(weights, plane, precision=EXACT, preferred_element_type=F32)[0:4]
            )
        out[n, 0:4] = -total
        out[n, 4:8] = jnp.zeros((4, 256), F32)


def pack_two(res, low, high):
    def body(c, carry):
        for n in range(2):
            low[c, 8 * n : 8 * n + 8] = pack_low(lambda i: res[c, i, 8 * n : 8 * n + 8])
            high[c, 8 * n : 8 * n + 8] = pack_high(
                lambda i: res[c, i, 48 + 8 * n : 56 + 8 * n]
            )
        return carry

    lax.fori_loop(0, 3, body, 0)


def project_kernel(
    field, zlo, zhi, lanes, fine, back, stiff, wjk, u, res, low, high, *scratch
):
    hz = lanes[7:8, :128]
    inner = 1.0 / hz
    first = 1.0 / (hz + zlo[192:193])
    last = 1.0 / (hz + zhi[192:193])
    k = iota((8, 128), 0)
    rk = jnp.where(
        k == 0, lanes[9:10, :128], jnp.where(k == 7, lanes[10:11, :128], lanes[8:9, :128])
    )
    rk = rk * keep_rows(8)
    by_plane = {0: rk * first, 7: rk * last}
    middle = rk * inner

    def factor(i, j):
        f = by_plane.get(i, middle)
        return 0.5 * f if j in (0, 7) else f

    finish_sum(field, zlo, zhi, u, factor)
    residual(u, lanes, fine, back, stiff, wjk, res, *scratch)
    pack_two(res, low, high)


def step_length(sums):
    total = jnp.sum(sums[...], axis=0, keepdims=True)
    return total[:, 0:1] / total[:, 1:2]


def advance_kernel(u_old, d, sums, lanes, fine, back, stiff, wjk, u, res, low, high, *scratch):
    alpha = step_length(sums)

    def body(t, carry):
        c, i = t // 8, t % 8
        u[c, i] = u_old[c, i] + alpha * d[c, i]
        return carry

    lax.fori_loop(0, 24, body, 0)
    residual(u, lanes, fine, back, stiff, wjk, res, *scratch)
    pack_two(res, low, high)


def around_widen_kernel(res, tlo, thi, out, down, up):
    lane = iota((8, 128), 1)

    def body(c, carry):
        lo6, lo7, hi0, hi1 = tlo[c, 0:8], tlo[c, 8:16], thi[c, 0:8], thi[c, 8:16]
        for i in range(8):
            x = res[c, i]
            first, last = x[0:8], x[56:64]
            out[c, i, 0:64] = x
            out[c, i, 0:8] = first + from_low(last, lo7, i)
            out[c, i, 56:64] = last + from_high(first, hi0, i)
            out[c, i, 64:72] = jnp.where(
                lane < 64, lanes_by(lo6, -16 * i), lanes_by(hi1, 112 - 16 * i)
            )
        for n in range(2):
            down[c, n] = out[c, n]
            up[c, n] = out[c, 6 + n]
        return carry

    lax.fori_loop(0, 3, body, 0)


def widen_planes(e, xf, half):
    lane, k = iota((8, 128), 1), iota((8, 128), 0)
    extra = e[64:72]
    planes = [e[8 * j : 8 * j + 8] for j in range(8)]
    under = jnp.where(lane < 16, extra, lanes_by(planes[6], 16))
    over = jnp.where(lane >= 112, extra, lanes_by(planes[1], -16))
    cols = slice(half * 128, half * 128 + 128)
    for j, v in enumerate([under] + planes + [over]):
        below, above = radial_parts(v)
        own = radial_sum(v, below, above)
        side = jnp.where(k == 0, rows_by(below, 2), jnp.where(k == 1, above, 0.0))
        hi, lo = split(jnp.concatenate([own, side], axis=0))
        xf[16 * j : 16 * j + 16, cols] = hi
        xf[160 + 16 * j : 176 + 16 * j, cols] = hi
        xf[320 + 16 * j : 336 + 16 * j, cols] = lo


def transform_kernel(field, forward, vectors, out, xf0, xf1, yf):
    def body(c, carry):
        for p in range(4):
            buf = (xf0, xf1)[p % 2]
            for half in range(2):
                widen_planes(field[c, 2 * p + half], buf, half)
            y = dot(forward[...], buf[...])
            yf[c, 2 * p] = y[:, :128]
            yf[c, 2 * p + 1] = y[:, 128:]
        return carry

    lax.fori_loop(0, 3, body, 0)

    def mid(rb, carry):
        rows = pl.ds(pl.multiple_of(rb * 16, 16), 16)
        y = [[yf[c, i, rows] for i in range(8)] for c in range(3)]
        for a in range(10):
            acc = [vectors[1, a] * y[c][0] for c in range(3)]
            for i in range(1, 8):
                s = vectors[i + 1, a]
                acc = [acc[c] + s * y[c][i] for c in range(3)]
            for c in range(3):
                out[c, a, rows] = acc[c]
        return carry

    lax.fori_loop(0, 7, mid, 0)


def solve_kernel(
    own, zlo, zhi, vectors, forward, inverse, scale, corr, low, high, xf0, xf1, yf, xb
):
    def body(c, carry):
        for buf, halo in ((xf0, zlo), (xf1, zhi)):
            widen_planes(halo[c, 0], buf, 0)
            widen_planes(halo[c, 1], buf, 1)
        y0, y1 = dot(forward[...], xf0[...]), dot(forward[...], xf1[...])
        yf[c, 0] = y0[:, :128]
        yf[c, 1] = y0[:, 128:]
        yf[c, 2] = y1[:, :128]
        yf[c, 3] = y1[:, 128:]
        return carry

    lax.fori_loop(0, 3, body, 0)

    def mid(rb, carry):
        rows = pl.ds(pl.multiple_of(rb * 16, 16), 16)
        y = [[yf[c, i, rows] for i in range(4)] for c in range(3)]
        spec = []
        for a in range(10):
            acc = [own[c, a, rows] for c in range(3)]
            for n, i in enumerate((0, 1, 8, 9)):
                s = vectors[i, a]
                acc = [acc[c] + s * y[c][n] for c in range(3)]
            f = scale[a, rows]
            spec.append([acc[c] * f for c in range(3)])
        for i in range(8):
            acc = [vectors[i + 1, 0] * spec[0][c] for c in range(3)]
            for a in range(1, 10):
                s = vectors[i + 1, a]
                acc = [acc[c] + s * spec[a][c] for c in range(3)]
            cols = slice((i % 2) * 128, (i % 2) * 128 + 128)
            for c in range(3):
                hi, lo = split(acc[c])
                for term, part in enumerate((hi, hi, lo)):
                    xb[c * 4 + i // 2, pl.ds(pl.multiple_of(term * 112 + rb * 16, 16), 16),
                       cols] = part
        return carry

    lax.fori_loop(0, 7, mid, 0)

    k = iota((8, 128), 0)
    r = iota((8, 128), 1) & (RADIAL - 1)
    inner = ((k == 0) & (r > 0)) | ((k == 7) & (r < RADIAL - 1))
    share = jnp.where(inner, 0.5, 1.0).astype(F32)
    for t in range(12):
        c, p = t // 4, t % 4
        y = dot(inverse[...], xb[t])
        for half in range(2):
            i = 2 * p + half
            for j in range(8):
                f = (0.5 if i in (0, 7) else 1.0) * (0.5 if j in (0, 7) else 1.0)
                corr[c, i, 8 * j : 8 * j + 8] = (
                    y[8 * j : 8 * j + 8, half * 128 : half * 128 + 128] * (share * f)
                )

    def last(c, carry):
        low[c] = pack_low(lambda i: corr[c, i, 0:8])
        high[c] = pack_high(lambda i: corr[c, i, 56:64])
        return carry

    lax.fori_loop(0, 3, last, 0)


def direction_kernel(field, zlo, zhi, res, lanes, grad, wjk, d, sums, xs, acc):
    keep = keep_rows(8)
    finish_sum(field, zlo, zhi, d, lambda i, j: keep)
    acc[...] = jnp.zeros_like(acc)
    vol = lanes[0:1, :128]
    kz, kt, kr = lanes[4:5, :128], lanes[5:6, :128], lanes[6:7, :128]

    def first(t, carry):
        c, rb = t // 4, t % 4
        rows = pl.ds(pl.multiple_of(rb * 16, 16), 16)
        x = [d[c, i, rows] for i in range(8)]
        num = sum(x[i] * res[c, i, rows] for i in range(8))
        sq = sum(float(W[i]) * (x[i] * x[i]) for i in range(8))
        gz = sum(float(W[i]) * (g * g) for i, g in enumerate(even_odd(D, x, -1)))
        acc[0] += num
        acc[1] += wjk[rows] * (SIGMA * vol * sq + kz * gz)
        for i in range(8):
            hi, lo = split(x[i])
            for term, part in enumerate((hi, hi, lo, lo)):
                xs[c * 4 + i // 2, pl.ds(pl.multiple_of(term * 64 + rb * 16, 16), 16),
                   (i % 2) * 128 : (i % 2) * 128 + 128] = part
        return carry

    lax.fori_loop(0, 12, first, 0)

    def second(c, carry):
        total = jnp.zeros((16, 128), F32)
        for p in range(4):
            y = dot(grad[...], xs[c * 4 + p])
            for half in range(2):
                v = y[:, half * 128 : half * 128 + 128]
                v = v * v
                plane = jnp.zeros((16, 128), F32)
                for q in range(4):
                    rows = slice(16 * q, 16 * q + 16)
                    plane = plane + wjk[rows] * (
                        kt * v[rows] + kr * v[64 + 16 * q : 80 + 16 * q]
                    )
                total = total + float(W[2 * p + half]) * plane
        acc[1] += total
        return carry

    lax.fori_loop(0, 3, second, 0)
    num = jnp.sum(jnp.sum(acc[0], axis=0, keepdims=True), axis=1, keepdims=True)
    den = jnp.sum(jnp.sum(acc[1], axis=0, keepdims=True), axis=1, keepdims=True)
    at = iota((128, 128), 1)
    sums[...] = jnp.where(at == 0, num, jnp.where(at == 1, den, 0.0))


def route_kernel(slot, corner, right, owner):
    hot = (slot[...] == iota((128, 128), 0)).astype(F32)
    nt = (((1,), (1,)), ((), ()))
    ids = corner[...].astype(F32)
    by_elem = lax.dot_general(hot, ids, nt, precision=EXACT, preferred_element_type=F32)
    by_corner = lax.dot_general(ids, hot, nt, precision=EXACT, preferred_element_type=F32)
    owner[...] = (by_corner + 0.5).astype(jnp.int32) // 136
    ids = (by_elem + 0.5).astype(jnp.int32)
    inside = ids - ids // 136 * 136
    pos = iota((128, 256), 1)
    for q in range(8):
        right[128 * q : 128 * q + 128] = (inside[:, q : q + 1] == pos).astype(F32).astype(BF16)


def place_kernel(base, change, right, owner, part, dense, left):
    dev = iota((128, 128), 0)
    spill = None
    for n in range(3):
        for c in range(3):
            both = base[c] if n == 0 else change[3 * (n - 1) + c]
            hi = both.astype(BF16).astype(F32)
            for q in range(8):
                mine = owner[q : q + 1] == dev
                cols = slice((q // 4) * 128, (q // 4) * 128 + 128)
                for m, piece in enumerate((hi, both - hi)):
                    at = (2 * c + m) * 128
                    left[n, at : at + 128, 128 * q : 128 * q + 128] = jnp.where(
                        mine, piece[q % 4 : q % 4 + 1, cols], 0.0
                    ).astype(BF16)
        y = dot(left[n], right[...])
        for c in range(3):
            block = 3 * n + c
            total = lanes_by(y[256 * c : 256 * c + 128] + y[256 * c + 128 : 256 * c + 256],
                             8 * block)
            first = total[:, :128]
            dense[:, 0, 128 * block : 128 * block + 128] = (
                first if spill is None else first + spill
            )
            spill = total[:, 128:]
    dense[:, 0, 1152:1280] = spill + lanes_by(part[...], 72)


def store_kernel(u, d, slot, u_hbm, d_hbm, u_out, d_out, sems):
    hot = (slot[...] == iota((128, 128), 0)).astype(F32)
    copies = []
    for c in range(3):
        for n, (x, y, out) in enumerate(((u, u_out, u_hbm), (d, d_out, d_hbm))):
            flat = x[c].reshape(512, 128)
            y[c] = jnp.dot(flat, hot, precision=EXACT, preferred_element_type=F32).reshape(
                8, 64, 128
            )
            copies.append(pltpu.make_async_copy(y.at[c], out.at[c], sems.at[2 * c + n]))
            copies[-1].start()
    for copy in copies:
        copy.wait()


def end_kernel(u_hbm, d_hbm, parts_hbm, vel_hbm, coarse, u, d, parts, vel, sems):
    first = pltpu.make_async_copy(parts_hbm, parts, sems.at[0])
    loads = [
        [
            pltpu.make_async_copy(a.at[c], b.at[c], sems.at[1 + 2 * c + n])
            for n, (a, b) in enumerate(((u_hbm, u), (d_hbm, d)))
        ]
        for c in range(3)
    ]
    stores = [
        pltpu.make_async_copy(vel.at[c], vel_hbm.at[c], sems.at[7 + c]) for c in range(3)
    ]
    first.start()
    for pair in loads:
        for copy in pair:
            copy.start()
    first.wait()
    total = jnp.sum(parts[...], axis=0)
    alpha = total[:, 1224:1225] / total[:, 1225:1226]
    for c in range(3):
        for copy in loads[c]:
            copy.wait()
        vel[c] = u[c] + alpha * d[c]
        stores[c].start()
    one, two = lanes_by(total, -408), lanes_by(total, -816)
    both = total + alpha * (one + alpha * two)
    for c in range(3):
        coarse[c : c + 1] = lanes_by(both, -136 * c)[:, :136]
    for copy in stores:
        copy.wait()


FIELD = (3, 8, 64, 128)


def both_ways(axis, to_next, to_prev):
    n = lax.axis_size(axis)
    up = [(i, (i + 1) % n) for i in range(n)]
    down = [((i + 1) % n, i) for i in range(n)]
    return lax.ppermute(to_next, axis, up), lax.ppermute(to_prev, axis, down)


def fine_scratch():
    return [
        pltpu.VMEM((2, 3, 432, 256), F32),
        pltpu.VMEM((2, 3, 144, 256), F32),
        pltpu.VMEM((18, 256, 256), BF16),
        pltpu.VMEM((18, 256, 256), BF16),
    ]


def local_scratch(count):
    return [
        pltpu.VMEM((12, 256, 256), BF16),
        pltpu.VMEM((count, 432, 256), BF16),
        pltpu.VMEM((count, 432, 256), BF16),
        pltpu.VMEM((count, 12, 64, 128), F32),
        pltpu.VMEM(FIELD, F32),
        pltpu.VMEM((3, 8, 128, 128), F32),
    ]


def shards(vel, slot, corner, axial, arc, rad, vectors, values):
    smem = pltpu.SMEM
    small = ((3, 8, 128), F32)
    count = len(CONSTANTS)
    mv, low, high, lanes, fine, back, stiff, grad, coarse_jk, wjk = call(
        start_kernel,
        [(FIELD, F32), small, small, ((16, 256), F32)] + [(m.shape, m.dtype) for m in CONSTANTS],
        (vel.reshape(FIELD), slot, arc, rad, axial, *(jnp.asarray(m) for m in CONSTANTS)),
        [
            pltpu.VMEM(FIELD, F32),
            pltpu.VMEM((1, 128), jnp.int32),
            pltpu.SemaphoreType.DMA((4 + count,)),
        ],
        spaces={
            0: pltpu.HBM, 1: pltpu.HBM, 2: smem, 3: smem, 4: smem,
            **{5 + i: pltpu.HBM for i in range(count)},
        },
    )
    forward, inverse, scale = call(
        solve_tables_kernel,
        [((112, 480), BF16), ((64, 336), BF16), ((10, 112, 128), F32)],
        (vectors, values[None], lanes),
    )

    def sum_rounds(field, low, high, beside=()):
        tlo, thi = both_ways("narrow", high, low)
        out, down, up = call(
            around_sum_kernel,
            [(FIELD, F32), ((200, 128), F32), ((200, 128), F32)],
            (field, tlo, thi, lanes),
        )
        zlo, zhi = both_ways("wide", up, down)
        zlo, zhi, beside = lax.optimization_barrier((zlo, zhi, beside))
        return (out, zlo, zhi), beside

    local = (lanes, fine, back, stiff, wjk)
    packs = [(FIELD, F32), (FIELD, F32), ((3, 16, 128), F32), ((3, 16, 128), F32)]
    u, res, low, high = call(
        project_kernel,
        packs,
        (*sum_rounds(mv, low, high)[0], *local),
        fine_scratch() + local_scratch(3),
    )
    for step in range(2):
        if step > 0:
            sums = lax.all_to_all(part, BOTH, 0, 0, tiled=True)
            u, res, low, high = call(
                advance_kernel, packs, (u, d, sums, *local), fine_scratch() + local_scratch(3)
            )
        tlo, thi = both_ways("narrow", high, low)
        wide_field, down, up = call(
            around_widen_kernel,
            [((3, 8, 72, 128), F32), ((3, 2, 72, 128), F32), ((3, 2, 72, 128), F32)],
            (res, tlo, thi),
        )
        zlo, zhi = both_ways("wide", up, down)
        (own,) = call(
            transform_kernel,
            [((3, 10, 112, 128), F32)],
            (wide_field, forward, vectors),
            [
                pltpu.VMEM((480, 256), BF16),
                pltpu.VMEM((480, 256), BF16),
                pltpu.VMEM((3, 8, 112, 128), F32),
            ],
            spaces={2: smem},
        )
        zlo, zhi, own = lax.optimization_barrier((zlo, zhi, own))
        corr, low, high = call(
            solve_kernel,
            [(FIELD, F32), small, small],
            (own, zlo, zhi, vectors, forward, inverse, scale),
            [
                pltpu.VMEM((480, 256), BF16),
                pltpu.VMEM((480, 256), BF16),
                pltpu.VMEM((3, 4, 112, 128), F32),
                pltpu.VMEM((12, 336, 256), BF16),
            ],
            spaces={3: smem},
        )
        beside = ()
        if step == 1:
            fields = [((6, 3, 432, 256), F32), ((6, 3, 144, 256), F32)]
            beside = (
                call(fields_kernel, fields, (u, fine), fine_scratch()[2:]),
                call(corners_kernel, [((3, 8, 256), F32)], (res,)),
                call(
                    route_kernel,
                    [((1024, 256), BF16), ((8, 128), jnp.int32)],
                    (slot, corner),
                    free=True,
                ),
            )
        halo, beside = sum_rounds(corr, low, high, beside)
        d, part = call(
            direction_kernel,
            [(FIELD, F32), ((128, 128), F32)],
            (*halo, res, lanes, grad, wjk),
            [pltpu.VMEM((12, 256, 256), BF16), pltpu.VMEM((2, 16, 128), F32)],
        )
    (pf, qf), (base,), (right, owner) = beside
    (change,) = call(
        change_kernel,
        [((6, 8, 256), F32)],
        (d, pf, qf, lanes, fine, stiff, wjk, coarse_jk),
        fine_scratch()
        + [
            pltpu.VMEM((3, 256, 256), BF16),
            pltpu.VMEM((6, 144, 256), F32),
            pltpu.VMEM((6, 432, 256), BF16),
            pltpu.VMEM((3, 2, 64, 128), F32),
        ],
    )
    (dense,) = call(
        place_kernel,
        [((128, 1, 1280), F32)],
        (base, change, right, owner, part),
        [pltpu.VMEM((3, 768, 1024), BF16)],
    )
    parts = lax.all_to_all(dense, BOTH, 0, 0, tiled=True)
    u, d = call(
        store_kernel,
        [(FIELD, F32), (FIELD, F32)],
        (u, d, slot),
        [pltpu.VMEM(FIELD, F32), pltpu.VMEM(FIELD, F32), pltpu.SemaphoreType.DMA((6,))],
        hbm_out={0, 1},
        free=True,
    )
    out, coarse = call(
        end_kernel,
        [(FIELD, F32), ((3, 136), F32)],
        (u, d, parts),
        [
            pltpu.VMEM(FIELD, F32),
            pltpu.VMEM(FIELD, F32),
            pltpu.VMEM((128, 1, 1280), F32),
            pltpu.VMEM(FIELD, F32),
            pltpu.SemaphoreType.DMA((10,)),
        ],
        spaces={0: pltpu.HBM, 1: pltpu.HBM, 2: pltpu.HBM},
        hbm_out={0},
    )
    return out.reshape(3, 512, 128), coarse


def solution(mesh):
    return jax.shard_map(
        shards,
        mesh=mesh,
        in_specs=(P(None, None, BOTH), P(BOTH, None), P(None, BOTH), P("wide"), P(), P(), P(), P()),
        out_specs=(P(None, None, BOTH), P(None, BOTH)),
        check_vma=False,
    )
```

```python
from functools import partial

import jax
import jax.numpy as jnp
import ml_dtypes
import numpy as np
from jax import lax
from jax.experimental import pallas as pl
from jax.experimental.pallas import tpu as pltpu
from jax.sharding import PartitionSpec as P

RADIAL = 16
SIGMA = 4.0
VISCOSITY = 0.05
F32 = jnp.float32
BF16 = jnp.bfloat16
EXACT = lax.Precision.HIGHEST
BOTH = ("wide", "narrow")


def node_tables():
    x = np.array(
        [-1.0, -0.8717401485096066, -0.5917001814331423, -0.2092992179024789]
    )
    x = np.concatenate([x, -x[::-1]])
    w = np.array([1.0 / 28.0, 0.2107042271435061, 0.3411226924835044, 0.4124587946587038])
    w = np.concatenate([w, w[::-1]])
    scale = np.array([np.prod([x[t] - x[p] for p in range(8) if p != t]) for t in range(8)])
    deriv = np.zeros((8, 8))
    for t in range(8):
        for s in range(8):
            if t != s:
                deriv[t, s] = scale[t] / (scale[s] * (x[t] - x[s]))
        deriv[t, t] = -np.sum(deriv[t])
    y = np.array(
        [
            -0.9815606342467192,
            -0.9041172563704749,
            -0.7699026741943047,
            -0.5873179542866175,
            -0.3678314989981802,
            -0.1252334085114689,
        ]
    )
    y = np.concatenate([y, -y[::-1]])
    v = np.array(
        [
            0.0471753363865118,
            0.1069393259953184,
            0.1600783285433462,
            0.2031674267230659,
            0.2334925365383548,
            0.2491470458134028,
        ]
    )
    v = np.concatenate([v, v[::-1]])
    interp = np.ones((12, 8))
    for s in range(8):
        for p in range(8):
            if p != s:
                interp[:, s] = interp[:, s] * (y - x[p]) / (x[s] - x[p])
    linear = np.stack([(1.0 - x) / 2.0, (1.0 + x) / 2.0])
    return w, deriv, v, interp, linear


W, D, VF, J, LIN = node_tables()
B = J @ D
JV = J.T * VF[None, :]
STIFF = D.T @ (W[:, None] * D)
WJK = np.kron(W, W)


WJK_ROWS = np.broadcast_to(WJK[:, None], (64, 128)).astype(np.float32)


def two_parts(matrix):
    hi = matrix.astype(np.float32).astype(ml_dtypes.bfloat16)
    lo = (matrix - hi.astype(np.float64)).astype(ml_dtypes.bfloat16)
    return hi, lo


def four_terms(matrix):
    hi, lo = two_parts(matrix)
    return np.concatenate([hi, lo, hi, lo], axis=1)


def three_terms(matrix):
    hi, lo = two_parts(matrix)
    return np.concatenate([hi, lo, hi], axis=1)


FINE = four_terms(np.concatenate([np.kron(J, J), np.kron(B, J), np.kron(J, B)]))
BACK = three_terms(np.kron(JV, JV))
STIFF_JK = four_terms(
    np.concatenate([np.kron(STIFF, np.diag(W)), np.kron(np.diag(W), STIFF)])
)
COARSE_Z = LIN @ JV
COARSE_JK = three_terms(
    np.concatenate(
        [
            np.kron(COARSE_Z, COARSE_Z),
            np.kron(COARSE_Z, np.stack([JV[0], JV[7]])),
            np.zeros((8, 144)),
        ]
    )
)
GRAD_JK = four_terms(np.concatenate([np.kron(D, np.eye(8)), np.kron(np.eye(8), D)]))


def call(kernel, outs, args, scratch=(), spaces=None, hbm_out=(), free=False):
    spaces = spaces or {}
    args = [
        a if free and i not in spaces
        else pltpu.with_memory_space_constraint(a, spaces.get(i, pltpu.VMEM))
        for i, a in enumerate(args)
    ]
    return pl.pallas_call(
        kernel,
        out_shape=[
            (pltpu.HBM if i in hbm_out else pltpu.VMEM)(s, d)
            for i, (s, d) in enumerate(outs)
        ],
        in_specs=[
            pl.BlockSpec(memory_space=spaces.get(i, pltpu.VMEM)) for i in range(len(args))
        ],
        out_specs=[
            pl.BlockSpec(memory_space=pltpu.HBM if i in hbm_out else pltpu.VMEM)
            for i in range(len(outs))
        ],
        scratch_shapes=list(scratch),
        compiler_params=pltpu.CompilerParams(vmem_limit_bytes=32 << 20),
        name=kernel.func.__name__ if isinstance(kernel, partial) else kernel.__name__,
    )(*args)


def iota(shape, dim):
    return lax.broadcasted_iota(jnp.int32, shape, dim)


def lanes_by(x, shift):
    return pltpu.roll(x, shift % x.shape[-1], x.ndim - 1)


def rows_by(x, shift):
    return pltpu.roll(x, shift % 8, x.ndim - 2)


def split(x):
    hi = x.astype(BF16)
    return hi, (x - hi.astype(F32)).astype(BF16)


def dot(a, b):
    return jnp.dot(a, b, preferred_element_type=F32)


def even_odd(matrix, xs, sign):
    n_out, n_in = matrix.shape
    half = n_in // 2
    even = [xs[i] + xs[n_in - 1 - i] for i in range(half)]
    odd = [xs[i] - xs[n_in - 1 - i] for i in range(half)]
    outs = [None] * n_out
    for a in range(n_out // 2):
        e = sum(
            float((matrix[a, i] + matrix[a, n_in - 1 - i]) / 2) * even[i] for i in range(half)
        )
        o = sum(
            float((matrix[a, i] - matrix[a, n_in - 1 - i]) / 2) * odd[i] for i in range(half)
        )
        outs[a] = e + o
        outs[n_out - 1 - a] = e - o if sign > 0 else o - e
    return outs


def keep_rows(rows):
    k = iota((rows, 128), 0) & 7
    r = iota((rows, 128), 1) & (RADIAL - 1)
    wall = ((k == 0) & (r == 0)) | ((k == 7) & (r == RADIAL - 1))
    return jnp.where(wall, 0.0, 1.0).astype(F32)


def radial_parts(x):
    r = iota((8, 128), 1) & (RADIAL - 1)
    below = jnp.where(r > 0, lanes_by(x, 1), 0.0)
    above = jnp.where(r < RADIAL - 1, lanes_by(x, -1), 0.0)
    return below, above


def radial_sum(x, below, above):
    k = iota((8, 128), 0)
    return x + jnp.where(k == 0, rows_by(below, 1), jnp.where(k == 7, rows_by(above, -1), 0.0))


def pack_low(plane_of):
    et = iota((8, 128), 1) >> 4
    out = jnp.zeros((8, 128), F32)
    for i in range(8):
        out = jnp.where(et == i, lanes_by(plane_of(i), 16 * i), out)
    return out


def pack_high(plane_of):
    et = iota((8, 128), 1) >> 4
    out = jnp.zeros((8, 128), F32)
    for i in range(8):
        out = jnp.where(et == i, lanes_by(plane_of(i), 16 * i + 16), out)
    return out


def from_low(plane, packed, i):
    lane = iota((8, 128), 1)
    return jnp.where(lane < 16, lanes_by(packed, -16 * i), lanes_by(plane, 16))


def from_high(plane, packed, i):
    lane = iota((8, 128), 1)
    return jnp.where(lane >= 112, lanes_by(packed, 112 - 16 * i), lanes_by(plane, -16))


CONSTANTS = (FINE, BACK, STIFF_JK, GRAD_JK, COARSE_JK, WJK_ROWS)
NT = (((1,), (1,)), ((), ()))


def faces_kernel(
    vel_hbm, slot_hbm, arc_hbm, rad_hbm, axial, down, up, lanes, vel, slot, arc, rad, sems
):
    copies = [
        pltpu.make_async_copy(arc_hbm, arc, sems.at[7]),
        pltpu.make_async_copy(rad_hbm, rad, sems.at[8]),
        pltpu.make_async_copy(slot_hbm, slot, sems.at[6]),
    ]
    for c in range(3):
        for n in range(2):
            copies.append(
                pltpu.make_async_copy(vel_hbm.at[c, 7 * n], vel.at[n, c], sems.at[3 * n + c])
            )
    for copy in copies:
        copy.start()
    for copy in copies[:2]:
        copy.wait()
    r = iota((1, 256), 1) & (RADIAL - 1)
    ht, hr = jnp.zeros((1, 256), F32), jnp.zeros((1, 256), F32)
    for i in range(RADIAL):
        ht = jnp.where(r == i, arc[i], ht)
        hr = jnp.where(r == i, rad[i], hr)
    hz = jnp.zeros((1, 256), F32) + axial[0]
    g = ht * hr / 8.0
    vol = hz * g
    g_low = g + jnp.where(r > 0, lanes_by(g, 1), 0.0)
    g_high = g + jnp.where(r < RADIAL - 1, lanes_by(g, -1), 0.0)
    rows = [
        vol,
        vol * (2.0 / hz),
        vol * (2.0 / ht),
        vol * (2.0 / hr),
        VISCOSITY * vol * (2.0 / hz) * (2.0 / hz),
        VISCOSITY * vol * (2.0 / ht) * (2.0 / ht),
        VISCOSITY * vol * (2.0 / hr) * (2.0 / hr),
        hz,
        1.0 / g,
        1.0 / g_low,
        1.0 / g_high,
    ]
    for n, row in enumerate(rows):
        lanes[n : n + 1] = row
    for n in range(len(rows), 16):
        lanes[n : n + 1] = jnp.zeros((1, 256), F32)
    for copy in copies[2:]:
        copy.wait()
    hot = (slot[...] == iota((128, 128), 0)).astype(F32)
    y = lax.dot_general(
        vel[...].reshape(384, 128), hot, NT, precision=EXACT, preferred_element_type=F32
    )
    y = y * vol[:, :128]
    for n, out in enumerate((down, up)):
        out[0:192] = y[192 * n : 192 * n + 192]
        out[192:200] = jnp.broadcast_to(hz[:, :128], (8, 128))


def inner_kernel(vel_hbm, slot_hbm, lanes, *refs):
    n = len(CONSTANTS)
    hbm, mv, held, (vel, slot, sems) = refs[:n], refs[n], refs[n + 1 : 2 * n + 1], refs[2 * n + 1 :]
    pairs = [(slot_hbm, slot)]
    pairs += [(vel_hbm.at[c, pl.ds(1, 6)], vel.at[c]) for c in range(3)]
    pairs += list(zip(hbm, held))
    copies = [pltpu.make_async_copy(a, b, sems.at[i]) for i, (a, b) in enumerate(pairs)]
    for copy in copies:
        copy.start()
    copies[0].wait()
    hot = (slot[...] == iota((128, 128), 0)).astype(F32)
    for c in range(3):
        copies[1 + c].wait()
        y = lax.dot_general(
            vel[c].reshape(384, 128), hot, NT, precision=EXACT, preferred_element_type=F32
        )
        mv[c] = (y * lanes[0:1, :128]).reshape(6, 64, 128)
    for copy in copies[4:]:
        copy.wait()


def pipe_sum_kernel(mv, down, up, zlo, zhi, field, low, high):
    def body(c, carry):
        rows = pl.ds(pl.multiple_of(c * 64, 64), 64)
        field[c, 0] = down[rows] + zlo[rows]
        for i in range(6):
            field[c, 1 + i] = mv[c, i]
        field[c, 7] = up[rows] + zhi[rows]
        low[c] = pack_low(lambda i: field[c, i, 0:8])
        high[c] = pack_high(lambda i: field[c, i, 56:64])
        return carry

    lax.fori_loop(0, 3, body, 0)


def solve_tables_kernel(
    vectors_hbm, values_hbm, lanes, forward, inverse, scale, vectors, values, sems
):
    copies = [
        pltpu.make_async_copy(vectors_hbm, vectors, sems.at[0]),
        pltpu.make_async_copy(values_hbm, values, sems.at[1]),
    ]
    for copy in copies:
        copy.start()
    for copy in copies:
        copy.wait()
    s = vectors[...]
    ident = (iota((10, 10), 0) == iota((10, 10), 1)).astype(F32)
    st = lax.dot_general(
        ident, s, (((1,), (1,)), ((), ())), precision=EXACT, preferred_element_type=F32
    )

    def mul(a, b):
        return jnp.dot(a, b, precision=EXACT, preferred_element_type=F32)

    row, col = iota((112, 10), 0), iota((112, 10), 1)
    live = row < 100
    by_b = ((row // 10 == col) & live).astype(F32)
    by_c = ((row % 10 == col) & live).astype(F32)
    node, pos = iota((10, 160), 0), iota((10, 160), 1)
    slot = pos & 15
    k_of = jnp.where(slot < 8, slot + 1, jnp.where(slot == 8, 0, jnp.where(slot == 9, 9, -1)))
    by_j = (node == (pos >> 4)).astype(F32)
    by_k = (node == k_of).astype(F32)
    full = mul(mul(by_b, st), by_j) * mul(mul(by_c, st), by_k)
    hi, lo = split(full)
    forward[:, 0:160] = hi
    forward[:, 160:320] = lo
    forward[:, 320:480] = hi

    row8, col8 = iota((64, 10), 0), iota((64, 10), 1)
    by_j8 = ((row8 >> 3) + 1 == col8).astype(F32)
    by_k8 = ((row8 & 7) + 1 == col8).astype(F32)
    node2, pos2 = iota((10, 112), 0), iota((10, 112), 1)
    b_of = jnp.where(pos2 < 100, pos2 // 10, -1)
    c_of = jnp.where(pos2 < 100, pos2 % 10, -1)
    to_b = (node2 == b_of).astype(F32)
    to_c = (node2 == c_of).astype(F32)
    full = mul(mul(by_j8, s), to_b) * mul(mul(by_k8, s), to_c)
    hi, lo = split(full)
    inverse[:, 0:112] = hi
    inverse[:, 112:224] = lo
    inverse[:, 224:336] = hi

    lam = jnp.broadcast_to(values[...], (8, 10))
    nt = (((1,), (1,)), ((), ()))
    lam_b = lax.dot_general(by_b, lam, nt, precision=EXACT, preferred_element_type=F32)[:, 0:1]
    lam_c = lax.dot_general(by_c, lam, nt, precision=EXACT, preferred_element_type=F32)[:, 0:1]
    vol = lanes[0:1, :128]
    flat = (
        SIGMA * vol
        + lam_b * jnp.broadcast_to(lanes[5:6, :128], (112, 128))
        + lam_c * jnp.broadcast_to(lanes[6:7, :128], (112, 128))
    )
    for a in range(10):
        scale[a] = 1.0 / (flat + values[0:1, a : a + 1] * lanes[4:5, :128])


def around_sum_kernel(field, tlo, thi, lanes, out, down, up):
    def body(c, carry):
        lo, hi = tlo[c], thi[c]
        for i in range(8):
            x = field[c, i]
            first, last = x[0:8], x[56:64]
            head = first + from_low(last, lo, i)
            tail = last + from_high(first, hi, i)
            out[c, i] = x
            out[c, i, 0:8] = head
            out[c, i, 56:64] = tail
        base = pl.multiple_of(c * 64, 64)
        down[pl.ds(base, 64)] = out[c, 0]
        up[pl.ds(base, 64)] = out[c, 7]
        return carry

    lax.fori_loop(0, 3, body, 0)
    hz = jnp.broadcast_to(lanes[7:8, :128], (8, 128))
    down[192:200] = hz
    up[192:200] = hz


def finish_sum(field, zlo, zhi, out, factor):
    def body(c, carry):
        base = pl.multiple_of(c * 64, 64)
        for i in range(8):
            x = field[c, i]
            if i == 0:
                x = x + zlo[pl.ds(base, 64)]
            if i == 7:
                x = x + zhi[pl.ds(base, 64)]
            for j in range(8):
                v = x[8 * j : 8 * j + 8]
                below, above = radial_parts(v)
                out[c, i, 8 * j : 8 * j + 8] = radial_sum(v, below, above) * factor(i, j)
        return carry

    lax.fori_loop(0, 3, body, 0)


def put(ref, at, rb, half, x):
    hi, lo = split(x)
    for term, part in enumerate((hi, hi, lo, lo)):
        rows = pl.ds(pl.multiple_of(term * 64 + rb * 16, 16), 16)
        ref[at, rows, half * 128 : half * 128 + 128] = part


def along_pipe(u, xu, xw, xs=None, sz=None):
    def body(t, carry):
        c, rb = t // 4, t % 4
        rows = pl.ds(pl.multiple_of(rb * 16, 16), 16)
        x = [u[c, i, rows] for i in range(8)]
        for a, val in enumerate(even_odd(J, x, 1)):
            put(xu, c * 6 + a // 2, rb, a % 2, val)
        for a, val in enumerate(even_odd(B, x, -1)):
            put(xw, c * 6 + a // 2, rb, a % 2, val)
        if xs is None:
            return carry
        for i in range(8):
            put(xs, c * 4 + i // 2, rb, i % 2, x[i])
        for i, val in enumerate(even_odd(STIFF, x, 1)):
            sz[c, i, rows] = val
        return carry

    lax.fori_loop(0, 12, body, 0)


def fine_dots(p, at, fine, xu, xw, pf, qf):
    for c in range(3):
        pf[at, c] = dot(fine[...], xu[c * 6 + p])
        qf[at, c] = dot(fine[0:144], xw[c * 6 + p])


def stiff_dots(p, stiff, xs, ks):
    for t in (2 * p, 2 * p + 1):
        y = dot(stiff[...], xs[t])
        c, q = t // 4, t % 4
        ks[c, 2 * q] = y[:, :128]
        ks[c, 2 * q + 1] = y[:, 128:]


def put_conv(xc, c, r, conv):
    hi, lo = split(conv)
    xc[c, 16 * r : 16 * r + 16] = hi
    xc[c, 144 + 16 * r : 160 + 16 * r] = hi
    xc[c, 288 + 16 * r : 304 + 16 * r] = lo


def back_dots(p, back, xc, yf, count):
    for c in range(count):
        y = dot(back[...], xc[c])
        yf[c, 2 * p] = y[:, :128]
        yf[c, 2 * p + 1] = y[:, 128:]


def fine_rows(pf, qf, p, c, r):
    rows = slice(16 * r, 16 * r + 16)
    return (
        qf[p, c, rows],
        pf[p, c, 144 + 16 * r : 160 + 16 * r],
        pf[p, c, 288 + 16 * r : 304 + 16 * r],
    )


def velocity_rows(pf, lanes, p, r):
    rows = slice(16 * r, 16 * r + 16)
    return [pf[p, n, rows] * lanes[n + 1 : n + 2] for n in range(3)]


def stiff_plane(lanes, wjk, sz, ks, c, i, rb):
    rows = pl.ds(pl.multiple_of(rb * 16, 16), 16)
    more = pl.ds(pl.multiple_of(64 + rb * 16, 16), 16)
    kz, kt, kr = lanes[4:5, :128], lanes[5:6, :128], lanes[6:7, :128]
    plane = kt * ks[c, i, rows] + kr * ks[c, i, more]
    return wjk[rows] * kz * sz[c, i, rows] + float(W[i]) * plane


def residual(u, lanes, fine, back, stiff, wjk, res, pf, qf, xu, xw, xs, xc0, xc1, yf, sz, ks):
    along_pipe(u, xu, xw, xs, sz)
    fine_dots(0, 0, fine, xu, xw, pf, qf)
    for p in range(6):
        if p < 5:
            fine_dots(p + 1, (p + 1) % 2, fine, xu, xw, pf, qf)
        stiff_dots(p, stiff, xs, ks)
        xc = (xc0, xc1)[p % 2]
        for r in range(9):
            v = velocity_rows(pf, lanes, p % 2, r)
            for c in range(3):
                g = fine_rows(pf, qf, p % 2, c, r)
                put_conv(xc, c, r, v[0] * g[0] + v[1] * g[1] + v[2] * g[2])
        back_dots(p, back, xc, yf, 3)
    keep = keep_rows(16)

    def body(t, carry):
        c, rb = t // 4, t % 4
        rows = pl.ds(pl.multiple_of(rb * 16, 16), 16)
        adv = even_odd(JV, [yf[c, a, rows] for a in range(12)], 1)
        for i in range(8):
            res[c, i, rows] = -(adv[i] + stiff_plane(lanes, wjk, sz, ks, c, i, rb)) * keep
        return carry

    lax.fori_loop(0, 12, body, 0)


def fields_kernel(u, fine, pf, qf, xu, xw):
    along_pipe(u, xu, xw)
    for p in range(6):
        fine_dots(p, p, fine, xu, xw, pf, qf)


def corner_weights():
    row, col = iota((8, 64), 0), iota((8, 64), 1)

    def weight(node, upper):
        acc = jnp.zeros((8, 64), F32)
        for n in range(8):
            acc = jnp.where(
                node == n, jnp.where(upper, float(LIN[1, n]), float(LIN[0, n])), acc
            )
        return acc

    return weight(col >> 3, (row & 2) != 0) * weight(col & 7, (row & 1) != 0)


def corners_kernel(res, out):
    weights = corner_weights()
    for c in range(3):
        planes = [res[c, i] for i in range(8)]
        z1 = sum(float(LIN[1, i]) * planes[i] for i in range(1, 8))
        z0 = sum(float(LIN[0, i]) * planes[i] for i in range(7))
        both = jnp.concatenate([z0, z1], axis=1)
        out[c] = jnp.dot(weights, both, precision=EXACT, preferred_element_type=F32)


def change_kernel(
    d, pf, qf, lanes, fine, stiff, wjk, coarse, out, pd, qd, xd, xe, xs, acc, xc, sz
):
    mean_w = LIN * W[None, :]
    mean_s = LIN @ STIFF

    def body(t, carry):
        c, rb = t // 4, t % 4
        rows = pl.ds(pl.multiple_of(rb * 16, 16), 16)
        x = [d[c, i, rows] for i in range(8)]
        for a, val in enumerate(even_odd(J, x, 1)):
            put(xd, c * 6 + a // 2, rb, a % 2, val)
        for a, val in enumerate(even_odd(B, x, -1)):
            put(xe, c * 6 + a // 2, rb, a % 2, val)
        for a in range(2):
            put(xs, c, rb, a, sum(float(mean_w[a, i]) * x[i] for i in range(8)))
            sz[c, a, rows] = sum(float(mean_s[a, i]) * x[i] for i in range(8))
        return carry

    lax.fori_loop(0, 12, body, 0)
    acc[...] = jnp.zeros_like(acc)

    def add_conv(n, p, r, conv):
        rows = slice(16 * r, 16 * r + 16)
        left, right = conv[:, :128], conv[:, 128:]
        for a in range(2):
            acc[n, rows, 128 * a : 128 * a + 128] += (
                float(COARSE_Z[a, 2 * p]) * left + float(COARSE_Z[a, 2 * p + 1]) * right
            )

    fine_dots(0, 0, fine, xd, xe, pd, qd)
    for p in range(6):
        if p < 5:
            fine_dots(p + 1, (p + 1) % 2, fine, xd, xe, pd, qd)
        for r in range(9):
            v = velocity_rows(pf, lanes, p, r)
            w = velocity_rows(pd, lanes, p % 2, r)
            for c in range(3):
                g = fine_rows(pf, qf, p, c, r)
                h = fine_rows(pd, qd, p % 2, c, r)
                one = (v[0] * h[0] + v[1] * h[1] + v[2] * h[2]) + (
                    w[0] * g[0] + w[1] * g[1] + w[2] * g[2]
                )
                add_conv(c, p, r, one)
                add_conv(3 + c, p, r, w[0] * h[0] + w[1] * h[1] + w[2] * h[2])
    r = iota((4, 256), 1) & (RADIAL - 1)
    upper = iota((4, 256), 0) & 1
    wall = ((upper == 0) & (r == 0)) | ((upper == 1) & (r == RADIAL - 1))
    wall = jnp.where(wall, 1.0, 0.0).astype(F32)
    keep = jnp.concatenate([keep_rows(64)] * 2, axis=1)
    wide = jnp.concatenate([wjk[...]] * 2, axis=1)
    kz, kt, kr = lanes[4:5], lanes[5:6], lanes[6:7]
    weights = corner_weights()
    for n in range(6):
        for q in range(9):
            put_conv(xc, n, q, acc[n, 16 * q : 16 * q + 16])
        y = dot(coarse[...], xc[n])
        total = y[0:4] - wall * y[4:8]
        if n < 3:
            ks = dot(stiff[...], xs[n])
            plane = jnp.concatenate([sz[n, 0], sz[n, 1]], axis=1) * wide * kz
            plane = (plane + kt * ks[0:64] + kr * ks[64:128]) * keep
            total = (
                total
                + jnp.dot(weights, plane, precision=EXACT, preferred_element_type=F32)[0:4]
            )
        out[n, 0:4] = -total
        out[n, 4:8] = jnp.zeros((4, 256), F32)


def pack_two(res, low, high):
    def body(c, carry):
        for n in range(2):
            low[c, 8 * n : 8 * n + 8] = pack_low(lambda i: res[c, i, 8 * n : 8 * n + 8])
            high[c, 8 * n : 8 * n + 8] = pack_high(
                lambda i: res[c, i, 48 + 8 * n : 56 + 8 * n]
            )
        return carry

    lax.fori_loop(0, 3, body, 0)


def project_kernel(
    field, tlo, thi, hz_low, hz_high, lanes, fine, back, stiff, wjk, u, res, low, high, *scratch
):
    hz = lanes[7:8, :128]
    inner = 1.0 / hz
    first = 1.0 / (hz + hz_low[192:193])
    last = 1.0 / (hz + hz_high[192:193])
    k = iota((8, 128), 0)
    rk = jnp.where(
        k == 0, lanes[9:10, :128], jnp.where(k == 7, lanes[10:11, :128], lanes[8:9, :128])
    )
    rk = rk * keep_rows(8)
    by_plane = {0: rk * first, 7: rk * last}
    middle = rk * inner

    def body(c, carry):
        lo, hi = tlo[c], thi[c]
        for i in range(8):
            x = field[c, i]
            for j in range(8):
                v = x[8 * j : 8 * j + 8]
                f = by_plane.get(i, middle)
                if j == 0:
                    v, f = v + from_low(x[56:64], lo, i), 0.5 * f
                if j == 7:
                    v, f = v + from_high(x[0:8], hi, i), 0.5 * f
                below, above = radial_parts(v)
                u[c, i, 8 * j : 8 * j + 8] = radial_sum(v, below, above) * f
        return carry

    lax.fori_loop(0, 3, body, 0)
    residual(u, lanes, fine, back, stiff, wjk, res, *scratch)
    pack_two(res, low, high)


def step_length(sums):
    total = jnp.sum(sums[...], axis=0, keepdims=True)
    return total[:, 0:1] / total[:, 1:2]


def advance_kernel(u_old, d, sums, lanes, fine, back, stiff, wjk, u, res, low, high, *scratch):
    alpha = step_length(sums)

    def body(t, carry):
        c, i = t // 8, t % 8
        u[c, i] = u_old[c, i] + alpha * d[c, i]
        return carry

    lax.fori_loop(0, 24, body, 0)
    residual(u, lanes, fine, back, stiff, wjk, res, *scratch)
    pack_two(res, low, high)


def around_widen_kernel(res, tlo, thi, out, down, up):
    lane = iota((8, 128), 1)

    def body(c, carry):
        lo6, lo7, hi0, hi1 = tlo[c, 0:8], tlo[c, 8:16], thi[c, 0:8], thi[c, 8:16]
        for i in range(8):
            x = res[c, i]
            first, last = x[0:8], x[56:64]
            out[c, i, 0:64] = x
            out[c, i, 0:8] = first + from_low(last, lo7, i)
            out[c, i, 56:64] = last + from_high(first, hi0, i)
            out[c, i, 64:72] = jnp.where(
                lane < 64, lanes_by(lo6, -16 * i), lanes_by(hi1, 112 - 16 * i)
            )
        for n in range(2):
            down[c, n] = out[c, n]
            up[c, n] = out[c, 6 + n]
        return carry

    lax.fori_loop(0, 3, body, 0)


def widen_planes(e, xf, half):
    lane, k = iota((8, 128), 1), iota((8, 128), 0)
    extra = e[64:72]
    planes = [e[8 * j : 8 * j + 8] for j in range(8)]
    under = jnp.where(lane < 16, extra, lanes_by(planes[6], 16))
    over = jnp.where(lane >= 112, extra, lanes_by(planes[1], -16))
    cols = slice(half * 128, half * 128 + 128)
    for j, v in enumerate([under] + planes + [over]):
        below, above = radial_parts(v)
        own = radial_sum(v, below, above)
        side = jnp.where(k == 0, rows_by(below, 2), jnp.where(k == 1, above, 0.0))
        hi, lo = split(jnp.concatenate([own, side], axis=0))
        xf[16 * j : 16 * j + 16, cols] = hi
        xf[160 + 16 * j : 176 + 16 * j, cols] = hi
        xf[320 + 16 * j : 336 + 16 * j, cols] = lo


def transform_kernel(field, forward, vectors, out, xf0, xf1, yf):
    def body(c, carry):
        for p in range(4):
            buf = (xf0, xf1)[p % 2]
            for half in range(2):
                widen_planes(field[c, 2 * p + half], buf, half)
            y = dot(forward[...], buf[...])
            yf[c, 2 * p] = y[:, :128]
            yf[c, 2 * p + 1] = y[:, 128:]
        return carry

    lax.fori_loop(0, 3, body, 0)

    def mid(rb, carry):
        rows = pl.ds(pl.multiple_of(rb * 16, 16), 16)
        y = [[yf[c, i, rows] for i in range(8)] for c in range(3)]
        for a in range(10):
            acc = [vectors[1, a] * y[c][0] for c in range(3)]
            for i in range(1, 8):
                s = vectors[i + 1, a]
                acc = [acc[c] + s * y[c][i] for c in range(3)]
            for c in range(3):
                out[c, a, rows] = acc[c]
        return carry

    lax.fori_loop(0, 7, mid, 0)


def solve_kernel(
    own, zlo, zhi, vectors, forward, inverse, scale, corr, low, high, xf0, xf1, yf, xb
):
    for c in range(3):
        for n, (buf, halo) in enumerate(((xf0, zlo), (xf1, zhi))):
            widen_planes(halo[c, 0], buf.at[c], 0)
            widen_planes(halo[c, 1], buf.at[c], 1)
            y = dot(forward[...], buf[c])
            yf[c, 2 * n] = y[:, :128]
            yf[c, 2 * n + 1] = y[:, 128:]

    def mid(rb, carry):
        rows = pl.ds(pl.multiple_of(rb * 16, 16), 16)
        y = [[yf[c, i, rows] for i in range(4)] for c in range(3)]
        spec = []
        for a in range(10):
            acc = [own[c, a, rows] for c in range(3)]
            for n, i in enumerate((0, 1, 8, 9)):
                s = vectors[i, a]
                acc = [acc[c] + s * y[c][n] for c in range(3)]
            f = scale[a, rows]
            spec.append([acc[c] * f for c in range(3)])
        for i in range(8):
            acc = [vectors[i + 1, 0] * spec[0][c] for c in range(3)]
            for a in range(1, 10):
                s = vectors[i + 1, a]
                acc = [acc[c] + s * spec[a][c] for c in range(3)]
            cols = slice((i % 2) * 128, (i % 2) * 128 + 128)
            for c in range(3):
                hi, lo = split(acc[c])
                for term, part in enumerate((hi, hi, lo)):
                    xb[c * 4 + i // 2, pl.ds(pl.multiple_of(term * 112 + rb * 16, 16), 16),
                       cols] = part
        return carry

    lax.fori_loop(0, 7, mid, 0)

    k = iota((8, 128), 0)
    r = iota((8, 128), 1) & (RADIAL - 1)
    inner = ((k == 0) & (r > 0)) | ((k == 7) & (r < RADIAL - 1))
    share = jnp.where(inner, 0.5, 1.0).astype(F32)
    for t in range(12):
        c, p = t // 4, t % 4
        y = dot(inverse[...], xb[t])
        for half in range(2):
            i = 2 * p + half
            for j in range(8):
                f = (0.5 if i in (0, 7) else 1.0) * (0.5 if j in (0, 7) else 1.0)
                corr[c, i, 8 * j : 8 * j + 8] = (
                    y[8 * j : 8 * j + 8, half * 128 : half * 128 + 128] * (share * f)
                )

    def last(c, carry):
        low[c] = pack_low(lambda i: corr[c, i, 0:8])
        high[c] = pack_high(lambda i: corr[c, i, 56:64])
        return carry

    lax.fori_loop(0, 3, last, 0)


def direction_kernel(field, zlo, zhi, res, lanes, grad, wjk, d, sums, xs, acc):
    keep = keep_rows(8)
    finish_sum(field, zlo, zhi, d, lambda i, j: keep)
    acc[...] = jnp.zeros_like(acc)
    vol = lanes[0:1, :128]
    kz, kt, kr = lanes[4:5, :128], lanes[5:6, :128], lanes[6:7, :128]

    def first(t, carry):
        c, rb = t // 4, t % 4
        rows = pl.ds(pl.multiple_of(rb * 16, 16), 16)
        x = [d[c, i, rows] for i in range(8)]
        num = sum(x[i] * res[c, i, rows] for i in range(8))
        sq = sum(float(W[i]) * (x[i] * x[i]) for i in range(8))
        gz = sum(float(W[i]) * (g * g) for i, g in enumerate(even_odd(D, x, -1)))
        acc[0] += num
        acc[1] += wjk[rows] * (SIGMA * vol * sq + kz * gz)
        for i in range(8):
            hi, lo = split(x[i])
            for term, part in enumerate((hi, hi, lo, lo)):
                xs[c * 4 + i // 2, pl.ds(pl.multiple_of(term * 64 + rb * 16, 16), 16),
                   (i % 2) * 128 : (i % 2) * 128 + 128] = part
        return carry

    lax.fori_loop(0, 12, first, 0)

    total = acc[1]
    for t in range(12):
        y = dot(grad[...], xs[t])
        for half in range(2):
            v = y[:, half * 128 : half * 128 + 128]
            v = v * v
            plane = jnp.zeros((16, 128), F32)
            for q in range(4):
                rows = slice(16 * q, 16 * q + 16)
                plane = plane + wjk[rows] * (kt * v[rows] + kr * v[64 + 16 * q : 80 + 16 * q])
            total = total + float(W[2 * (t % 4) + half]) * plane
    acc[1] = total
    num = jnp.sum(jnp.sum(acc[0], axis=0, keepdims=True), axis=1, keepdims=True)
    den = jnp.sum(jnp.sum(acc[1], axis=0, keepdims=True), axis=1, keepdims=True)
    at = iota((128, 128), 1)
    sums[...] = jnp.where(at == 0, num, jnp.where(at == 1, den, 0.0))


def route_kernel(slot, corner, right, owner):
    hot = (slot[...] == iota((128, 128), 0)).astype(F32)
    nt = (((1,), (1,)), ((), ()))
    ids = corner[...].astype(F32)
    by_elem = lax.dot_general(hot, ids, nt, precision=EXACT, preferred_element_type=F32)
    by_corner = lax.dot_general(ids, hot, nt, precision=EXACT, preferred_element_type=F32)
    owner[...] = (by_corner + 0.5).astype(jnp.int32) // 136
    ids = (by_elem + 0.5).astype(jnp.int32)
    inside = ids - ids // 136 * 136
    pos = iota((128, 256), 1)
    for q in range(8):
        right[128 * q : 128 * q + 128] = (inside[:, q : q + 1] == pos).astype(F32).astype(BF16)


def placed(values, right, owner, left):
    dev = iota((128, 128), 0)
    for c, both in enumerate(values):
        hi = both.astype(BF16).astype(F32)
        for q in range(8):
            mine = owner[q : q + 1] == dev
            cols = slice((q // 4) * 128, (q // 4) * 128 + 128)
            for m, piece in enumerate((hi, both - hi)):
                at = (2 * c + m) * 128
                left[at : at + 128, 128 * q : 128 * q + 128] = jnp.where(
                    mine, piece[q % 4 : q % 4 + 1, cols], 0.0
                ).astype(BF16)
    y = dot(left[...], right[...])
    return [y[256 * c : 256 * c + 128] + y[256 * c + 128 : 256 * c + 256] for c in range(3)]


def place_base_kernel(base, right, owner, out, left):
    for c, total in enumerate(placed([base[c] for c in range(3)], right, owner, left)):
        out[c] = lanes_by(total, 8 * c)


def place_kernel(base, change, right, owner, part, dense, left0, left1):
    blocks = [base[c] for c in range(3)]
    for n, left in enumerate((left0, left1)):
        values = [change[3 * n + c] for c in range(3)]
        for c, total in enumerate(placed(values, right, owner, left)):
            blocks.append(lanes_by(total, 8 * (3 * n + 3 + c)))
    spill = None
    for n, total in enumerate(blocks):
        first = total[:, :128]
        dense[pl.ds(n, 128, stride=10)] = first if spill is None else first + spill
        spill = total[:, 128:]
    dense[pl.ds(9, 128, stride=10)] = spill + lanes_by(part[...], 72)


def store_kernel(u, d, slot, u_hbm, d_hbm, u_out, d_out, sems):
    hot = (slot[...] == iota((128, 128), 0)).astype(F32)
    copies = []
    for c in range(3):
        for n, (x, y, out) in enumerate(((u, u_out, u_hbm), (d, d_out, d_hbm))):
            flat = x[c].reshape(512, 128)
            y[c] = jnp.dot(flat, hot, precision=EXACT, preferred_element_type=F32).reshape(
                8, 64, 128
            )
            copies.append(pltpu.make_async_copy(y.at[c], out.at[c], sems.at[2 * c + n]))
            copies[-1].start()
    for copy in copies:
        copy.wait()


def end_kernel(u_hbm, d_hbm, parts, vel_hbm, coarse_hbm, u, d, vel, coarse, sems):
    last = pltpu.make_async_copy(coarse, coarse_hbm, sems.at[0])
    loads = [
        [
            pltpu.make_async_copy(a.at[c], b.at[c], sems.at[1 + 2 * c + n])
            for n, (a, b) in enumerate(((u_hbm, u), (d_hbm, d)))
        ]
        for c in range(3)
    ]
    stores = [
        pltpu.make_async_copy(vel.at[c], vel_hbm.at[c], sems.at[7 + c]) for c in range(3)
    ]
    for pair in loads:
        for copy in pair:
            copy.start()
    sums = [
        jnp.sum(parts[pl.ds(n, 128, stride=10)], axis=0, keepdims=True) for n in range(10)
    ]
    alpha = sums[9][:, 72:73] / sums[9][:, 73:74]
    for c in range(3):
        for copy in loads[c]:
            copy.wait()
        vel[c] = u[c] + alpha * d[c]
        stores[c].start()
    total = jnp.concatenate(sums, axis=1)
    one, two = lanes_by(total, -408), lanes_by(total, -816)
    both = total + alpha * (one + alpha * two)
    for c in range(3):
        coarse[c : c + 1] = lanes_by(both, -136 * c)[:, :136]
    last.start()
    for copy in (*stores, last):
        copy.wait()


FIELD = (3, 8, 64, 128)


def both_ways(axis, to_next, to_prev):
    n = lax.axis_size(axis)
    up = [(i, (i + 1) % n) for i in range(n)]
    down = [((i + 1) % n, i) for i in range(n)]
    return lax.ppermute(to_next, axis, up), lax.ppermute(to_prev, axis, down)


def fine_scratch():
    return [
        pltpu.VMEM((2, 3, 432, 256), F32),
        pltpu.VMEM((2, 3, 144, 256), F32),
        pltpu.VMEM((18, 256, 256), BF16),
        pltpu.VMEM((18, 256, 256), BF16),
    ]


def local_scratch(count):
    return [
        pltpu.VMEM((12, 256, 256), BF16),
        pltpu.VMEM((count, 432, 256), BF16),
        pltpu.VMEM((count, 432, 256), BF16),
        pltpu.VMEM((count, 12, 64, 128), F32),
        pltpu.VMEM(FIELD, F32),
        pltpu.VMEM((3, 8, 128, 128), F32),
    ]


def shards(vel, slot, corner, axial, arc, rad, vectors, values):
    smem, hbm = pltpu.SMEM, pltpu.HBM
    small = ((3, 8, 128), F32)
    count = len(CONSTANTS)
    vel = vel.reshape(FIELD)
    down, up, lanes = call(
        faces_kernel,
        [((200, 128), F32), ((200, 128), F32), ((16, 256), F32)],
        (vel, slot, arc, rad, axial),
        [
            pltpu.VMEM((2, 3, 64, 128), F32),
            pltpu.VMEM((1, 128), jnp.int32),
            pltpu.SMEM((RADIAL,), F32),
            pltpu.SMEM((RADIAL,), F32),
            pltpu.SemaphoreType.DMA((9,)),
        ],
        spaces={0: hbm, 1: hbm, 2: hbm, 3: hbm, 4: smem},
    )
    zlo, zhi = both_ways("wide", up, down)
    mv, fine, back, stiff, grad, coarse_jk, wjk = call(
        inner_kernel,
        [((3, 6, 64, 128), F32)] + [(m.shape, m.dtype) for m in CONSTANTS],
        (vel, slot, lanes, *(jnp.asarray(m) for m in CONSTANTS)),
        [
            pltpu.VMEM((3, 6, 64, 128), F32),
            pltpu.VMEM((1, 128), jnp.int32),
            pltpu.SemaphoreType.DMA((4 + count,)),
        ],
        spaces={0: hbm, 1: hbm, **{3 + i: hbm for i in range(count)}},
    )
    zlo, zhi, mv, fine, back, stiff, grad, coarse_jk, wjk = lax.optimization_barrier(
        (zlo, zhi, mv, fine, back, stiff, grad, coarse_jk, wjk)
    )
    field, low, high = call(
        pipe_sum_kernel, [(FIELD, F32), small, small], (mv, down, up, zlo, zhi)
    )
    forward, inverse, scale = call(
        solve_tables_kernel,
        [((112, 480), BF16), ((64, 336), BF16), ((10, 112, 128), F32)],
        (vectors, values[None], lanes),
        [
            pltpu.VMEM((10, 10), F32),
            pltpu.VMEM((1, 10), F32),
            pltpu.SemaphoreType.DMA((2,)),
        ],
        spaces={0: hbm, 1: hbm},
    )

    def sum_rounds(field, low, high, beside=()):
        tlo, thi = both_ways("narrow", high, low)
        out, down, up = call(
            around_sum_kernel,
            [(FIELD, F32), ((200, 128), F32), ((200, 128), F32)],
            (field, tlo, thi, lanes),
        )
        zlo, zhi = both_ways("wide", up, down)
        zlo, zhi, beside = lax.optimization_barrier((zlo, zhi, beside))
        return (out, zlo, zhi), beside

    local = (lanes, fine, back, stiff, wjk)
    packs = [(FIELD, F32), (FIELD, F32), ((3, 16, 128), F32), ((3, 16, 128), F32)]
    u, res, low, high = call(
        project_kernel,
        packs,
        (field, *both_ways("narrow", high, low), zlo, zhi, *local),
        fine_scratch() + local_scratch(3),
    )
    for step in range(2):
        if step > 0:
            sums = lax.all_to_all(part, BOTH, 0, 0, tiled=True)
            u, res, low, high = call(
                advance_kernel, packs, (u, d, sums, *local), fine_scratch() + local_scratch(3)
            )
        tlo, thi = both_ways("narrow", high, low)
        wide_field, down, up = call(
            around_widen_kernel,
            [((3, 8, 72, 128), F32), ((3, 2, 72, 128), F32), ((3, 2, 72, 128), F32)],
            (res, tlo, thi),
        )
        zlo, zhi = both_ways("wide", up, down)
        (own,) = call(
            transform_kernel,
            [((3, 10, 112, 128), F32)],
            (wide_field, forward, vectors),
            [
                pltpu.VMEM((480, 256), BF16),
                pltpu.VMEM((480, 256), BF16),
                pltpu.VMEM((3, 8, 112, 128), F32),
            ],
            spaces={2: smem},
        )
        zlo, zhi, own = lax.optimization_barrier((zlo, zhi, own))
        corr, low, high = call(
            solve_kernel,
            [(FIELD, F32), small, small],
            (own, zlo, zhi, vectors, forward, inverse, scale),
            [
                pltpu.VMEM((3, 480, 256), BF16),
                pltpu.VMEM((3, 480, 256), BF16),
                pltpu.VMEM((3, 4, 112, 128), F32),
                pltpu.VMEM((12, 336, 256), BF16),
            ],
            spaces={3: smem},
        )
        beside = ()
        if step == 1:
            fields = [((6, 3, 432, 256), F32), ((6, 3, 144, 256), F32)]
            right, owner = call(
                route_kernel,
                [((1024, 256), BF16), ((8, 128), jnp.int32)],
                (slot, corner),
                free=True,
            )
            (base,) = call(corners_kernel, [((3, 8, 256), F32)], (res,))
            (base,) = call(
                place_base_kernel,
                [((3, 128, 256), F32)],
                (base, right, owner),
                [pltpu.VMEM((768, 1024), BF16)],
            )
            beside = (call(fields_kernel, fields, (u, fine), fine_scratch()[2:]), base)
        halo, beside = sum_rounds(corr, low, high, beside)
        d, part = call(
            direction_kernel,
            [(FIELD, F32), ((128, 128), F32)],
            (*halo, res, lanes, grad, wjk),
            [pltpu.VMEM((12, 256, 256), BF16), pltpu.VMEM((2, 16, 128), F32)],
        )
    (pf, qf), base = beside
    (change,) = call(
        change_kernel,
        [((6, 8, 256), F32)],
        (d, pf, qf, lanes, fine, stiff, wjk, coarse_jk),
        fine_scratch()
        + [
            pltpu.VMEM((3, 256, 256), BF16),
            pltpu.VMEM((6, 144, 256), F32),
            pltpu.VMEM((6, 432, 256), BF16),
            pltpu.VMEM((3, 2, 64, 128), F32),
        ],
    )
    (dense,) = call(
        place_kernel,
        [((1280, 128), F32)],
        (base, change, right, owner, part),
        [pltpu.VMEM((768, 1024), BF16), pltpu.VMEM((768, 1024), BF16)],
    )
    parts = lax.all_to_all(dense.reshape(128, 1, 1280), BOTH, 0, 0, tiled=True)
    parts = parts.reshape(1280, 128)
    u, d = call(
        store_kernel,
        [(FIELD, F32), (FIELD, F32)],
        (u, d, slot),
        [pltpu.VMEM(FIELD, F32), pltpu.VMEM(FIELD, F32), pltpu.SemaphoreType.DMA((6,))],
        hbm_out={0, 1},
        free=True,
    )
    out, coarse = call(
        end_kernel,
        [(FIELD, F32), ((3, 136), F32)],
        (u, d, parts),
        [
            pltpu.VMEM(FIELD, F32),
            pltpu.VMEM(FIELD, F32),
            pltpu.VMEM(FIELD, F32),
            pltpu.VMEM((3, 136), F32),
            pltpu.SemaphoreType.DMA((10,)),
        ],
        spaces={0: pltpu.HBM, 1: pltpu.HBM},
        hbm_out={0, 1},
    )
    return out.reshape(3, 512, 128), coarse


def solution(mesh):
    return jax.shard_map(
        shards,
        mesh=mesh,
        in_specs=(P(None, None, BOTH), P(BOTH, None), P(None, BOTH), P("wide"), P(), P(), P(), P()),
        out_specs=(P(None, None, BOTH), P(None, BOTH)),
        check_vma=False,
    )
```

```python
from functools import partial

import jax
import jax.numpy as jnp
import ml_dtypes
import numpy as np
from jax import lax
from jax.experimental import pallas as pl
from jax.experimental.pallas import tpu as pltpu
from jax.sharding import PartitionSpec as P

RADIAL = 16
SIGMA = 4.0
VISCOSITY = 0.05
F32 = jnp.float32
BF16 = jnp.bfloat16
EXACT = lax.Precision.HIGHEST
BOTH = ("wide", "narrow")


def node_tables():
    x = np.array(
        [-1.0, -0.8717401485096066, -0.5917001814331423, -0.2092992179024789]
    )
    x = np.concatenate([x, -x[::-1]])
    w = np.array([1.0 / 28.0, 0.2107042271435061, 0.3411226924835044, 0.4124587946587038])
    w = np.concatenate([w, w[::-1]])
    scale = np.array([np.prod([x[t] - x[p] for p in range(8) if p != t]) for t in range(8)])
    deriv = np.zeros((8, 8))
    for t in range(8):
        for s in range(8):
            if t != s:
                deriv[t, s] = scale[t] / (scale[s] * (x[t] - x[s]))
        deriv[t, t] = -np.sum(deriv[t])
    y = np.array(
        [
            -0.9815606342467192,
            -0.9041172563704749,
            -0.7699026741943047,
            -0.5873179542866175,
            -0.3678314989981802,
            -0.1252334085114689,
        ]
    )
    y = np.concatenate([y, -y[::-1]])
    v = np.array(
        [
            0.0471753363865118,
            0.1069393259953184,
            0.1600783285433462,
            0.2031674267230659,
            0.2334925365383548,
            0.2491470458134028,
        ]
    )
    v = np.concatenate([v, v[::-1]])
    interp = np.ones((12, 8))
    for s in range(8):
        for p in range(8):
            if p != s:
                interp[:, s] = interp[:, s] * (y - x[p]) / (x[s] - x[p])
    linear = np.stack([(1.0 - x) / 2.0, (1.0 + x) / 2.0])
    return w, deriv, v, interp, linear


W, D, VF, J, LIN = node_tables()
B = J @ D
JV = J.T * VF[None, :]
STIFF = D.T @ (W[:, None] * D)
WJK = np.kron(W, W)


WJK_ROWS = np.broadcast_to(WJK[:, None], (64, 128)).astype(np.float32)


def two_parts(matrix):
    hi = matrix.astype(np.float32).astype(ml_dtypes.bfloat16)
    lo = (matrix - hi.astype(np.float64)).astype(ml_dtypes.bfloat16)
    return hi, lo


def four_terms(matrix):
    hi, lo = two_parts(matrix)
    return np.concatenate([hi, lo, hi, lo], axis=1)


def three_terms(matrix):
    hi, lo = two_parts(matrix)
    return np.concatenate([hi, lo, hi], axis=1)


FINE = four_terms(np.concatenate([np.kron(J, J), np.kron(B, J), np.kron(J, B)]))
BACK = three_terms(np.kron(JV, JV))
STIFF_JK = four_terms(
    np.concatenate([np.kron(STIFF, np.diag(W)), np.kron(np.diag(W), STIFF)])
)
COARSE_Z = LIN @ JV
COARSE_JK = three_terms(
    np.concatenate(
        [
            np.kron(COARSE_Z, COARSE_Z),
            np.kron(COARSE_Z, np.stack([JV[0], JV[7]])),
            np.zeros((8, 144)),
        ]
    )
)
GRAD_JK = four_terms(np.concatenate([np.kron(D, np.eye(8)), np.kron(np.eye(8), D)]))


def call(kernel, outs, args, scratch=(), spaces=None, hbm_out=(), free=False):
    spaces = spaces or {}
    args = [
        a if free and i not in spaces
        else pltpu.with_memory_space_constraint(a, spaces.get(i, pltpu.VMEM))
        for i, a in enumerate(args)
    ]
    return pl.pallas_call(
        kernel,
        out_shape=[
            (pltpu.HBM if i in hbm_out else pltpu.VMEM)(s, d)
            for i, (s, d) in enumerate(outs)
        ],
        in_specs=[
            pl.BlockSpec(memory_space=spaces.get(i, pltpu.VMEM)) for i in range(len(args))
        ],
        out_specs=[
            pl.BlockSpec(memory_space=pltpu.HBM if i in hbm_out else pltpu.VMEM)
            for i in range(len(outs))
        ],
        scratch_shapes=list(scratch),
        compiler_params=pltpu.CompilerParams(vmem_limit_bytes=32 << 20),
        name=kernel.func.__name__ if isinstance(kernel, partial) else kernel.__name__,
    )(*args)


def iota(shape, dim):
    return lax.broadcasted_iota(jnp.int32, shape, dim)


def lanes_by(x, shift):
    return pltpu.roll(x, shift % x.shape[-1], x.ndim - 1)


def rows_by(x, shift):
    return pltpu.roll(x, shift % 8, x.ndim - 2)


def split(x):
    hi = x.astype(BF16)
    return hi, (x - hi.astype(F32)).astype(BF16)


def dot(a, b):
    return jnp.dot(a, b, preferred_element_type=F32)


def even_odd(matrix, xs, sign):
    n_out, n_in = matrix.shape
    half = n_in // 2
    even = [xs[i] + xs[n_in - 1 - i] for i in range(half)]
    odd = [xs[i] - xs[n_in - 1 - i] for i in range(half)]
    outs = [None] * n_out
    for a in range(n_out // 2):
        e = sum(
            float((matrix[a, i] + matrix[a, n_in - 1 - i]) / 2) * even[i] for i in range(half)
        )
        o = sum(
            float((matrix[a, i] - matrix[a, n_in - 1 - i]) / 2) * odd[i] for i in range(half)
        )
        outs[a] = e + o
        outs[n_out - 1 - a] = e - o if sign > 0 else o - e
    return outs


def keep_rows(rows):
    k = iota((rows, 128), 0) & 7
    r = iota((rows, 128), 1) & (RADIAL - 1)
    wall = ((k == 0) & (r == 0)) | ((k == 7) & (r == RADIAL - 1))
    return jnp.where(wall, 0.0, 1.0).astype(F32)


def radial_parts(x):
    r = iota((8, 128), 1) & (RADIAL - 1)
    below = jnp.where(r > 0, lanes_by(x, 1), 0.0)
    above = jnp.where(r < RADIAL - 1, lanes_by(x, -1), 0.0)
    return below, above


def radial_sum(x, below, above):
    k = iota((8, 128), 0)
    return x + jnp.where(k == 0, rows_by(below, 1), jnp.where(k == 7, rows_by(above, -1), 0.0))


def pack_low(plane_of):
    et = iota((8, 128), 1) >> 4
    out = jnp.zeros((8, 128), F32)
    for i in range(8):
        out = jnp.where(et == i, lanes_by(plane_of(i), 16 * i), out)
    return out


def pack_high(plane_of):
    et = iota((8, 128), 1) >> 4
    out = jnp.zeros((8, 128), F32)
    for i in range(8):
        out = jnp.where(et == i, lanes_by(plane_of(i), 16 * i + 16), out)
    return out


def from_low(plane, packed, i):
    lane = iota((8, 128), 1)
    return jnp.where(lane < 16, lanes_by(packed, -16 * i), lanes_by(plane, 16))


def from_high(plane, packed, i):
    lane = iota((8, 128), 1)
    return jnp.where(lane >= 112, lanes_by(packed, 112 - 16 * i), lanes_by(plane, -16))


CONSTANTS = (FINE, BACK, STIFF_JK, GRAD_JK, COARSE_JK, WJK_ROWS)
NT = (((1,), (1,)), ((), ()))


def faces_kernel(
    vel_hbm, slot_hbm, arc_hbm, rad_hbm, axial, down, up, lanes, vel, slot, arc, rad, sems
):
    copies = [
        pltpu.make_async_copy(arc_hbm, arc, sems.at[7]),
        pltpu.make_async_copy(rad_hbm, rad, sems.at[8]),
        pltpu.make_async_copy(slot_hbm, slot, sems.at[6]),
    ]
    for c in range(3):
        for n in range(2):
            copies.append(
                pltpu.make_async_copy(vel_hbm.at[c, 7 * n], vel.at[n, c], sems.at[3 * n + c])
            )
    for copy in copies:
        copy.start()
    for copy in copies[:2]:
        copy.wait()
    r = iota((1, 256), 1) & (RADIAL - 1)
    ht, hr = jnp.zeros((1, 256), F32), jnp.zeros((1, 256), F32)
    for i in range(RADIAL):
        ht = jnp.where(r == i, arc[i], ht)
        hr = jnp.where(r == i, rad[i], hr)
    hz = jnp.zeros((1, 256), F32) + axial[0]
    g = ht * hr / 8.0
    vol = hz * g
    g_low = g + jnp.where(r > 0, lanes_by(g, 1), 0.0)
    g_high = g + jnp.where(r < RADIAL - 1, lanes_by(g, -1), 0.0)
    rows = [
        vol,
        vol * (2.0 / hz),
        vol * (2.0 / ht),
        vol * (2.0 / hr),
        VISCOSITY * vol * (2.0 / hz) * (2.0 / hz),
        VISCOSITY * vol * (2.0 / ht) * (2.0 / ht),
        VISCOSITY * vol * (2.0 / hr) * (2.0 / hr),
        hz,
        1.0 / g,
        1.0 / g_low,
        1.0 / g_high,
    ]
    for n, row in enumerate(rows):
        lanes[n : n + 1] = row
    for n in range(len(rows), 16):
        lanes[n : n + 1] = jnp.zeros((1, 256), F32)
    for copy in copies[2:]:
        copy.wait()
    hot = (slot[...] == iota((128, 128), 0)).astype(F32)
    y = lax.dot_general(
        vel[...].reshape(384, 128), hot, NT, precision=EXACT, preferred_element_type=F32
    )
    y = y * vol[:, :128]
    for n, out in enumerate((down, up)):
        out[0:192] = y[192 * n : 192 * n + 192]
        out[192:200] = jnp.broadcast_to(hz[:, :128], (8, 128))


def inner_kernel(vel_hbm, slot_hbm, lanes, *refs):
    n = len(CONSTANTS)
    hbm, mv, held, (vel, slot, sems) = refs[:n], refs[n], refs[n + 1 : 2 * n + 1], refs[2 * n + 1 :]
    pairs = [(slot_hbm, slot)]
    pairs += [(vel_hbm.at[c, pl.ds(1, 6)], vel.at[c]) for c in range(3)]
    pairs += list(zip(hbm, held))
    copies = [pltpu.make_async_copy(a, b, sems.at[i]) for i, (a, b) in enumerate(pairs)]
    for copy in copies:
        copy.start()
    copies[0].wait()
    hot = (slot[...] == iota((128, 128), 0)).astype(F32)
    for c in range(3):
        copies[1 + c].wait()
        y = lax.dot_general(
            vel[c].reshape(384, 128), hot, NT, precision=EXACT, preferred_element_type=F32
        )
        mv[c] = (y * lanes[0:1, :128]).reshape(6, 64, 128)
    for copy in copies[4:]:
        copy.wait()


def pipe_sum_kernel(mv, down, up, zlo, zhi, field, low, high):
    def body(c, carry):
        rows = pl.ds(pl.multiple_of(c * 64, 64), 64)
        field[c, 0] = down[rows] + zlo[rows]
        for i in range(6):
            field[c, 1 + i] = mv[c, i]
        field[c, 7] = up[rows] + zhi[rows]
        low[c] = pack_low(lambda i: field[c, i, 0:8])
        high[c] = pack_high(lambda i: field[c, i, 56:64])
        return carry

    lax.fori_loop(0, 3, body, 0)


def solve_tables_kernel(
    vectors_hbm, values_hbm, lanes, forward, inverse, scale, vectors, values, sems
):
    copies = [
        pltpu.make_async_copy(vectors_hbm, vectors, sems.at[0]),
        pltpu.make_async_copy(values_hbm, values, sems.at[1]),
    ]
    for copy in copies:
        copy.start()
    for copy in copies:
        copy.wait()
    s = vectors[...]
    ident = (iota((10, 10), 0) == iota((10, 10), 1)).astype(F32)
    st = lax.dot_general(
        ident, s, (((1,), (1,)), ((), ())), precision=EXACT, preferred_element_type=F32
    )

    def mul(a, b):
        return jnp.dot(a, b, precision=EXACT, preferred_element_type=F32)

    row, col = iota((112, 10), 0), iota((112, 10), 1)
    live = row < 100
    by_b = ((row // 10 == col) & live).astype(F32)
    by_c = ((row % 10 == col) & live).astype(F32)
    node, pos = iota((10, 160), 0), iota((10, 160), 1)
    slot = pos & 15
    k_of = jnp.where(slot < 8, slot + 1, jnp.where(slot == 8, 0, jnp.where(slot == 9, 9, -1)))
    by_j = (node == (pos >> 4)).astype(F32)
    by_k = (node == k_of).astype(F32)
    full = mul(mul(by_b, st), by_j) * mul(mul(by_c, st), by_k)
    hi, lo = split(full)
    forward[:, 0:160] = hi
    forward[:, 160:320] = lo
    forward[:, 320:480] = hi

    row8, col8 = iota((64, 10), 0), iota((64, 10), 1)
    by_j8 = ((row8 >> 3) + 1 == col8).astype(F32)
    by_k8 = ((row8 & 7) + 1 == col8).astype(F32)
    node2, pos2 = iota((10, 112), 0), iota((10, 112), 1)
    b_of = jnp.where(pos2 < 100, pos2 // 10, -1)
    c_of = jnp.where(pos2 < 100, pos2 % 10, -1)
    to_b = (node2 == b_of).astype(F32)
    to_c = (node2 == c_of).astype(F32)
    full = mul(mul(by_j8, s), to_b) * mul(mul(by_k8, s), to_c)
    hi, lo = split(full)
    inverse[:, 0:112] = hi
    inverse[:, 112:224] = lo
    inverse[:, 224:336] = hi

    lam = jnp.broadcast_to(values[...], (8, 10))
    nt = (((1,), (1,)), ((), ()))
    lam_b = lax.dot_general(by_b, lam, nt, precision=EXACT, preferred_element_type=F32)[:, 0:1]
    lam_c = lax.dot_general(by_c, lam, nt, precision=EXACT, preferred_element_type=F32)[:, 0:1]
    vol = lanes[0:1, :128]
    flat = (
        SIGMA * vol
        + lam_b * jnp.broadcast_to(lanes[5:6, :128], (112, 128))
        + lam_c * jnp.broadcast_to(lanes[6:7, :128], (112, 128))
    )
    for a in range(10):
        scale[a] = 1.0 / (flat + values[0:1, a : a + 1] * lanes[4:5, :128])


def around_sum_kernel(field, tlo, thi, lanes, out, down, up):
    def body(c, carry):
        lo, hi = tlo[c], thi[c]
        for i in range(8):
            x = field[c, i]
            first, last = x[0:8], x[56:64]
            head = first + from_low(last, lo, i)
            tail = last + from_high(first, hi, i)
            out[c, i] = x
            out[c, i, 0:8] = head
            out[c, i, 56:64] = tail
        base = pl.multiple_of(c * 64, 64)
        down[pl.ds(base, 64)] = out[c, 0]
        up[pl.ds(base, 64)] = out[c, 7]
        return carry

    lax.fori_loop(0, 3, body, 0)
    hz = jnp.broadcast_to(lanes[7:8, :128], (8, 128))
    down[192:200] = hz
    up[192:200] = hz


def finish_sum(field, zlo, zhi, out, factor):
    def body(c, carry):
        base = pl.multiple_of(c * 64, 64)
        for i in range(8):
            x = field[c, i]
            if i == 0:
                x = x + zlo[pl.ds(base, 64)]
            if i == 7:
                x = x + zhi[pl.ds(base, 64)]
            for j in range(8):
                v = x[8 * j : 8 * j + 8]
                below, above = radial_parts(v)
                out[c, i, 8 * j : 8 * j + 8] = radial_sum(v, below, above) * factor(i, j)
        return carry

    lax.fori_loop(0, 3, body, 0)


def put(ref, at, rb, half, x):
    hi, lo = split(x)
    for term, part in enumerate((hi, hi, lo, lo)):
        start = term * 64 + rb * 16
        rows = pl.ds(start if isinstance(start, int) else pl.multiple_of(start, 16), 16)
        ref[at, rows, half * 128 : half * 128 + 128] = part


def along_pipe(u, c, rb, xu, xw):
    rows = pl.ds(rb * 16 if isinstance(rb, int) else pl.multiple_of(rb * 16, 16), 16)
    x = [u[c, i, rows] for i in range(8)]
    for a, val in enumerate(even_odd(J, x, 1)):
        put(xu, c * 6 + a // 2, rb, a % 2, val)
    for a, val in enumerate(even_odd(B, x, -1)):
        put(xw, c * 6 + a // 2, rb, a % 2, val)
    return rows, x


def fine_dots(pairs, parts, fine, xu, xw, pf, qf):
    for p in pairs:
        for c in parts:
            pf[p, c] = dot(fine[...], xu[c * 6 + p])
            qf[p, c] = dot(fine[0:144], xw[c * 6 + p])


def stiff_dots(c, stiff, xs, ks):
    for q in range(4):
        y = dot(stiff[...], xs[4 * c + q])
        ks[c, 2 * q] = y[:, :128]
        ks[c, 2 * q + 1] = y[:, 128:]


def put_conv(xc, c, r, conv):
    hi, lo = split(conv)
    xc[c, 16 * r : 16 * r + 16] = hi
    xc[c, 144 + 16 * r : 160 + 16 * r] = hi
    xc[c, 288 + 16 * r : 304 + 16 * r] = lo


def back_dots(p, back, xc, yf, count):
    for c in range(count):
        y = dot(back[...], xc[c])
        yf[c, 2 * p] = y[:, :128]
        yf[c, 2 * p + 1] = y[:, 128:]


def fine_rows(pf, qf, p, c, r):
    rows = slice(16 * r, 16 * r + 16)
    return (
        qf[p, c, rows],
        pf[p, c, 144 + 16 * r : 160 + 16 * r],
        pf[p, c, 288 + 16 * r : 304 + 16 * r],
    )


def velocity_rows(pf, lanes, p, r):
    rows = slice(16 * r, 16 * r + 16)
    return [pf[p, n, rows] * lanes[n + 1 : n + 2] for n in range(3)]


def stiff_plane(lanes, wjk, sz, ks, c, i, rb):
    rows = pl.ds(pl.multiple_of(rb * 16, 16), 16)
    more = pl.ds(pl.multiple_of(64 + rb * 16, 16), 16)
    kz, kt, kr = lanes[4:5, :128], lanes[5:6, :128], lanes[6:7, :128]
    plane = kt * ks[c, i, rows] + kr * ks[c, i, more]
    return wjk[rows] * kz * sz[c, i, rows] + float(W[i]) * plane


def residual(u, lanes, fine, back, stiff, wjk, res, pf, qf, xu, xw, xs, xc0, xc1, yf, sz, ks):
    for c in range(3):
        for rb in range(4):
            rows, x = along_pipe(u, c, rb, xu, xw)
            for i in range(8):
                put(xs, c * 4 + i // 2, rb, i % 2, x[i])
            for i, val in enumerate(even_odd(STIFF, x, 1)):
                sz[c, i, rows] = val
        fine_dots(range(6), (c,), fine, xu, xw, pf, qf)
        stiff_dots(c, stiff, xs, ks)
    for p in range(6):
        xc = (xc0, xc1)[p % 2]
        for r in range(9):
            v = velocity_rows(pf, lanes, p, r)
            for c in range(3):
                g = fine_rows(pf, qf, p, c, r)
                put_conv(xc, c, r, v[0] * g[0] + v[1] * g[1] + v[2] * g[2])
        back_dots(p, back, xc, yf, 3)
    keep = keep_rows(16)

    def body(t, carry):
        c, rb = t // 4, t % 4
        rows = pl.ds(pl.multiple_of(rb * 16, 16), 16)
        adv = even_odd(JV, [yf[c, a, rows] for a in range(12)], 1)
        for i in range(8):
            res[c, i, rows] = -(adv[i] + stiff_plane(lanes, wjk, sz, ks, c, i, rb)) * keep
        return carry

    lax.fori_loop(0, 12, body, 0)


def fields_kernel(u, fine, pf, qf, xu, xw):
    def body(t, carry):
        along_pipe(u, t // 4, t % 4, xu, xw)
        return carry

    lax.fori_loop(0, 12, body, 0)
    fine_dots(range(6), range(3), fine, xu, xw, pf, qf)


def corner_weights():
    row, col = iota((8, 64), 0), iota((8, 64), 1)

    def weight(node, upper):
        acc = jnp.zeros((8, 64), F32)
        for n in range(8):
            acc = jnp.where(
                node == n, jnp.where(upper, float(LIN[1, n]), float(LIN[0, n])), acc
            )
        return acc

    return weight(col >> 3, (row & 2) != 0) * weight(col & 7, (row & 1) != 0)


def corners_kernel(res, out):
    weights = corner_weights()
    for c in range(3):
        planes = [res[c, i] for i in range(8)]
        z1 = sum(float(LIN[1, i]) * planes[i] for i in range(1, 8))
        z0 = sum(float(LIN[0, i]) * planes[i] for i in range(7))
        both = jnp.concatenate([z0, z1], axis=1)
        out[c] = jnp.dot(weights, both, precision=EXACT, preferred_element_type=F32)


def change_kernel(
    d, pf, qf, lanes, fine, stiff, wjk, coarse, out, pd, qd, xd, xe, xs, acc, xc, sz
):
    mean_w = LIN * W[None, :]
    mean_s = LIN @ STIFF

    def body(t, carry):
        c, rb = t // 4, t % 4
        rows, x = along_pipe(d, c, rb, xd, xe)
        for a in range(2):
            put(xs, c, rb, a, sum(float(mean_w[a, i]) * x[i] for i in range(8)))
            sz[c, a, rows] = sum(float(mean_s[a, i]) * x[i] for i in range(8))
        return carry

    lax.fori_loop(0, 12, body, 0)
    acc[...] = jnp.zeros_like(acc)

    def add_conv(n, p, r, conv):
        rows = slice(16 * r, 16 * r + 16)
        left, right = conv[:, :128], conv[:, 128:]
        for a in range(2):
            acc[n, rows, 128 * a : 128 * a + 128] += (
                float(COARSE_Z[a, 2 * p]) * left + float(COARSE_Z[a, 2 * p + 1]) * right
            )

    fine_dots((0,), range(3), fine, xd, xe, pd, qd)
    for p in range(6):
        if p < 5:
            fine_dots((p + 1,), range(3), fine, xd, xe, pd, qd)
        for r in range(9):
            v = velocity_rows(pf, lanes, p, r)
            w = velocity_rows(pd, lanes, p, r)
            for c in range(3):
                g = fine_rows(pf, qf, p, c, r)
                h = fine_rows(pd, qd, p, c, r)
                one = (v[0] * h[0] + v[1] * h[1] + v[2] * h[2]) + (
                    w[0] * g[0] + w[1] * g[1] + w[2] * g[2]
                )
                add_conv(c, p, r, one)
                add_conv(3 + c, p, r, w[0] * h[0] + w[1] * h[1] + w[2] * h[2])
    r = iota((4, 256), 1) & (RADIAL - 1)
    upper = iota((4, 256), 0) & 1
    wall = ((upper == 0) & (r == 0)) | ((upper == 1) & (r == RADIAL - 1))
    wall = jnp.where(wall, 1.0, 0.0).astype(F32)
    keep = jnp.concatenate([keep_rows(64)] * 2, axis=1)
    wide = jnp.concatenate([wjk[...]] * 2, axis=1)
    kz, kt, kr = lanes[4:5], lanes[5:6], lanes[6:7]
    weights = corner_weights()
    for n in range(6):
        for q in range(9):
            put_conv(xc, n, q, acc[n, 16 * q : 16 * q + 16])
        y = dot(coarse[...], xc[n])
        total = y[0:4] - wall * y[4:8]
        if n < 3:
            ks = dot(stiff[...], xs[n])
            plane = jnp.concatenate([sz[n, 0], sz[n, 1]], axis=1) * wide * kz
            plane = (plane + kt * ks[0:64] + kr * ks[64:128]) * keep
            total = (
                total
                + jnp.dot(weights, plane, precision=EXACT, preferred_element_type=F32)[0:4]
            )
        out[n, 0:4] = -total
        out[n, 4:8] = jnp.zeros((4, 256), F32)


def pack_two(res, low, high):
    def body(c, carry):
        for n in range(2):
            low[c, 8 * n : 8 * n + 8] = pack_low(lambda i: res[c, i, 8 * n : 8 * n + 8])
            high[c, 8 * n : 8 * n + 8] = pack_high(
                lambda i: res[c, i, 48 + 8 * n : 56 + 8 * n]
            )
        return carry

    lax.fori_loop(0, 3, body, 0)


def project_kernel(
    field, tlo, thi, hz_low, hz_high, lanes, fine, back, stiff, wjk, u, res, low, high, *scratch
):
    hz = lanes[7:8, :128]
    inner = 1.0 / hz
    first = 1.0 / (hz + hz_low[192:193])
    final = 1.0 / (hz + hz_high[192:193])
    k = iota((8, 128), 0)
    rk = jnp.where(
        k == 0, lanes[9:10, :128], jnp.where(k == 7, lanes[10:11, :128], lanes[8:9, :128])
    )
    rk = rk * keep_rows(8)
    by_plane = {0: rk * first, 7: rk * final}
    middle = rk * inner

    def around(c, carry):
        lo, hi = tlo[c], thi[c]
        for i in range(8):
            x = field[c, i]
            first, last = x[0:8], x[56:64]
            u[c, i] = x
            u[c, i, 0:8] = first + from_low(last, lo, i)
            u[c, i, 56:64] = last + from_high(first, hi, i)
        return carry

    def across(c, carry):
        for i in range(8):
            x = u[c, i]
            for j in range(8):
                v = x[8 * j : 8 * j + 8]
                f = by_plane.get(i, middle)
                f = 0.5 * f if j in (0, 7) else f
                below, above = radial_parts(v)
                u[c, i, 8 * j : 8 * j + 8] = radial_sum(v, below, above) * f
        return carry

    lax.fori_loop(0, 3, around, 0)
    lax.fori_loop(0, 3, across, 0)
    residual(u, lanes, fine, back, stiff, wjk, res, *scratch)
    pack_two(res, low, high)


def step_length(sums):
    total = jnp.sum(sums[...], axis=0, keepdims=True)
    return total[:, 0:1] / total[:, 1:2]


def advance_kernel(u_old, d, sums, lanes, fine, back, stiff, wjk, u, res, low, high, *scratch):
    alpha = step_length(sums)

    def body(t, carry):
        c, i = t // 8, t % 8
        u[c, i] = u_old[c, i] + alpha * d[c, i]
        return carry

    lax.fori_loop(0, 24, body, 0)
    residual(u, lanes, fine, back, stiff, wjk, res, *scratch)
    pack_two(res, low, high)


def around_widen_kernel(res, tlo, thi, out, down, up):
    lane = iota((8, 128), 1)

    def body(c, carry):
        lo6, lo7, hi0, hi1 = tlo[c, 0:8], tlo[c, 8:16], thi[c, 0:8], thi[c, 8:16]
        for i in range(8):
            x = res[c, i]
            first, last = x[0:8], x[56:64]
            out[c, i, 0:64] = x
            out[c, i, 0:8] = first + from_low(last, lo7, i)
            out[c, i, 56:64] = last + from_high(first, hi0, i)
            out[c, i, 64:72] = jnp.where(
                lane < 64, lanes_by(lo6, -16 * i), lanes_by(hi1, 112 - 16 * i)
            )
        for n in range(2):
            down[c, n] = out[c, n]
            up[c, n] = out[c, 6 + n]
        return carry

    lax.fori_loop(0, 3, body, 0)


def widen_planes(e, xf, half):
    lane, k = iota((8, 128), 1), iota((8, 128), 0)
    extra = e[64:72]
    planes = [e[8 * j : 8 * j + 8] for j in range(8)]
    under = jnp.where(lane < 16, extra, lanes_by(planes[6], 16))
    over = jnp.where(lane >= 112, extra, lanes_by(planes[1], -16))
    cols = slice(half * 128, half * 128 + 128)
    for j, v in enumerate([under] + planes + [over]):
        below, above = radial_parts(v)
        own = radial_sum(v, below, above)
        side = jnp.where(k == 0, rows_by(below, 2), jnp.where(k == 1, above, 0.0))
        hi, lo = split(jnp.concatenate([own, side], axis=0))
        xf[16 * j : 16 * j + 16, cols] = hi
        xf[160 + 16 * j : 176 + 16 * j, cols] = hi
        xf[320 + 16 * j : 336 + 16 * j, cols] = lo


def transform_kernel(field, forward, vectors, out, xf0, xf1, yf):
    def body(c, carry):
        for p in range(4):
            buf = (xf0, xf1)[p % 2]
            for half in range(2):
                widen_planes(field[c, 2 * p + half], buf, half)
            y = dot(forward[...], buf[...])
            yf[c, 2 * p] = y[:, :128]
            yf[c, 2 * p + 1] = y[:, 128:]
        return carry

    lax.fori_loop(0, 3, body, 0)

    def mid(rb, carry):
        rows = pl.ds(pl.multiple_of(rb * 16, 16), 16)
        y = [[yf[c, i, rows] for i in range(8)] for c in range(3)]
        for a in range(10):
            acc = [vectors[1, a] * y[c][0] for c in range(3)]
            for i in range(1, 8):
                s = vectors[i + 1, a]
                acc = [acc[c] + s * y[c][i] for c in range(3)]
            for c in range(3):
                out[c, a, rows] = acc[c]
        return carry

    lax.fori_loop(0, 7, mid, 0)


def solve_kernel(
    own, zlo, zhi, vectors, forward, inverse, scale, corr, low, high, xf0, xf1, yf, xb
):
    for c in range(3):
        for n, (buf, halo) in enumerate(((xf0, zlo), (xf1, zhi))):
            widen_planes(halo[c, 0], buf.at[c], 0)
            widen_planes(halo[c, 1], buf.at[c], 1)
            y = dot(forward[...], buf[c])
            yf[c, 2 * n] = y[:, :128]
            yf[c, 2 * n + 1] = y[:, 128:]

    def mid(rb, carry):
        rows = pl.ds(pl.multiple_of(rb * 16, 16), 16)
        y = [[yf[c, i, rows] for i in range(4)] for c in range(3)]
        spec = []
        for a in range(10):
            acc = [own[c, a, rows] for c in range(3)]
            for n, i in enumerate((0, 1, 8, 9)):
                s = vectors[i, a]
                acc = [acc[c] + s * y[c][n] for c in range(3)]
            f = scale[a, rows]
            spec.append([acc[c] * f for c in range(3)])
        for i in range(8):
            acc = [vectors[i + 1, 0] * spec[0][c] for c in range(3)]
            for a in range(1, 10):
                s = vectors[i + 1, a]
                acc = [acc[c] + s * spec[a][c] for c in range(3)]
            cols = slice((i % 2) * 128, (i % 2) * 128 + 128)
            for c in range(3):
                hi, lo = split(acc[c])
                for term, part in enumerate((hi, hi, lo)):
                    xb[c * 4 + i // 2, pl.ds(pl.multiple_of(term * 112 + rb * 16, 16), 16),
                       cols] = part
        return carry

    lax.fori_loop(0, 7, mid, 0)

    k = iota((8, 128), 0)
    r = iota((8, 128), 1) & (RADIAL - 1)
    inner = ((k == 0) & (r > 0)) | ((k == 7) & (r < RADIAL - 1))
    share = jnp.where(inner, 0.5, 1.0).astype(F32)
    for t in range(12):
        c, p = t // 4, t % 4
        y = dot(inverse[...], xb[t])
        for half in range(2):
            i = 2 * p + half
            for j in range(8):
                f = (0.5 if i in (0, 7) else 1.0) * (0.5 if j in (0, 7) else 1.0)
                corr[c, i, 8 * j : 8 * j + 8] = (
                    y[8 * j : 8 * j + 8, half * 128 : half * 128 + 128] * (share * f)
                )

    def last(c, carry):
        low[c] = pack_low(lambda i: corr[c, i, 0:8])
        high[c] = pack_high(lambda i: corr[c, i, 56:64])
        return carry

    lax.fori_loop(0, 3, last, 0)


def direction_kernel(field, zlo, zhi, res, lanes, grad, wjk, d, sums, xs, acc):
    keep = keep_rows(8)
    finish_sum(field, zlo, zhi, d, lambda i, j: keep)
    acc[...] = jnp.zeros_like(acc)
    vol = lanes[0:1, :128]
    kz, kt, kr = lanes[4:5, :128], lanes[5:6, :128], lanes[6:7, :128]

    def first(t, carry):
        c, rb = t // 4, t % 4
        rows = pl.ds(pl.multiple_of(rb * 16, 16), 16)
        x = [d[c, i, rows] for i in range(8)]
        num = sum(x[i] * res[c, i, rows] for i in range(8))
        sq = sum(float(W[i]) * (x[i] * x[i]) for i in range(8))
        gz = sum(float(W[i]) * (g * g) for i, g in enumerate(even_odd(D, x, -1)))
        acc[0] += num
        acc[1] += wjk[rows] * (SIGMA * vol * sq + kz * gz)
        for i in range(8):
            hi, lo = split(x[i])
            for term, part in enumerate((hi, hi, lo, lo)):
                xs[c * 4 + i // 2, pl.ds(pl.multiple_of(term * 64 + rb * 16, 16), 16),
                   (i % 2) * 128 : (i % 2) * 128 + 128] = part
        return carry

    lax.fori_loop(0, 12, first, 0)

    total = acc[1]
    for t in range(12):
        y = dot(grad[...], xs[t])
        for half in range(2):
            v = y[:, half * 128 : half * 128 + 128]
            v = v * v
            plane = jnp.zeros((16, 128), F32)
            for q in range(4):
                rows = slice(16 * q, 16 * q + 16)
                plane = plane + wjk[rows] * (kt * v[rows] + kr * v[64 + 16 * q : 80 + 16 * q])
            total = total + float(W[2 * (t % 4) + half]) * plane
    acc[1] = total
    num = jnp.sum(jnp.sum(acc[0], axis=0, keepdims=True), axis=1, keepdims=True)
    den = jnp.sum(jnp.sum(acc[1], axis=0, keepdims=True), axis=1, keepdims=True)
    at = iota((128, 128), 1)
    sums[...] = jnp.where(at == 0, num, jnp.where(at == 1, den, 0.0))


def route_kernel(slot, corner, right, owner):
    hot = (slot[...] == iota((128, 128), 0)).astype(F32)
    nt = (((1,), (1,)), ((), ()))
    ids = corner[...].astype(F32)
    by_elem = lax.dot_general(hot, ids, nt, precision=EXACT, preferred_element_type=F32)
    by_corner = lax.dot_general(ids, hot, nt, precision=EXACT, preferred_element_type=F32)
    owner[...] = (by_corner + 0.5).astype(jnp.int32) // 136
    ids = (by_elem + 0.5).astype(jnp.int32)
    inside = ids - ids // 136 * 136
    pos = iota((128, 256), 1)
    for q in range(8):
        right[128 * q : 128 * q + 128] = (inside[:, q : q + 1] == pos).astype(F32).astype(BF16)


def placed(values, right, owner, left):
    dev = iota((128, 128), 0)
    for c, both in enumerate(values):
        hi = both.astype(BF16).astype(F32)
        for q in range(8):
            mine = owner[q : q + 1] == dev
            cols = slice((q // 4) * 128, (q // 4) * 128 + 128)
            for m, piece in enumerate((hi, both - hi)):
                at = (2 * c + m) * 128
                left[at : at + 128, 128 * q : 128 * q + 128] = jnp.where(
                    mine, piece[q % 4 : q % 4 + 1, cols], 0.0
                ).astype(BF16)
    y = dot(left[...], right[...])
    return [y[256 * c : 256 * c + 128] + y[256 * c + 128 : 256 * c + 256] for c in range(3)]


def place_base_kernel(base, right, owner, out, left):
    for c, total in enumerate(placed([base[c] for c in range(3)], right, owner, left)):
        out[c] = lanes_by(total, 8 * c)


def place_kernel(base, change, right, owner, part, dense, left0, left1):
    blocks = [base[c] for c in range(3)]
    for n, left in enumerate((left0, left1)):
        values = [change[3 * n + c] for c in range(3)]
        for c, total in enumerate(placed(values, right, owner, left)):
            blocks.append(lanes_by(total, 8 * (3 * n + 3 + c)))
    spill = None
    for n, total in enumerate(blocks):
        first = total[:, :128]
        dense[pl.ds(n, 128, stride=10)] = first if spill is None else first + spill
        spill = total[:, 128:]
    dense[pl.ds(9, 128, stride=10)] = spill + lanes_by(part[...], 72)


def store_kernel(u, d, slot, u_hbm, d_hbm, u_out, d_out, sems):
    hot = (slot[...] == iota((128, 128), 0)).astype(F32)
    copies = []
    for c in range(3):
        for n, (x, y, out) in enumerate(((u, u_out, u_hbm), (d, d_out, d_hbm))):
            flat = x[c].reshape(512, 128)
            y[c] = jnp.dot(flat, hot, precision=EXACT, preferred_element_type=F32).reshape(
                8, 64, 128
            )
            copies.append(pltpu.make_async_copy(y.at[c], out.at[c], sems.at[2 * c + n]))
            copies[-1].start()
    for copy in copies:
        copy.wait()


def end_kernel(u_hbm, d_hbm, parts, vel_hbm, coarse_hbm, u, d, vel, coarse, sems):
    last = pltpu.make_async_copy(coarse, coarse_hbm, sems.at[0])
    loads = [
        [
            pltpu.make_async_copy(a.at[c], b.at[c], sems.at[1 + 2 * c + n])
            for n, (a, b) in enumerate(((u_hbm, u), (d_hbm, d)))
        ]
        for c in range(3)
    ]
    stores = [
        pltpu.make_async_copy(vel.at[c], vel_hbm.at[c], sems.at[7 + c]) for c in range(3)
    ]
    for pair in loads:
        for copy in pair:
            copy.start()
    sums = [
        jnp.sum(parts[pl.ds(n, 128, stride=10)], axis=0, keepdims=True) for n in range(10)
    ]
    alpha = sums[9][:, 72:73] / sums[9][:, 73:74]
    for c in range(3):
        for copy in loads[c]:
            copy.wait()
        vel[c] = u[c] + alpha * d[c]
        stores[c].start()
    total = jnp.concatenate(sums, axis=1)
    one, two = lanes_by(total, -408), lanes_by(total, -816)
    both = total + alpha * (one + alpha * two)
    for c in range(3):
        coarse[c : c + 1] = lanes_by(both, -136 * c)[:, :136]
    last.start()
    for copy in (*stores, last):
        copy.wait()


FIELD = (3, 8, 64, 128)


def both_ways(axis, to_next, to_prev):
    n = lax.axis_size(axis)
    up = [(i, (i + 1) % n) for i in range(n)]
    down = [((i + 1) % n, i) for i in range(n)]
    return lax.ppermute(to_next, axis, up), lax.ppermute(to_prev, axis, down)


def fine_scratch():
    return [
        pltpu.VMEM((6, 3, 432, 256), F32),
        pltpu.VMEM((6, 3, 144, 256), F32),
        pltpu.VMEM((18, 256, 256), BF16),
        pltpu.VMEM((18, 256, 256), BF16),
    ]


def local_scratch(count):
    return [
        pltpu.VMEM((12, 256, 256), BF16),
        pltpu.VMEM((count, 432, 256), BF16),
        pltpu.VMEM((count, 432, 256), BF16),
        pltpu.VMEM((count, 12, 64, 128), F32),
        pltpu.VMEM(FIELD, F32),
        pltpu.VMEM((3, 8, 128, 128), F32),
    ]


def shards(vel, slot, corner, axial, arc, rad, vectors, values):
    smem, hbm = pltpu.SMEM, pltpu.HBM
    small = ((3, 8, 128), F32)
    count = len(CONSTANTS)
    vel = vel.reshape(FIELD)
    down, up, lanes = call(
        faces_kernel,
        [((200, 128), F32), ((200, 128), F32), ((16, 256), F32)],
        (vel, slot, arc, rad, axial),
        [
            pltpu.VMEM((2, 3, 64, 128), F32),
            pltpu.VMEM((1, 128), jnp.int32),
            pltpu.SMEM((RADIAL,), F32),
            pltpu.SMEM((RADIAL,), F32),
            pltpu.SemaphoreType.DMA((9,)),
        ],
        spaces={0: hbm, 1: hbm, 2: hbm, 3: hbm, 4: smem},
    )
    zlo, zhi = both_ways("wide", up, down)
    mv, fine, back, stiff, grad, coarse_jk, wjk = call(
        inner_kernel,
        [((3, 6, 64, 128), F32)] + [(m.shape, m.dtype) for m in CONSTANTS],
        (vel, slot, lanes, *(jnp.asarray(m) for m in CONSTANTS)),
        [
            pltpu.VMEM((3, 6, 64, 128), F32),
            pltpu.VMEM((1, 128), jnp.int32),
            pltpu.SemaphoreType.DMA((4 + count,)),
        ],
        spaces={0: hbm, 1: hbm, **{3 + i: hbm for i in range(count)}},
    )
    zlo, zhi, mv, fine, back, stiff, grad, coarse_jk, wjk = lax.optimization_barrier(
        (zlo, zhi, mv, fine, back, stiff, grad, coarse_jk, wjk)
    )
    field, low, high = call(
        pipe_sum_kernel, [(FIELD, F32), small, small], (mv, down, up, zlo, zhi)
    )
    forward, inverse, scale = call(
        solve_tables_kernel,
        [((112, 480), BF16), ((64, 336), BF16), ((10, 112, 128), F32)],
        (vectors, values[None], lanes),
        [
            pltpu.VMEM((10, 10), F32),
            pltpu.VMEM((1, 10), F32),
            pltpu.SemaphoreType.DMA((2,)),
        ],
        spaces={0: hbm, 1: hbm},
    )

    def sum_rounds(field, low, high, beside=()):
        tlo, thi = both_ways("narrow", high, low)
        out, down, up = call(
            around_sum_kernel,
            [(FIELD, F32), ((200, 128), F32), ((200, 128), F32)],
            (field, tlo, thi, lanes),
        )
        zlo, zhi = both_ways("wide", up, down)
        zlo, zhi, beside = lax.optimization_barrier((zlo, zhi, beside))
        return (out, zlo, zhi), beside

    local = (lanes, fine, back, stiff, wjk)
    packs = [(FIELD, F32), (FIELD, F32), ((3, 16, 128), F32), ((3, 16, 128), F32)]
    u, res, low, high = call(
        project_kernel,
        packs,
        (field, *both_ways("narrow", high, low), zlo, zhi, *local),
        fine_scratch() + local_scratch(3),
    )
    for step in range(2):
        if step > 0:
            sums = lax.all_to_all(part, BOTH, 0, 0, tiled=True)
            u, res, low, high = call(
                advance_kernel, packs, (u, d, sums, *local), fine_scratch() + local_scratch(3)
            )
        tlo, thi = both_ways("narrow", high, low)
        wide_field, down, up = call(
            around_widen_kernel,
            [((3, 8, 72, 128), F32), ((3, 2, 72, 128), F32), ((3, 2, 72, 128), F32)],
            (res, tlo, thi),
        )
        zlo, zhi = both_ways("wide", up, down)
        (own,) = call(
            transform_kernel,
            [((3, 10, 112, 128), F32)],
            (wide_field, forward, vectors),
            [
                pltpu.VMEM((480, 256), BF16),
                pltpu.VMEM((480, 256), BF16),
                pltpu.VMEM((3, 8, 112, 128), F32),
            ],
            spaces={2: smem},
        )
        zlo, zhi, own = lax.optimization_barrier((zlo, zhi, own))
        corr, low, high = call(
            solve_kernel,
            [(FIELD, F32), small, small],
            (own, zlo, zhi, vectors, forward, inverse, scale),
            [
                pltpu.VMEM((3, 480, 256), BF16),
                pltpu.VMEM((3, 480, 256), BF16),
                pltpu.VMEM((3, 4, 112, 128), F32),
                pltpu.VMEM((12, 336, 256), BF16),
            ],
            spaces={3: smem},
        )
        beside = ()
        if step == 1:
            fields = [((6, 3, 432, 256), F32), ((6, 3, 144, 256), F32)]
            right, owner = call(
                route_kernel,
                [((1024, 256), BF16), ((8, 128), jnp.int32)],
                (slot, corner),
                free=True,
            )
            (base,) = call(corners_kernel, [((3, 8, 256), F32)], (res,))
            (base,) = call(
                place_base_kernel,
                [((3, 128, 256), F32)],
                (base, right, owner),
                [pltpu.VMEM((768, 1024), BF16)],
            )
            beside = (call(fields_kernel, fields, (u, fine), fine_scratch()[2:]), base)
        halo, beside = sum_rounds(corr, low, high, beside)
        d, part = call(
            direction_kernel,
            [(FIELD, F32), ((128, 128), F32)],
            (*halo, res, lanes, grad, wjk),
            [pltpu.VMEM((12, 256, 256), BF16), pltpu.VMEM((2, 16, 128), F32)],
        )
    (pf, qf), base = beside
    (change,) = call(
        change_kernel,
        [((6, 8, 256), F32)],
        (d, pf, qf, lanes, fine, stiff, wjk, coarse_jk),
        fine_scratch()
        + [
            pltpu.VMEM((3, 256, 256), BF16),
            pltpu.VMEM((6, 144, 256), F32),
            pltpu.VMEM((6, 432, 256), BF16),
            pltpu.VMEM((3, 2, 64, 128), F32),
        ],
    )
    (dense,) = call(
        place_kernel,
        [((1280, 128), F32)],
        (base, change, right, owner, part),
        [pltpu.VMEM((768, 1024), BF16), pltpu.VMEM((768, 1024), BF16)],
    )
    parts = lax.all_to_all(dense.reshape(128, 1, 1280), BOTH, 0, 0, tiled=True)
    parts = parts.reshape(1280, 128)
    u, d = call(
        store_kernel,
        [(FIELD, F32), (FIELD, F32)],
        (u, d, slot),
        [pltpu.VMEM(FIELD, F32), pltpu.VMEM(FIELD, F32), pltpu.SemaphoreType.DMA((6,))],
        hbm_out={0, 1},
        free=True,
    )
    out, coarse = call(
        end_kernel,
        [(FIELD, F32), ((3, 136), F32)],
        (u, d, parts),
        [
            pltpu.VMEM(FIELD, F32),
            pltpu.VMEM(FIELD, F32),
            pltpu.VMEM(FIELD, F32),
            pltpu.VMEM((3, 136), F32),
            pltpu.SemaphoreType.DMA((10,)),
        ],
        spaces={0: pltpu.HBM, 1: pltpu.HBM},
        hbm_out={0, 1},
    )
    return out.reshape(3, 512, 128), coarse


def solution(mesh):
    return jax.shard_map(
        shards,
        mesh=mesh,
        in_specs=(P(None, None, BOTH), P(BOTH, None), P(None, BOTH), P("wide"), P(), P(), P(), P()),
        out_specs=(P(None, None, BOTH), P(None, BOTH)),
        check_vma=False,
    )
```

```python
from functools import partial

import jax
import jax.numpy as jnp
import ml_dtypes
import numpy as np
from jax import lax
from jax.experimental import pallas as pl
from jax.experimental.pallas import tpu as pltpu
from jax.sharding import PartitionSpec as P

RADIAL = 16
SIGMA = 4.0
VISCOSITY = 0.05
F32 = jnp.float32
BF16 = jnp.bfloat16
EXACT = lax.Precision.HIGHEST
BOTH = ("wide", "narrow")


def node_tables():
    x = np.array(
        [-1.0, -0.8717401485096066, -0.5917001814331423, -0.2092992179024789]
    )
    x = np.concatenate([x, -x[::-1]])
    w = np.array([1.0 / 28.0, 0.2107042271435061, 0.3411226924835044, 0.4124587946587038])
    w = np.concatenate([w, w[::-1]])
    scale = np.array([np.prod([x[t] - x[p] for p in range(8) if p != t]) for t in range(8)])
    deriv = np.zeros((8, 8))
    for t in range(8):
        for s in range(8):
            if t != s:
                deriv[t, s] = scale[t] / (scale[s] * (x[t] - x[s]))
        deriv[t, t] = -np.sum(deriv[t])
    y = np.array(
        [
            -0.9815606342467192,
            -0.9041172563704749,
            -0.7699026741943047,
            -0.5873179542866175,
            -0.3678314989981802,
            -0.1252334085114689,
        ]
    )
    y = np.concatenate([y, -y[::-1]])
    v = np.array(
        [
            0.0471753363865118,
            0.1069393259953184,
            0.1600783285433462,
            0.2031674267230659,
            0.2334925365383548,
            0.2491470458134028,
        ]
    )
    v = np.concatenate([v, v[::-1]])
    interp = np.ones((12, 8))
    for s in range(8):
        for p in range(8):
            if p != s:
                interp[:, s] = interp[:, s] * (y - x[p]) / (x[s] - x[p])
    linear = np.stack([(1.0 - x) / 2.0, (1.0 + x) / 2.0])
    return w, deriv, v, interp, linear


W, D, VF, J, LIN = node_tables()
B = J @ D
JV = J.T * VF[None, :]
STIFF = D.T @ (W[:, None] * D)
WJK = np.kron(W, W)


WJK_ROWS = np.broadcast_to(WJK[:, None], (64, 128)).astype(np.float32)


def two_parts(matrix):
    hi = matrix.astype(np.float32).astype(ml_dtypes.bfloat16)
    lo = (matrix - hi.astype(np.float64)).astype(ml_dtypes.bfloat16)
    return hi, lo


def four_terms(matrix):
    hi, lo = two_parts(matrix)
    return np.concatenate([hi, lo, hi, lo], axis=1)


def three_terms(matrix):
    hi, lo = two_parts(matrix)
    return np.concatenate([hi, lo, hi], axis=1)


FINE = four_terms(np.concatenate([np.kron(J, J), np.kron(B, J), np.kron(J, B)]))
BACK = three_terms(np.kron(JV, JV))
STIFF_JK = four_terms(
    np.concatenate([np.kron(STIFF, np.diag(W)), np.kron(np.diag(W), STIFF)])
)
COARSE_Z = LIN @ JV
COARSE_JK = three_terms(
    np.concatenate(
        [
            np.kron(COARSE_Z, COARSE_Z),
            np.kron(COARSE_Z, np.stack([JV[0], JV[7]])),
            np.zeros((8, 144)),
        ]
    )
)
GRAD_JK = four_terms(np.concatenate([np.kron(D, np.eye(8)), np.kron(np.eye(8), D)]))


def call(kernel, outs, args, scratch=(), spaces=None, hbm_out=(), free=False):
    spaces = spaces or {}
    args = [
        a if free and i not in spaces
        else pltpu.with_memory_space_constraint(a, spaces.get(i, pltpu.VMEM))
        for i, a in enumerate(args)
    ]
    return pl.pallas_call(
        kernel,
        out_shape=[
            (pltpu.HBM if i in hbm_out else pltpu.VMEM)(s, d)
            for i, (s, d) in enumerate(outs)
        ],
        in_specs=[
            pl.BlockSpec(memory_space=spaces.get(i, pltpu.VMEM)) for i in range(len(args))
        ],
        out_specs=[
            pl.BlockSpec(memory_space=pltpu.HBM if i in hbm_out else pltpu.VMEM)
            for i in range(len(outs))
        ],
        scratch_shapes=list(scratch),
        compiler_params=pltpu.CompilerParams(vmem_limit_bytes=32 << 20),
        name=kernel.func.__name__ if isinstance(kernel, partial) else kernel.__name__,
    )(*args)


def iota(shape, dim):
    return lax.broadcasted_iota(jnp.int32, shape, dim)


def lanes_by(x, shift):
    return pltpu.roll(x, shift % x.shape[-1], x.ndim - 1)


def rows_by(x, shift):
    return pltpu.roll(x, shift % 8, x.ndim - 2)


def split(x):
    hi = x.astype(BF16)
    return hi, (x - hi.astype(F32)).astype(BF16)


def dot(a, b):
    return jnp.dot(a, b, preferred_element_type=F32)


def even_odd(matrix, xs, sign):
    n_out, n_in = matrix.shape
    half = n_in // 2
    even = [xs[i] + xs[n_in - 1 - i] for i in range(half)]
    odd = [xs[i] - xs[n_in - 1 - i] for i in range(half)]
    outs = [None] * n_out
    for a in range(n_out // 2):
        e = sum(
            float((matrix[a, i] + matrix[a, n_in - 1 - i]) / 2) * even[i] for i in range(half)
        )
        o = sum(
            float((matrix[a, i] - matrix[a, n_in - 1 - i]) / 2) * odd[i] for i in range(half)
        )
        outs[a] = e + o
        outs[n_out - 1 - a] = e - o if sign > 0 else o - e
    return outs


def keep_rows(rows):
    k = iota((rows, 128), 0) & 7
    r = iota((rows, 128), 1) & (RADIAL - 1)
    wall = ((k == 0) & (r == 0)) | ((k == 7) & (r == RADIAL - 1))
    return jnp.where(wall, 0.0, 1.0).astype(F32)


def radial_parts(x):
    r = iota((8, 128), 1) & (RADIAL - 1)
    below = jnp.where(r > 0, lanes_by(x, 1), 0.0)
    above = jnp.where(r < RADIAL - 1, lanes_by(x, -1), 0.0)
    return below, above


def radial_sum(x, below, above):
    k = iota((8, 128), 0)
    return x + jnp.where(k == 0, rows_by(below, 1), jnp.where(k == 7, rows_by(above, -1), 0.0))


def pack_low(plane_of):
    et = iota((8, 128), 1) >> 4
    out = jnp.zeros((8, 128), F32)
    for i in range(8):
        out = jnp.where(et == i, lanes_by(plane_of(i), 16 * i), out)
    return out


def pack_high(plane_of):
    et = iota((8, 128), 1) >> 4
    out = jnp.zeros((8, 128), F32)
    for i in range(8):
        out = jnp.where(et == i, lanes_by(plane_of(i), 16 * i + 16), out)
    return out


def from_low(plane, packed, i):
    lane = iota((8, 128), 1)
    return jnp.where(lane < 16, lanes_by(packed, -16 * i), lanes_by(plane, 16))


def from_high(plane, packed, i):
    lane = iota((8, 128), 1)
    return jnp.where(lane >= 112, lanes_by(packed, 112 - 16 * i), lanes_by(plane, -16))


CONSTANTS = (FINE, BACK, STIFF_JK, GRAD_JK, COARSE_JK, WJK_ROWS)
NT = (((1,), (1,)), ((), ()))


def faces_kernel(
    vel_hbm, slot_hbm, arc_hbm, rad_hbm, axial, down, up, lanes, vel, slot, arc, rad, sems
):
    copies = [
        pltpu.make_async_copy(arc_hbm, arc, sems.at[7]),
        pltpu.make_async_copy(rad_hbm, rad, sems.at[8]),
        pltpu.make_async_copy(slot_hbm, slot, sems.at[6]),
    ]
    for c in range(3):
        for n in range(2):
            copies.append(
                pltpu.make_async_copy(vel_hbm.at[c, 7 * n], vel.at[n, c], sems.at[3 * n + c])
            )
    for copy in copies:
        copy.start()
    for copy in copies[:2]:
        copy.wait()
    r = iota((1, 256), 1) & (RADIAL - 1)
    ht, hr = jnp.zeros((1, 256), F32), jnp.zeros((1, 256), F32)
    for i in range(RADIAL):
        ht = jnp.where(r == i, arc[i], ht)
        hr = jnp.where(r == i, rad[i], hr)
    hz = jnp.zeros((1, 256), F32) + axial[0]
    g = ht * hr / 8.0
    vol = hz * g
    g_low = g + jnp.where(r > 0, lanes_by(g, 1), 0.0)
    g_high = g + jnp.where(r < RADIAL - 1, lanes_by(g, -1), 0.0)
    rows = [
        vol,
        vol * (2.0 / hz),
        vol * (2.0 / ht),
        vol * (2.0 / hr),
        VISCOSITY * vol * (2.0 / hz) * (2.0 / hz),
        VISCOSITY * vol * (2.0 / ht) * (2.0 / ht),
        VISCOSITY * vol * (2.0 / hr) * (2.0 / hr),
        hz,
        1.0 / g,
        1.0 / g_low,
        1.0 / g_high,
    ]
    for n, row in enumerate(rows):
        lanes[n : n + 1] = row
    for n in range(len(rows), 16):
        lanes[n : n + 1] = jnp.zeros((1, 256), F32)
    for copy in copies[2:]:
        copy.wait()
    hot = (slot[...] == iota((128, 128), 0)).astype(F32)
    y = lax.dot_general(
        vel[...].reshape(384, 128), hot, NT, precision=EXACT, preferred_element_type=F32
    )
    y = y * vol[:, :128]
    for n, out in enumerate((down, up)):
        out[0:192] = y[192 * n : 192 * n + 192]
        out[192:200] = jnp.broadcast_to(hz[:, :128], (8, 128))


def inner_kernel(vel_hbm, slot_hbm, lanes, *refs):
    n = len(CONSTANTS)
    hbm, mv, held, (vel, slot, sems) = refs[:n], refs[n], refs[n + 1 : 2 * n + 1], refs[2 * n + 1 :]
    pairs = [(slot_hbm, slot)]
    pairs += [(vel_hbm.at[c, pl.ds(1, 6)], vel.at[c]) for c in range(3)]
    pairs += list(zip(hbm, held))
    copies = [pltpu.make_async_copy(a, b, sems.at[i]) for i, (a, b) in enumerate(pairs)]
    for copy in copies:
        copy.start()
    copies[0].wait()
    hot = (slot[...] == iota((128, 128), 0)).astype(F32)
    for c in range(3):
        copies[1 + c].wait()
        y = lax.dot_general(
            vel[c].reshape(384, 128), hot, NT, precision=EXACT, preferred_element_type=F32
        )
        mv[c] = (y * lanes[0:1, :128]).reshape(6, 64, 128)
    for copy in copies[4:]:
        copy.wait()


def pipe_sum_kernel(mv, down, up, zlo, zhi, field, low, high):
    def body(c, carry):
        rows = pl.ds(pl.multiple_of(c * 64, 64), 64)
        field[c, 0] = down[rows] + zlo[rows]
        for i in range(6):
            field[c, 1 + i] = mv[c, i]
        field[c, 7] = up[rows] + zhi[rows]
        low[c] = pack_low(lambda i: field[c, i, 0:8])
        high[c] = pack_high(lambda i: field[c, i, 56:64])
        return carry

    lax.fori_loop(0, 3, body, 0)


def solve_tables_kernel(
    vectors_hbm, values_hbm, lanes, forward, inverse, scale, vectors, values, sems
):
    copies = [
        pltpu.make_async_copy(vectors_hbm, vectors, sems.at[0]),
        pltpu.make_async_copy(values_hbm, values, sems.at[1]),
    ]
    for copy in copies:
        copy.start()
    for copy in copies:
        copy.wait()
    s = vectors[...]
    ident = (iota((10, 10), 0) == iota((10, 10), 1)).astype(F32)
    st = lax.dot_general(
        ident, s, (((1,), (1,)), ((), ())), precision=EXACT, preferred_element_type=F32
    )

    def mul(a, b):
        return jnp.dot(a, b, precision=EXACT, preferred_element_type=F32)

    row, col = iota((112, 10), 0), iota((112, 10), 1)
    live = row < 100
    by_b = ((row // 10 == col) & live).astype(F32)
    by_c = ((row % 10 == col) & live).astype(F32)
    node, pos = iota((10, 160), 0), iota((10, 160), 1)
    slot = pos & 15
    k_of = jnp.where(slot < 8, slot + 1, jnp.where(slot == 8, 0, jnp.where(slot == 9, 9, -1)))
    by_j = (node == (pos >> 4)).astype(F32)
    by_k = (node == k_of).astype(F32)
    full = mul(mul(by_b, st), by_j) * mul(mul(by_c, st), by_k)
    hi, lo = split(full)
    forward[:, 0:160] = hi
    forward[:, 160:320] = lo
    forward[:, 320:480] = hi

    row8, col8 = iota((64, 10), 0), iota((64, 10), 1)
    by_j8 = ((row8 >> 3) + 1 == col8).astype(F32)
    by_k8 = ((row8 & 7) + 1 == col8).astype(F32)
    node2, pos2 = iota((10, 112), 0), iota((10, 112), 1)
    b_of = jnp.where(pos2 < 100, pos2 // 10, -1)
    c_of = jnp.where(pos2 < 100, pos2 % 10, -1)
    to_b = (node2 == b_of).astype(F32)
    to_c = (node2 == c_of).astype(F32)
    full = mul(mul(by_j8, s), to_b) * mul(mul(by_k8, s), to_c)
    hi, lo = split(full)
    inverse[:, 0:112] = hi
    inverse[:, 112:224] = lo
    inverse[:, 224:336] = hi

    lam = jnp.broadcast_to(values[...], (8, 10))
    nt = (((1,), (1,)), ((), ()))
    lam_b = lax.dot_general(by_b, lam, nt, precision=EXACT, preferred_element_type=F32)[:, 0:1]
    lam_c = lax.dot_general(by_c, lam, nt, precision=EXACT, preferred_element_type=F32)[:, 0:1]
    vol = lanes[0:1, :128]
    flat = (
        SIGMA * vol
        + lam_b * jnp.broadcast_to(lanes[5:6, :128], (112, 128))
        + lam_c * jnp.broadcast_to(lanes[6:7, :128], (112, 128))
    )
    for a in range(10):
        scale[a] = 1.0 / (flat + values[0:1, a : a + 1] * lanes[4:5, :128])


def around_sum_kernel(field, tlo, thi, lanes, out, down, up):
    def body(c, carry):
        lo, hi = tlo[c], thi[c]
        for i in range(8):
            x = field[c, i]
            first, last = x[0:8], x[56:64]
            head = first + from_low(last, lo, i)
            tail = last + from_high(first, hi, i)
            out[c, i] = x
            out[c, i, 0:8] = head
            out[c, i, 56:64] = tail
        base = pl.multiple_of(c * 64, 64)
        down[pl.ds(base, 64)] = out[c, 0]
        up[pl.ds(base, 64)] = out[c, 7]
        return carry

    lax.fori_loop(0, 3, body, 0)
    hz = jnp.broadcast_to(lanes[7:8, :128], (8, 128))
    down[192:200] = hz
    up[192:200] = hz


def finish_sum(field, zlo, zhi, out, factor):
    def body(c, carry):
        base = pl.multiple_of(c * 64, 64)
        for i in range(8):
            x = field[c, i]
            if i == 0:
                x = x + zlo[pl.ds(base, 64)]
            if i == 7:
                x = x + zhi[pl.ds(base, 64)]
            for j in range(8):
                v = x[8 * j : 8 * j + 8]
                below, above = radial_parts(v)
                out[c, i, 8 * j : 8 * j + 8] = radial_sum(v, below, above) * factor(i, j)
        return carry

    lax.fori_loop(0, 3, body, 0)


def put(ref, at, rb, half, x):
    hi, lo = split(x)
    for term, part in enumerate((hi, hi, lo, lo)):
        start = term * 64 + rb * 16
        rows = pl.ds(start if isinstance(start, int) else pl.multiple_of(start, 16), 16)
        ref[at, rows, half * 128 : half * 128 + 128] = part


def along_pipe(u, c, rb, xu, xw):
    rows = pl.ds(rb * 16 if isinstance(rb, int) else pl.multiple_of(rb * 16, 16), 16)
    x = [u[c, i, rows] for i in range(8)]
    for a, val in enumerate(even_odd(J, x, 1)):
        put(xu, c * 6 + a // 2, rb, a % 2, val)
    for a, val in enumerate(even_odd(B, x, -1)):
        put(xw, c * 6 + a // 2, rb, a % 2, val)
    return rows, x


def fine_dots(pairs, parts, fine, xu, xw, pf, qf):
    for p in pairs:
        for c in parts:
            pf[p, c] = dot(fine[...], xu[c * 6 + p])
            qf[p, c] = dot(fine[0:144], xw[c * 6 + p])


def stiff_dots(c, stiff, xs, ks):
    for q in range(4):
        y = dot(stiff[...], xs[4 * c + q])
        ks[c, 2 * q] = y[:, :128]
        ks[c, 2 * q + 1] = y[:, 128:]


def put_conv(xc, c, r, conv):
    hi, lo = split(conv)
    xc[c, 16 * r : 16 * r + 16] = hi
    xc[c, 144 + 16 * r : 160 + 16 * r] = hi
    xc[c, 288 + 16 * r : 304 + 16 * r] = lo


def back_dots(p, back, xc, yf, count):
    for c in range(count):
        y = dot(back[...], xc[c])
        yf[c, 2 * p] = y[:, :128]
        yf[c, 2 * p + 1] = y[:, 128:]


def fine_rows(pf, qf, p, c, r):
    rows = slice(16 * r, 16 * r + 16)
    return (
        qf[p, c, rows],
        pf[p, c, 144 + 16 * r : 160 + 16 * r],
        pf[p, c, 288 + 16 * r : 304 + 16 * r],
    )


def velocity_rows(pf, lanes, p, r):
    rows = slice(16 * r, 16 * r + 16)
    return [pf[p, n, rows] * lanes[n + 1 : n + 2] for n in range(3)]


def stiff_plane(lanes, wjk, sz, ks, c, i, rb):
    rows = pl.ds(pl.multiple_of(rb * 16, 16), 16)
    more = pl.ds(pl.multiple_of(64 + rb * 16, 16), 16)
    kz, kt, kr = lanes[4:5, :128], lanes[5:6, :128], lanes[6:7, :128]
    plane = kt * ks[c, i, rows] + kr * ks[c, i, more]
    return wjk[rows] * kz * sz[c, i, rows] + float(W[i]) * plane


def residual(u, lanes, fine, back, stiff, wjk, res, pf, qf, xu, xw, xs, xc0, xc1, yf, sz, ks):
    for c in range(3):
        for rb in range(4):
            rows, x = along_pipe(u, c, rb, xu, xw)
            for i in range(8):
                put(xs, c * 4 + i // 2, rb, i % 2, x[i])
            for i, val in enumerate(even_odd(STIFF, x, 1)):
                sz[c, i, rows] = val
        fine_dots(range(6), (c,), fine, xu, xw, pf, qf)
        stiff_dots(c, stiff, xs, ks)
    for p in range(6):
        xc = (xc0, xc1)[p % 2]
        for r in range(9):
            v = velocity_rows(pf, lanes, p, r)
            for c in range(3):
                g = fine_rows(pf, qf, p, c, r)
                put_conv(xc, c, r, v[0] * g[0] + v[1] * g[1] + v[2] * g[2])
        back_dots(p, back, xc, yf, 3)
    keep = keep_rows(16)

    def body(t, carry):
        c, rb = t // 4, t % 4
        rows = pl.ds(pl.multiple_of(rb * 16, 16), 16)
        adv = even_odd(JV, [yf[c, a, rows] for a in range(12)], 1)
        for i in range(8):
            res[c, i, rows] = -(adv[i] + stiff_plane(lanes, wjk, sz, ks, c, i, rb)) * keep
        return carry

    lax.fori_loop(0, 12, body, 0)


def fields_kernel(u, fine, pf, qf, xu, xw):
    def body(t, carry):
        along_pipe(u, t // 4, t % 4, xu, xw)
        return carry

    lax.fori_loop(0, 12, body, 0)
    fine_dots(range(6), range(3), fine, xu, xw, pf, qf)


def corner_weights():
    row, col = iota((8, 64), 0), iota((8, 64), 1)

    def weight(node, upper):
        acc = jnp.zeros((8, 64), F32)
        for n in range(8):
            acc = jnp.where(
                node == n, jnp.where(upper, float(LIN[1, n]), float(LIN[0, n])), acc
            )
        return acc

    return weight(col >> 3, (row & 2) != 0) * weight(col & 7, (row & 1) != 0)


def corners_kernel(res, out):
    weights = corner_weights()
    for c in range(3):
        planes = [res[c, i] for i in range(8)]
        z1 = sum(float(LIN[1, i]) * planes[i] for i in range(1, 8))
        z0 = sum(float(LIN[0, i]) * planes[i] for i in range(7))
        both = jnp.concatenate([z0, z1], axis=1)
        out[c] = jnp.dot(weights, both, precision=EXACT, preferred_element_type=F32)


def change_kernel(
    d, pf, qf, lanes, fine, stiff, wjk, coarse, out, pd, qd, xd, xe, xs, acc, xc, sz
):
    mean_w = LIN * W[None, :]
    mean_s = LIN @ STIFF

    def body(t, carry):
        c, rb = t // 4, t % 4
        rows, x = along_pipe(d, c, rb, xd, xe)
        for a in range(2):
            put(xs, c, rb, a, sum(float(mean_w[a, i]) * x[i] for i in range(8)))
            sz[c, a, rows] = sum(float(mean_s[a, i]) * x[i] for i in range(8))
        return carry

    lax.fori_loop(0, 12, body, 0)
    acc[...] = jnp.zeros_like(acc)

    def add_conv(n, p, r, conv):
        rows = slice(16 * r, 16 * r + 16)
        left, right = conv[:, :128], conv[:, 128:]
        for a in range(2):
            acc[n, rows, 128 * a : 128 * a + 128] += (
                float(COARSE_Z[a, 2 * p]) * left + float(COARSE_Z[a, 2 * p + 1]) * right
            )

    fine_dots((0,), range(3), fine, xd, xe, pd, qd)
    for p in range(6):
        if p < 5:
            fine_dots((p + 1,), range(3), fine, xd, xe, pd, qd)
        for r in range(9):
            v = velocity_rows(pf, lanes, p, r)
            w = velocity_rows(pd, lanes, p, r)
            for c in range(3):
                g = fine_rows(pf, qf, p, c, r)
                h = fine_rows(pd, qd, p, c, r)
                one = (v[0] * h[0] + v[1] * h[1] + v[2] * h[2]) + (
                    w[0] * g[0] + w[1] * g[1] + w[2] * g[2]
                )
                add_conv(c, p, r, one)
                add_conv(3 + c, p, r, w[0] * h[0] + w[1] * h[1] + w[2] * h[2])
    r = iota((4, 256), 1) & (RADIAL - 1)
    upper = iota((4, 256), 0) & 1
    wall = ((upper == 0) & (r == 0)) | ((upper == 1) & (r == RADIAL - 1))
    wall = jnp.where(wall, 1.0, 0.0).astype(F32)
    keep = jnp.concatenate([keep_rows(64)] * 2, axis=1)
    wide = jnp.concatenate([wjk[...]] * 2, axis=1)
    kz, kt, kr = lanes[4:5], lanes[5:6], lanes[6:7]
    weights = corner_weights()
    for n in range(6):
        for q in range(9):
            put_conv(xc, n, q, acc[n, 16 * q : 16 * q + 16])
        y = dot(coarse[...], xc[n])
        total = y[0:4] - wall * y[4:8]
        if n < 3:
            ks = dot(stiff[...], xs[n])
            plane = jnp.concatenate([sz[n, 0], sz[n, 1]], axis=1) * wide * kz
            plane = (plane + kt * ks[0:64] + kr * ks[64:128]) * keep
            total = (
                total
                + jnp.dot(weights, plane, precision=EXACT, preferred_element_type=F32)[0:4]
            )
        out[n, 0:4] = -total
        out[n, 4:8] = jnp.zeros((4, 256), F32)


def pack_two(res, low, high):
    def body(c, carry):
        for n in range(2):
            low[c, 8 * n : 8 * n + 8] = pack_low(lambda i: res[c, i, 8 * n : 8 * n + 8])
            high[c, 8 * n : 8 * n + 8] = pack_high(
                lambda i: res[c, i, 48 + 8 * n : 56 + 8 * n]
            )
        return carry

    lax.fori_loop(0, 3, body, 0)


def project_kernel(
    field, tlo, thi, hz_low, hz_high, lanes, fine, back, stiff, wjk, u, res, low, high, *scratch
):
    hz = lanes[7:8, :128]
    inner = 1.0 / hz
    first = 1.0 / (hz + hz_low[192:193])
    final = 1.0 / (hz + hz_high[192:193])
    k = iota((8, 128), 0)
    rk = jnp.where(
        k == 0, lanes[9:10, :128], jnp.where(k == 7, lanes[10:11, :128], lanes[8:9, :128])
    )
    rk = rk * keep_rows(8)
    by_plane = {0: rk * first, 7: rk * final}
    middle = rk * inner

    def around(c, carry):
        lo, hi = tlo[c], thi[c]
        for i in range(8):
            x = field[c, i]
            first, last = x[0:8], x[56:64]
            u[c, i] = x
            u[c, i, 0:8] = first + from_low(last, lo, i)
            u[c, i, 56:64] = last + from_high(first, hi, i)
        return carry

    def across(c, carry):
        for i in range(8):
            x = u[c, i]
            for j in range(8):
                v = x[8 * j : 8 * j + 8]
                f = by_plane.get(i, middle)
                f = 0.5 * f if j in (0, 7) else f
                below, above = radial_parts(v)
                u[c, i, 8 * j : 8 * j + 8] = radial_sum(v, below, above) * f
        return carry

    lax.fori_loop(0, 3, around, 0)
    lax.fori_loop(0, 3, across, 0)
    residual(u, lanes, fine, back, stiff, wjk, res, *scratch)
    pack_two(res, low, high)


def step_length(sums):
    total = jnp.sum(sums[...], axis=0, keepdims=True)
    return total[:, 0:1] / total[:, 1:2]


def advance_kernel(u_old, d, sums, lanes, fine, back, stiff, wjk, u, res, low, high, *scratch):
    alpha = step_length(sums)

    def body(t, carry):
        c, i = t // 8, t % 8
        u[c, i] = u_old[c, i] + alpha * d[c, i]
        return carry

    lax.fori_loop(0, 24, body, 0)
    residual(u, lanes, fine, back, stiff, wjk, res, *scratch)
    pack_two(res, low, high)


def around_widen_kernel(res, tlo, thi, out, down, up):
    lane = iota((8, 128), 1)

    def body(c, carry):
        lo6, lo7, hi0, hi1 = tlo[c, 0:8], tlo[c, 8:16], thi[c, 0:8], thi[c, 8:16]
        for i in range(8):
            x = res[c, i]
            first, last = x[0:8], x[56:64]
            out[c, i, 0:64] = x
            out[c, i, 0:8] = first + from_low(last, lo7, i)
            out[c, i, 56:64] = last + from_high(first, hi0, i)
            out[c, i, 64:72] = jnp.where(
                lane < 64, lanes_by(lo6, -16 * i), lanes_by(hi1, 112 - 16 * i)
            )
        for n in range(2):
            down[c, n] = out[c, n]
            up[c, n] = out[c, 6 + n]
        return carry

    lax.fori_loop(0, 3, body, 0)


def widen_planes(e, xf, half):
    lane, k = iota((8, 128), 1), iota((8, 128), 0)
    extra = e[64:72]
    planes = [e[8 * j : 8 * j + 8] for j in range(8)]
    under = jnp.where(lane < 16, extra, lanes_by(planes[6], 16))
    over = jnp.where(lane >= 112, extra, lanes_by(planes[1], -16))
    cols = slice(half * 128, half * 128 + 128)
    for j, v in enumerate([under] + planes + [over]):
        below, above = radial_parts(v)
        own = radial_sum(v, below, above)
        side = jnp.where(k == 0, rows_by(below, 2), jnp.where(k == 1, above, 0.0))
        hi, lo = split(jnp.concatenate([own, side], axis=0))
        xf[16 * j : 16 * j + 16, cols] = hi
        xf[160 + 16 * j : 176 + 16 * j, cols] = hi
        xf[320 + 16 * j : 336 + 16 * j, cols] = lo


def transform_kernel(field, forward, vectors, out, xf0, xf1, yf):
    def body(c, carry):
        for p in range(4):
            buf = (xf0, xf1)[p % 2]
            for half in range(2):
                widen_planes(field[c, 2 * p + half], buf, half)
            y = dot(forward[...], buf[...])
            yf[c, 2 * p] = y[:, :128]
            yf[c, 2 * p + 1] = y[:, 128:]
        return carry

    lax.fori_loop(0, 3, body, 0)

    def mid(rb, carry):
        rows = pl.ds(pl.multiple_of(rb * 16, 16), 16)
        y = [[yf[c, i, rows] for i in range(8)] for c in range(3)]
        for a in range(10):
            acc = [vectors[1, a] * y[c][0] for c in range(3)]
            for i in range(1, 8):
                s = vectors[i + 1, a]
                acc = [acc[c] + s * y[c][i] for c in range(3)]
            for c in range(3):
                out[c, a, rows] = acc[c]
        return carry

    lax.fori_loop(0, 7, mid, 0)


def solve_kernel(
    own, zlo, zhi, vectors, forward, inverse, scale, corr, low, high, xf0, xf1, yf, xb
):
    for c in range(3):
        for n, (buf, halo) in enumerate(((xf0, zlo), (xf1, zhi))):
            widen_planes(halo[c, 0], buf.at[c], 0)
            widen_planes(halo[c, 1], buf.at[c], 1)
            y = dot(forward[...], buf[c])
            yf[c, 2 * n] = y[:, :128]
            yf[c, 2 * n + 1] = y[:, 128:]

    def mid(rb, carry):
        rows = pl.ds(pl.multiple_of(rb * 16, 16), 16)
        y = [[yf[c, i, rows] for i in range(4)] for c in range(3)]
        spec = []
        for a in range(10):
            acc = [own[c, a, rows] for c in range(3)]
            for n, i in enumerate((0, 1, 8, 9)):
                s = vectors[i, a]
                acc = [acc[c] + s * y[c][n] for c in range(3)]
            f = scale[a, rows]
            spec.append([acc[c] * f for c in range(3)])
        for i in range(8):
            acc = [vectors[i + 1, 0] * spec[0][c] for c in range(3)]
            for a in range(1, 10):
                s = vectors[i + 1, a]
                acc = [acc[c] + s * spec[a][c] for c in range(3)]
            cols = slice((i % 2) * 128, (i % 2) * 128 + 128)
            for c in range(3):
                hi, lo = split(acc[c])
                for term, part in enumerate((hi, hi, lo)):
                    xb[c * 4 + i // 2, pl.ds(pl.multiple_of(term * 112 + rb * 16, 16), 16),
                       cols] = part
        return carry

    lax.fori_loop(0, 7, mid, 0)

    k = iota((8, 128), 0)
    r = iota((8, 128), 1) & (RADIAL - 1)
    inner = ((k == 0) & (r > 0)) | ((k == 7) & (r < RADIAL - 1))
    share = jnp.where(inner, 0.5, 1.0).astype(F32)
    for t in range(12):
        c, p = t // 4, t % 4
        y = dot(inverse[...], xb[t])
        for half in range(2):
            i = 2 * p + half
            for j in range(8):
                f = (0.5 if i in (0, 7) else 1.0) * (0.5 if j in (0, 7) else 1.0)
                corr[c, i, 8 * j : 8 * j + 8] = (
                    y[8 * j : 8 * j + 8, half * 128 : half * 128 + 128] * (share * f)
                )

    def last(c, carry):
        low[c] = pack_low(lambda i: corr[c, i, 0:8])
        high[c] = pack_high(lambda i: corr[c, i, 56:64])
        return carry

    lax.fori_loop(0, 3, last, 0)


def direction_kernel(field, zlo, zhi, res, lanes, grad, wjk, d, sums, xs, acc):
    keep = keep_rows(8)
    finish_sum(field, zlo, zhi, d, lambda i, j: keep)
    acc[...] = jnp.zeros_like(acc)
    vol = lanes[0:1, :128]
    kz, kt, kr = lanes[4:5, :128], lanes[5:6, :128], lanes[6:7, :128]

    def first(t, carry):
        c, rb = t // 4, t % 4
        rows = pl.ds(pl.multiple_of(rb * 16, 16), 16)
        x = [d[c, i, rows] for i in range(8)]
        num = sum(x[i] * res[c, i, rows] for i in range(8))
        sq = sum(float(W[i]) * (x[i] * x[i]) for i in range(8))
        gz = sum(float(W[i]) * (g * g) for i, g in enumerate(even_odd(D, x, -1)))
        acc[0] += num
        acc[1] += wjk[rows] * (SIGMA * vol * sq + kz * gz)
        for i in range(8):
            hi, lo = split(x[i])
            for term, part in enumerate((hi, hi, lo, lo)):
                xs[c * 4 + i // 2, pl.ds(pl.multiple_of(term * 64 + rb * 16, 16), 16),
                   (i % 2) * 128 : (i % 2) * 128 + 128] = part
        return carry

    lax.fori_loop(0, 12, first, 0)

    total = acc[1]
    for t in range(12):
        y = dot(grad[...], xs[t])
        for half in range(2):
            v = y[:, half * 128 : half * 128 + 128]
            v = v * v
            plane = jnp.zeros((16, 128), F32)
            for q in range(4):
                rows = slice(16 * q, 16 * q + 16)
                plane = plane + wjk[rows] * (kt * v[rows] + kr * v[64 + 16 * q : 80 + 16 * q])
            total = total + float(W[2 * (t % 4) + half]) * plane
    acc[1] = total
    num = jnp.sum(jnp.sum(acc[0], axis=0, keepdims=True), axis=1, keepdims=True)
    den = jnp.sum(jnp.sum(acc[1], axis=0, keepdims=True), axis=1, keepdims=True)
    at = iota((128, 128), 1)
    sums[...] = jnp.where(at == 0, num, jnp.where(at == 1, den, 0.0))


def route_kernel(slot, corner, right, owner):
    hot = (slot[...] == iota((128, 128), 0)).astype(F32)
    nt = (((1,), (1,)), ((), ()))
    ids = corner[...].astype(F32)
    by_elem = lax.dot_general(hot, ids, nt, precision=EXACT, preferred_element_type=F32)
    by_corner = lax.dot_general(ids, hot, nt, precision=EXACT, preferred_element_type=F32)
    owner[...] = (by_corner + 0.5).astype(jnp.int32) // 136
    ids = (by_elem + 0.5).astype(jnp.int32)
    inside = ids - ids // 136 * 136
    pos = iota((128, 256), 1)
    for q in range(8):
        right[128 * q : 128 * q + 128] = (inside[:, q : q + 1] == pos).astype(F32).astype(BF16)


def placed(values, right, owner, left):
    dev = iota((128, 128), 0)
    for c, both in enumerate(values):
        hi = both.astype(BF16).astype(F32)
        for q in range(8):
            mine = owner[q : q + 1] == dev
            cols = slice((q // 4) * 128, (q // 4) * 128 + 128)
            for m, piece in enumerate((hi, both - hi)):
                at = (2 * c + m) * 128
                left[at : at + 128, 128 * q : 128 * q + 128] = jnp.where(
                    mine, piece[q % 4 : q % 4 + 1, cols], 0.0
                ).astype(BF16)
    y = dot(left[...], right[...])
    return [y[256 * c : 256 * c + 128] + y[256 * c + 128 : 256 * c + 256] for c in range(3)]


def place_base_kernel(base, right, owner, out, left):
    for c, total in enumerate(placed([base[c] for c in range(3)], right, owner, left)):
        out[c] = lanes_by(total, 8 * c)


def place_kernel(base, change, right, owner, part, dense, left0, left1):
    blocks = [base[c] for c in range(3)]
    for n, left in enumerate((left0, left1)):
        values = [change[3 * n + c] for c in range(3)]
        for c, total in enumerate(placed(values, right, owner, left)):
            blocks.append(lanes_by(total, 8 * (3 * n + 3 + c)))
    spill = None
    for n, total in enumerate(blocks):
        first = total[:, :128]
        dense[pl.ds(n, 128, stride=10)] = first if spill is None else first + spill
        spill = total[:, 128:]
    dense[pl.ds(9, 128, stride=10)] = spill + lanes_by(part[...], 72)


def store_kernel(u, d, slot, u_hbm, d_hbm, u_out, d_out, sems):
    hot = (slot[...] == iota((128, 128), 0)).astype(F32)
    copies = []
    for c in range(3):
        for n, (x, y, out) in enumerate(((u, u_out, u_hbm), (d, d_out, d_hbm))):
            flat = x[c].reshape(512, 128)
            y[c] = jnp.dot(flat, hot, precision=EXACT, preferred_element_type=F32).reshape(
                8, 64, 128
            )
            copies.append(pltpu.make_async_copy(y.at[c], out.at[c], sems.at[2 * c + n]))
            copies[-1].start()
    for copy in copies:
        copy.wait()


def end_kernel(u_hbm, d_hbm, parts, vel_hbm, coarse_hbm, u, d, vel, coarse, sems):
    last = pltpu.make_async_copy(coarse, coarse_hbm, sems.at[0])
    pieces = [(c, pl.ds(4 * h, 4)) for c in range(3) for h in range(2)]
    loads = [
        [
            pltpu.make_async_copy(a.at[at], b.at[at], sems.at[1 + 2 * m + n])
            for n, (a, b) in enumerate(((u_hbm, u), (d_hbm, d)))
        ]
        for m, at in enumerate(pieces)
    ]
    stores = [
        pltpu.make_async_copy(vel.at[at], vel_hbm.at[at], sems.at[13 + m])
        for m, at in enumerate(pieces)
    ]
    for pair in loads:
        for copy in pair:
            copy.start()
    sums = [
        jnp.sum(parts[pl.ds(n, 128, stride=10)], axis=0, keepdims=True) for n in range(10)
    ]
    alpha = sums[9][:, 72:73] / sums[9][:, 73:74]
    for m, at in enumerate(pieces):
        for copy in loads[m]:
            copy.wait()
        vel[at] = u[at] + alpha * d[at]
        stores[m].start()
    total = jnp.concatenate(sums, axis=1)
    one, two = lanes_by(total, -408), lanes_by(total, -816)
    both = total + alpha * (one + alpha * two)
    for c in range(3):
        coarse[c : c + 1] = lanes_by(both, -136 * c)[:, :136]
    last.start()
    for copy in (*stores, last):
        copy.wait()


FIELD = (3, 8, 64, 128)


def both_ways(axis, to_next, to_prev):
    n = lax.axis_size(axis)
    up = [(i, (i + 1) % n) for i in range(n)]
    down = [((i + 1) % n, i) for i in range(n)]
    from_next = lax.ppermute(to_prev, axis, down)
    return lax.ppermute(to_next, axis, up), from_next


def fine_scratch():
    return [
        pltpu.VMEM((6, 3, 432, 256), F32),
        pltpu.VMEM((6, 3, 144, 256), F32),
        pltpu.VMEM((18, 256, 256), BF16),
        pltpu.VMEM((18, 256, 256), BF16),
    ]


def local_scratch(count):
    return [
        pltpu.VMEM((12, 256, 256), BF16),
        pltpu.VMEM((count, 432, 256), BF16),
        pltpu.VMEM((count, 432, 256), BF16),
        pltpu.VMEM((count, 12, 64, 128), F32),
        pltpu.VMEM(FIELD, F32),
        pltpu.VMEM((3, 8, 128, 128), F32),
    ]


def shards(vel, slot, corner, axial, arc, rad, vectors, values):
    smem, hbm = pltpu.SMEM, pltpu.HBM
    small = ((3, 8, 128), F32)
    count = len(CONSTANTS)
    vel = vel.reshape(FIELD)
    down, up, lanes = call(
        faces_kernel,
        [((200, 128), F32), ((200, 128), F32), ((16, 256), F32)],
        (vel, slot, arc, rad, axial),
        [
            pltpu.VMEM((2, 3, 64, 128), F32),
            pltpu.VMEM((1, 128), jnp.int32),
            pltpu.SMEM((RADIAL,), F32),
            pltpu.SMEM((RADIAL,), F32),
            pltpu.SemaphoreType.DMA((9,)),
        ],
        spaces={0: hbm, 1: hbm, 2: hbm, 3: hbm, 4: smem},
    )
    zlo, zhi = both_ways("wide", up, down)
    mv, fine, back, stiff, grad, coarse_jk, wjk = call(
        inner_kernel,
        [((3, 6, 64, 128), F32)] + [(m.shape, m.dtype) for m in CONSTANTS],
        (vel, slot, lanes, *(jnp.asarray(m) for m in CONSTANTS)),
        [
            pltpu.VMEM((3, 6, 64, 128), F32),
            pltpu.VMEM((1, 128), jnp.int32),
            pltpu.SemaphoreType.DMA((4 + count,)),
        ],
        spaces={0: hbm, 1: hbm, **{3 + i: hbm for i in range(count)}},
    )
    zlo, zhi, mv, fine, back, stiff, grad, coarse_jk, wjk = lax.optimization_barrier(
        (zlo, zhi, mv, fine, back, stiff, grad, coarse_jk, wjk)
    )
    field, low, high = call(
        pipe_sum_kernel, [(FIELD, F32), small, small], (mv, down, up, zlo, zhi)
    )
    forward, inverse, scale = call(
        solve_tables_kernel,
        [((112, 480), BF16), ((64, 336), BF16), ((10, 112, 128), F32)],
        (vectors, values[None], lanes),
        [
            pltpu.VMEM((10, 10), F32),
            pltpu.VMEM((1, 10), F32),
            pltpu.SemaphoreType.DMA((2,)),
        ],
        spaces={0: hbm, 1: hbm},
    )

    def sum_rounds(field, low, high, beside=()):
        tlo, thi = both_ways("narrow", high, low)
        out, down, up = call(
            around_sum_kernel,
            [(FIELD, F32), ((200, 128), F32), ((200, 128), F32)],
            (field, tlo, thi, lanes),
        )
        zlo, zhi = both_ways("wide", up, down)
        zlo, zhi, beside = lax.optimization_barrier((zlo, zhi, beside))
        return (out, zlo, zhi), beside

    local = (lanes, fine, back, stiff, wjk)
    packs = [(FIELD, F32), (FIELD, F32), ((3, 16, 128), F32), ((3, 16, 128), F32)]
    u, res, low, high = call(
        project_kernel,
        packs,
        (field, *both_ways("narrow", high, low), zlo, zhi, *local),
        fine_scratch() + local_scratch(3),
    )
    for step in range(2):
        if step > 0:
            sums = lax.all_to_all(part, BOTH, 0, 0, tiled=True)
            u, res, low, high = call(
                advance_kernel, packs, (u, d, sums, *local), fine_scratch() + local_scratch(3)
            )
        tlo, thi = both_ways("narrow", high, low)
        wide_field, down, up = call(
            around_widen_kernel,
            [((3, 8, 72, 128), F32), ((3, 2, 72, 128), F32), ((3, 2, 72, 128), F32)],
            (res, tlo, thi),
        )
        zlo, zhi = both_ways("wide", up, down)
        (own,) = call(
            transform_kernel,
            [((3, 10, 112, 128), F32)],
            (wide_field, forward, vectors),
            [
                pltpu.VMEM((480, 256), BF16),
                pltpu.VMEM((480, 256), BF16),
                pltpu.VMEM((3, 8, 112, 128), F32),
            ],
            spaces={2: smem},
        )
        zlo, zhi, own = lax.optimization_barrier((zlo, zhi, own))
        corr, low, high = call(
            solve_kernel,
            [(FIELD, F32), small, small],
            (own, zlo, zhi, vectors, forward, inverse, scale),
            [
                pltpu.VMEM((3, 480, 256), BF16),
                pltpu.VMEM((3, 480, 256), BF16),
                pltpu.VMEM((3, 4, 112, 128), F32),
                pltpu.VMEM((12, 336, 256), BF16),
            ],
            spaces={3: smem},
        )
        beside = ()
        if step == 1:
            fields = [((6, 3, 432, 256), F32), ((6, 3, 144, 256), F32)]
            right, owner = call(
                route_kernel,
                [((1024, 256), BF16), ((8, 128), jnp.int32)],
                (slot, corner),
                free=True,
            )
            (base,) = call(corners_kernel, [((3, 8, 256), F32)], (res,))
            (base,) = call(
                place_base_kernel,
                [((3, 128, 256), F32)],
                (base, right, owner),
                [pltpu.VMEM((768, 1024), BF16)],
            )
            beside = (call(fields_kernel, fields, (u, fine), fine_scratch()[2:]), base)
        halo, beside = sum_rounds(corr, low, high, beside)
        d, part = call(
            direction_kernel,
            [(FIELD, F32), ((128, 128), F32)],
            (*halo, res, lanes, grad, wjk),
            [pltpu.VMEM((12, 256, 256), BF16), pltpu.VMEM((2, 16, 128), F32)],
        )
    (pf, qf), base = beside
    (change,) = call(
        change_kernel,
        [((6, 8, 256), F32)],
        (d, pf, qf, lanes, fine, stiff, wjk, coarse_jk),
        fine_scratch()
        + [
            pltpu.VMEM((3, 256, 256), BF16),
            pltpu.VMEM((6, 144, 256), F32),
            pltpu.VMEM((6, 432, 256), BF16),
            pltpu.VMEM((3, 2, 64, 128), F32),
        ],
    )
    (dense,) = call(
        place_kernel,
        [((1280, 128), F32)],
        (base, change, right, owner, part),
        [pltpu.VMEM((768, 1024), BF16), pltpu.VMEM((768, 1024), BF16)],
    )
    parts = lax.all_to_all(dense.reshape(128, 1, 1280), BOTH, 0, 0, tiled=True)
    parts = parts.reshape(1280, 128)
    u, d = call(
        store_kernel,
        [(FIELD, F32), (FIELD, F32)],
        (u, d, slot),
        [pltpu.VMEM(FIELD, F32), pltpu.VMEM(FIELD, F32), pltpu.SemaphoreType.DMA((6,))],
        hbm_out={0, 1},
        free=True,
    )
    out, coarse = call(
        end_kernel,
        [(FIELD, F32), ((3, 136), F32)],
        (u, d, parts),
        [
            pltpu.VMEM(FIELD, F32),
            pltpu.VMEM(FIELD, F32),
            pltpu.VMEM(FIELD, F32),
            pltpu.VMEM((3, 136), F32),
            pltpu.SemaphoreType.DMA((19,)),
        ],
        spaces={0: pltpu.HBM, 1: pltpu.HBM},
        hbm_out={0, 1},
    )
    return out.reshape(3, 512, 128), coarse


def solution(mesh):
    return jax.shard_map(
        shards,
        mesh=mesh,
        in_specs=(P(None, None, BOTH), P(BOTH, None), P(None, BOTH), P("wide"), P(), P(), P(), P()),
        out_specs=(P(None, None, BOTH), P(None, BOTH)),
        check_vma=False,
    )
```
